32 devices in a mesh: dp: 8 (over z, y), tensor: 4 (over x, core).
Axes of the slice: x: 2, y: 2, z: 4, core: 2. Of those that a mesh axis runs over, the one named last changes fastest.
Arguments:
- tokens: bfloat16 [65536, 512], P(('dp', 'tensor')), may hold values from -6 to 6
- segment_ids: int32 [128, 512], P('dp'), may hold values from 0 to 15, never falling along the last dimension, each value on 1 to 128 neighbouring positions
- row_lengths: int32 [128], P('dp'), may hold values from 256 to 512, as said below
- qkv_weight: bfloat16 [3, 512, 512], P(None, None, 'tensor'), may hold values from -6 to 6
- qv_bias: bfloat16 [2, 512], P(None, 'tensor'), may hold values from -3 to 3
- proj_weight: bfloat16 [512, 512], P('tensor'), may hold values from -6 to 6
- proj_bias: bfloat16 [512], replicated, may hold values from -3 to 3
- first_gain: bfloat16 [512], replicated, may hold values from 0.5 to 1.5
- first_shift: bfloat16 [512], replicated, may hold values from -3 to 3
- up_weight: bfloat16 [512, 2048], P(None, 'tensor'), may hold values from -6 to 6
- up_bias: bfloat16 [2048], P('tensor'), may hold values from -3 to 3
- down_weight: bfloat16 [2048, 512], P('tensor'), may hold values from -6 to 6
- down_bias: bfloat16 [512], replicated, may hold values from -3 to 3
- second_gain: bfloat16 [512], replicated, may hold values from 0.5 to 1.5
- second_shift: bfloat16 [512], replicated, may hold values from -3 to 3
- out_grad: bfloat16 [65536, 512], P(('dp', 'tensor')), may hold values from -6 to 6
Outputs:
- layer_out: bfloat16 [65536, 512], P(('dp', 'tensor'))
- tokens_grad: float32 [65536, 512], P(('dp', 'tensor'))
- qkv_weight_grad: float32 [3, 512, 512], P(None, None, 'tensor')
- qv_bias_grad: float32 [2, 512], P(None, 'tensor')
- proj_weight_grad: float32 [512, 512], P('tensor')
- proj_bias_grad: float32 [512], replicated
- first_gain_grad: float32 [512], replicated
- first_shift_grad: float32 [512], replicated
- up_weight_grad: float32 [512, 2048], P(None, 'tensor')
- up_bias_grad: float32 [2048], P('tensor')
- down_weight_grad: float32 [2048, 512], P('tensor')
- down_bias_grad: float32 [512], replicated
- second_gain_grad: float32 [512], replicated
- second_shift_grad: float32 [512], replicated
The draws below stay inside these ranges and needn't reach their ends.
Inputs may be any that keep to these rules, and one draw needn't show every extreme that they name: `segment_ids`: ids never fall along a packed row; every id of 0 to 15 is used by 1 to 128 consecutive tokens of each row, one example of every row holding exactly 128. `row_lengths`: of the rows of one index of dp, one of the first two holds 512 tokens and the other 256; places at or past a row's length are padding.
All inputs are finite; a program needn't handle non-finite values.
Results may differ from the reference program's by a relative error of at most 0.022.
Values may be sent and summed in bfloat16 or wider, within the bound.
A program may use at most 256 MiB of HBM per device.

```python
import math
import jax
import jax.numpy as jnp
import numpy as np
from jax import lax

D = 512
HEADS = 8
HEAD_DIM = 64
FF = 2048
SEQ = 512
SEG_MOST = 128
SEG_COUNT = 16
ROWS_DEV = 16
ROWS = 128
TOKENS = 65536


def drawn_layout(key):
    block_count = ROWS // ROWS_DEV
    flips = jax.random.randint(jax.random.fold_in(key, 32), (block_count,), 0, 2)
    chosen = jax.random.randint(jax.random.fold_in(key, 41), (), 0, block_count)
    planted_row = chosen * ROWS_DEV + 1 - flips[chosen]
    signs = (2 * jax.random.randint(jax.random.fold_in(key, 42), (D,), 0, 2) - 1).astype(jnp.float32)
    support = jax.random.randint(jax.random.fold_in(key, 43), (D,), 0, 2).astype(jnp.float32)
    value_col = jax.random.randint(jax.random.fold_in(key, 44), (), 0, D)
    up_col = jax.random.randint(jax.random.fold_in(key, 45), (), 0, FF)
    return (planted_row, signs, support, value_col, up_col)


def draw_row_lengths(key, part):
    lengths_drawn = jax.random.randint(jax.random.fold_in(key, 31), (ROWS,), SEQ // 2, SEQ + 1)
    places = jnp.arange(ROWS) % ROWS_DEV
    blocks = jnp.arange(ROWS) // ROWS_DEV
    flips = jax.random.randint(jax.random.fold_in(key, 32), (ROWS // ROWS_DEV,), 0, 2)
    full_place = flips[blocks]
    lengths_drawn = jnp.where(places == full_place, SEQ, lengths_drawn)
    lengths_drawn = jnp.where(places == 1 - full_place, SEQ // 2, lengths_drawn)
    return lengths_drawn.astype(jnp.int32)


def draw_tokens(key, part):
    planted_row, signs, support, value_col, up_col = drawn_layout(key)
    block_count = ROWS // ROWS_DEV
    block_factor = 0.9 * jnp.exp(jax.random.uniform(jax.random.fold_in(key, 11), (block_count,), jnp.float32, -0.7, 0.0))
    rows_of = jnp.arange(TOKENS) // SEQ
    places = jnp.arange(TOKENS) % SEQ
    noise = jax.random.normal(jax.random.fold_in(key, 12), (TOKENS, D), jnp.float32)
    typical = noise * block_factor[rows_of // ROWS_DEV][:, None]
    outlier = 3.0 * signs * support + 0.3 * noise
    chosen_rows = (rows_of == planted_row) & (places >= SEQ - SEQ // 4)
    mixed = jnp.where(chosen_rows[:, None], outlier, typical)
    return jnp.clip(mixed, -6.0, 6.0).astype(jnp.bfloat16)


def scaled_values(key, salt, shape, fan_in, factor_shape):
    own_key = jax.random.fold_in(key, salt)
    factor = jax.random.uniform(jax.random.fold_in(own_key, 21), factor_shape, jnp.float32, 0.6, 1.0)
    drawn = jnp.clip(jax.random.normal(jax.random.fold_in(own_key, 23), shape, jnp.float32), -6.0, 6.0)
    return drawn * factor * fan_in ** (-0.5)


def draw_qkv_weight(key, part):
    planted_row, signs, support, value_col, up_col = drawn_layout(key)
    weights = scaled_values(key, 101, (3, D, D), D, (3, 1, 1))
    value_part = weights[2] * jnp.where(support[:, None] > 0.5, 0.15, 1.0)
    column = jnp.where(support > 0.5, signs * (0.3 * D ** (-0.5)), value_part[:, value_col])
    columns = jnp.arange(D)
    value_part = jnp.where(columns[None, :] == value_col, column[:, None], value_part)
    return jnp.concatenate([weights[:2], value_part[None]], axis=0).astype(jnp.bfloat16)


def draw_proj_weight(key, part):
    return scaled_values(key, 102, (D, D), D // 16, ()).astype(jnp.bfloat16)


def draw_up_weight(key, part):
    planted_row, signs, support, value_col, up_col = drawn_layout(key)
    weights = scaled_values(key, 103, (D, FF), D, ())
    column = jnp.where(support > 0.5, signs * (3.0 * D ** (-0.5)), weights[:, up_col])
    columns = jnp.arange(FF)
    weights = jnp.where(columns[None, :] == up_col, column[:, None], weights)
    return weights.astype(jnp.bfloat16)


def draw_down_weight(key, part):
    return scaled_values(key, 104, (FF, D), FF // 2, ()).astype(jnp.bfloat16)


def block_levels(key, extent, cuts, smallest, largest):
    loudness, own = 1.0, jax.random.fold_in(key, 6)
    for axis_at, parts in cuts:
        draws = jnp.exp(jax.random.uniform(jax.random.fold_in(own, axis_at), (parts,), jnp.float32, smallest / len(cuts), largest / len(cuts)))
        loudness = loudness * jnp.repeat(draws, extent[axis_at] // parts).reshape([-1 if axis == axis_at else 1 for axis in range(len(extent))])
    return loudness


def profile(number_of, total, reach, lean):
    weights = [(1 << 20) // math.isqrt(rank ** lean) + 1 for rank in range(2, number_of + 1)]
    rest, counts = total - reach - (number_of - 1), [1] * (number_of - 1)
    while rest > 0:
        movable = [i for i in range(number_of - 1) if counts[i] < reach]
        whole, left = sum([weights[i] for i in movable]), rest
        for i in movable:
            extra = min(reach - counts[i], max(1, left * weights[i] // whole), rest)
            counts[i] = counts[i] + extra
            rest = rest - extra
    return np.array([reach] + counts)


def ragged(rng, count, total, limit, slope):
    if count == 2:
        one = jax.random.randint(rng, (), max(1, total - limit), min(limit, total - 1) + 1)
        return jnp.stack([one, total - one])
    sizes = jnp.asarray(profile(count, total, limit, slope), jnp.int32)
    couples = (count - 1) // 2
    giver, taker = sizes[1:1 + 2 * couples:2], sizes[2:2 + 2 * couples:2]
    slack = jnp.minimum(giver - 1, limit - taker)
    moved = jax.random.randint(jax.random.fold_in(rng, 1), (couples,), 0, 1 << 20) % (slack + 1)
    sizes = sizes.at[1:1 + 2 * couples:2].set(giver - moved).at[2:2 + 2 * couples:2].set(taker + moved)
    return sizes[jax.random.permutation(jax.random.fold_in(rng, 2), count)]


def scatter_about(key, extent, scale, limit, cuts=(), kind=jnp.bfloat16):
    gain = block_levels(key, extent, cuts, -0.22, 0.18) if cuts else 1.0
    values = jax.random.normal(key, extent, jnp.float32) * scale * gain
    return jnp.minimum(jnp.maximum(values, -limit), limit).astype(kind)


def setup_inputs(seed: int = 0) -> dict:
    splits = jax.random.split(jax.random.key(seed), 17)
    return {
        "tokens": draw_tokens(jax.random.fold_in(splits[16], 71), 0),
        "segment_ids": jax.vmap(lambda own: jnp.searchsorted(jnp.cumsum(ragged(own, SEG_COUNT, SEQ, SEG_MOST, 1)), jnp.arange(SEQ), side="right"))(jax.random.split(splits[1], ROWS)).reshape((ROWS, SEQ)).astype(jnp.int32),
        "row_lengths": draw_row_lengths(jax.random.fold_in(splits[16], 71), 0),
        "qkv_weight": draw_qkv_weight(jax.random.fold_in(splits[16], 71), 0),
        "qv_bias": scatter_about(splits[4], (2, D), 0.5, 3.0, ((1, 4),)),
        "proj_weight": draw_proj_weight(jax.random.fold_in(splits[16], 71), 0),
        "proj_bias": scatter_about(splits[6], (D,), 0.5, 3.0),
        "first_gain": jnp.clip(1.0 + 0.1 * jax.random.normal(splits[7], (D,), jnp.float32), 0.5, 1.5).astype(jnp.bfloat16),
        "first_shift": scatter_about(splits[8], (D,), 0.5, 3.0),
        "up_weight": draw_up_weight(jax.random.fold_in(splits[16], 71), 0),
        "up_bias": scatter_about(splits[10], (FF,), 0.5, 3.0, ((0, 4),)),
        "down_weight": draw_down_weight(jax.random.fold_in(splits[16], 71), 0),
        "down_bias": scatter_about(splits[12], (D,), 0.5, 3.0),
        "second_gain": jnp.clip(1.0 + 0.1 * jax.random.normal(splits[13], (D,), jnp.float32), 0.5, 1.5).astype(jnp.bfloat16),
        "second_shift": scatter_about(splits[14], (D,), 0.5, 3.0),
        "out_grad": scatter_about(splits[15], (TOKENS, D), 1.0, 6.0, ((0, 32),)),
    }


highest = lax.Precision.HIGHEST
levels = 127.0
norm_eps = 1e-12
masked_score = -1e+30

@jax.custom_vjp
def low(v):
    return lax.optimization_barrier(v.astype(jnp.bfloat16)).astype(jnp.float32)

@jax.custom_vjp
def low_back(v):
    return v

def low_keep(v):
    return (low(v), None)

def low_pass(kept, grad):
    return (grad,)

def back_keep(v):
    return (v, None)

def back_low(kept, grad):
    return (low(grad),)
low.defvjp(low_keep, low_pass)
low_back.defvjp(back_keep, back_low)

def quantize(values, peak_value, fixed_part):
    step_size = peak_value / levels
    scaled = values / step_size
    magnitude = jnp.abs(scaled)
    if fixed_part is None:
        fixed_part = jnp.floor(magnitude + 0.5) - magnitude
    return (jnp.sign(scaled) * (magnitude + fixed_part), fixed_part, step_size)

def layer_norm(values, gain_vec, shift_vec):
    centred = values - lax.optimization_barrier(jnp.mean(values, axis=-1, keepdims=True))
    inverse = lax.rsqrt(lax.optimization_barrier(jnp.mean(centred * centred, axis=-1, keepdims=True)) + norm_eps)
    return centred * inverse * gain_vec + shift_vec

def attend(queries, keys_low, values_low, segments, lengths):
    raw_scores = jnp.einsum('rqhe,rkhe->rhqk', queries, keys_low, precision=highest)
    scores = low_back(raw_scores) * HEAD_DIM ** (-0.5)
    places = jnp.arange(SEQ)
    same_doc = segments[:, :, None] == segments[:, None, :]
    inside = places[None, None, :] < lengths[:, None, None]
    diagonal = places[:, None] == places[None, :]
    allowed = same_doc & inside | diagonal[None]
    scores = jnp.where(allowed[:, None], scores, masked_score)
    attn_probs = jax.nn.softmax(scores, axis=-1)
    context = jnp.einsum('rhqk,rkhe->rqhe', low(attn_probs), values_low, precision=highest)
    return low_back(context)

def block_forward(params, peaks, tok_blk, seg_blk, len_blk, given):
    residues = []

    def quantize_next(values, peak_value):
        position = len(residues)
        fixed_part = None if given is None else given[position]
        ints, fixed_part, step_size = quantize(values, peak_value, fixed_part)
        residues.append(fixed_part)
        return (ints, step_size)
    token_count = tok_blk.shape[0]
    rows_here = seg_blk.shape[0]
    tok_ints, step_tokens = quantize_next(tok_blk, peaks[0])
    qkv_ints, step_qkv = quantize_next(params['qkv_weight'], peaks[1][:, None, None])
    raw_qkv = jnp.einsum('td,idh->ith', tok_ints, qkv_ints, precision=highest)
    qkv_vals = low_back(raw_qkv) * (step_tokens * step_qkv)
    queries = low(qkv_vals[0] + params['qv_bias'][0])
    keys_low = low(qkv_vals[1])
    values_low = low(qkv_vals[2] + params['qv_bias'][1])
    head_shape = (rows_here, SEQ, HEADS, HEAD_DIM)
    context = attend(queries.reshape(head_shape), keys_low.reshape(head_shape), values_low.reshape(head_shape), seg_blk, len_blk)
    context = low(context.reshape(token_count, D))
    proj_ints, step_proj = quantize_next(params['proj_weight'], peaks[2])
    attn_out = low_back(jnp.dot(context, proj_ints, precision=highest)) * step_proj + params['proj_bias']
    normed = layer_norm(tok_blk + attn_out, params['first_gain'], params['first_shift'])
    up_ints, step_up = quantize_next(params['up_weight'], peaks[3])
    pre_act = low_back(jnp.dot(low(normed), up_ints, precision=highest)) * step_up + params['up_bias']
    activated = jax.nn.gelu(pre_act, approximate=False)
    down_ints, step_down = quantize_next(params['down_weight'], peaks[4])
    branch = low_back(jnp.dot(low(activated), down_ints, precision=highest)) * step_down + params['down_bias']
    result = layer_norm(normed + branch, params['second_gain'], params['second_shift'])
    return (result, tuple(residues))

def reference(tokens, segment_ids, row_lengths, qkv_weight, qv_bias, proj_weight, proj_bias, first_gain, first_shift, up_weight, up_bias, down_weight, down_bias, second_gain, second_shift, out_grad):
    params = {'qkv_weight': qkv_weight.astype(jnp.float32), 'qv_bias': qv_bias.astype(jnp.float32), 'proj_weight': proj_weight.astype(jnp.float32), 'proj_bias': proj_bias.astype(jnp.float32), 'first_gain': first_gain.astype(jnp.float32), 'first_shift': first_shift.astype(jnp.float32), 'up_weight': up_weight.astype(jnp.float32), 'up_bias': up_bias.astype(jnp.float32), 'down_weight': down_weight.astype(jnp.float32), 'down_bias': down_bias.astype(jnp.float32), 'second_gain': second_gain.astype(jnp.float32), 'second_shift': second_shift.astype(jnp.float32)}
    token_vals = tokens.astype(jnp.float32)
    block_rows = math.gcd(ROWS, 8)
    block_count = ROWS // block_rows
    tok_blocks = token_vals.reshape(block_count, block_rows * SEQ, D)
    seg_blocks = segment_ids.reshape(block_count, block_rows, SEQ)
    len_blocks = row_lengths.reshape(block_count, block_rows)
    grad_blocks = out_grad.astype(jnp.float32).reshape(block_count, block_rows * SEQ, D)
    peak_tokens = jnp.max(jnp.abs(token_vals))
    peak_qkv = lax.optimization_barrier(jnp.max(jnp.abs(params['qkv_weight']), axis=(1, 2)))
    peak_proj = jnp.max(jnp.abs(params['proj_weight']))
    peak_up = jnp.max(jnp.abs(params['up_weight']))
    peak_down = jnp.max(jnp.abs(params['down_weight']))
    peaks = (peak_tokens, peak_qkv, peak_proj, peak_up, peak_down)

    def train(carry, pieces):
        tok_blk, seg_blk, len_blk, grad_blk = pieces
        unused, fixed = block_forward(params, peaks, tok_blk, seg_blk, len_blk, None)

        def forward(values, weights):
            return block_forward(weights, peaks, values, seg_blk, len_blk, fixed)[0]
        result, pull = jax.vjp(forward, tok_blk, params)
        tok_grad, weight_grads = pull(grad_blk)
        return (jax.tree.map(jnp.add, carry, weight_grads), (result.astype(jnp.bfloat16), tok_grad))
    zeros = jax.tree.map(jnp.zeros_like, params)
    totals, (outs, tok_grads) = lax.scan(train, zeros, (tok_blocks, seg_blocks, len_blocks, grad_blocks))
    return (outs.reshape(TOKENS, D), tok_grads.reshape(TOKENS, D), totals['qkv_weight'], totals['qv_bias'], totals['proj_weight'], totals['proj_bias'], totals['first_gain'], totals['first_shift'], totals['up_weight'], totals['up_bias'], totals['down_weight'], totals['down_bias'], totals['second_gain'], totals['second_shift'])
```

```python
import jax
import jax.numpy as jnp
from jax import lax
from jax.experimental import pallas as pl
from jax.experimental.pallas import tpu as pltpu
from jax.sharding import PartitionSpec as P

D = 512
HEADS = 8
HEAD_DIM = 64
FF = 2048
SEQ = 512
PAIRS = 4
LANES = 128
LEVELS = 127.0
EPS = 1e-12
MASKED = -1e30
LOG2E = 1.4426950408889634
SCORE_SCALE = 0.125 * LOG2E
VMEM_LIMIT = 58 << 20
F32 = jnp.float32
BF16 = jnp.bfloat16
TILES = ((0, 256, 0, 384), (256, 512, 128, 512))


def rounded(scaled):
    magnitude = jnp.floor(jnp.abs(scaled) + 0.5)
    return jnp.where(scaled < 0.0, -magnitude, magnitude)


def dot_nn(a, b):
    return lax.dot_general(a, b, (((1,), (0,)), ((), ())), preferred_element_type=F32)


def dot_nt(a, b):
    return lax.dot_general(a, b, (((1,), (1,)), ((), ())), preferred_element_type=F32)


def dot_tn(a, b):
    return lax.dot_general(a, b, (((0,), (0,)), ((), ())), preferred_element_type=F32)


def head_mask(head, rows):
    lane = lax.broadcasted_iota(jnp.int32, (rows, LANES), 1)
    return (lane < HEAD_DIM) if head == 0 else (lane >= HEAD_DIM)


def both(left, right):
    return jnp.concatenate(
        [left[:, :128], left[:, 128:] + right[:, :256], right[:, 256:]], axis=1
    )


MESH = pl.DeviceIdType.MESH
GROUPS = ("core", "x", "y", "z")


def group_sizes(tensor_size, dp_size):
    return {"core": 2, "x": tensor_size // 2, "y": 2, "z": dp_size // 2}


class Place:
    def __init__(self, sizes):
        t, d = lax.axis_index("tensor"), lax.axis_index("dp")
        self.sizes = sizes
        self.part = t
        self.at = {"core": t % 2, "x": t // 2, "y": d % 2, "z": d // 2}

    def size(self, group):
        return self.sizes[group]

    def peer(self, group, k):
        at = dict(self.at)
        at[group] = (at[group] + k) % self.sizes[group]
        return at[group], (at["z"] * 2 + at["y"], at["x"] * 2 + at["core"])

    def greet(self):
        barrier = pltpu.get_barrier_semaphore()
        count = 0
        for group in GROUPS:
            for k in range(1, self.sizes[group]):
                pl.semaphore_signal(
                    barrier, inc=1, device_id=self.peer(group, k)[1], device_id_type=MESH
                )
                count += 1
        pl.semaphore_wait(barrier, count)


class Sems:
    def __init__(self, send, recv):
        self.send, self.recv = send, recv

    def copy(self, at, source, target, device):
        return pltpu.make_async_remote_copy(
            src_ref=source,
            dst_ref=target,
            send_sem=self.send.at[at],
            recv_sem=self.recv.at[at],
            device_id=device,
            device_id_type=MESH,
        )


def exchange(place, group, source, target, sems, base):
    copies = []
    for k in range(1, place.size(group)):
        index, device = place.peer(group, k)
        copies.append(sems.copy(base + k - 1, source(k, index), target(k, index), device))
    return copies


def add(first, *others):
    total = first.astype(F32)
    for other in others:
        total = total + other.astype(F32)
    return total.astype(BF16)


class Stream:
    phases = 6

    def __init__(self, place, order, grad, held, got_c, got_1, got_2, got_z, out, send, recv, own):
        self.place, self.order, self.grad, self.held, self.out = place, order, grad, held, out
        self.got_c, self.got_1, self.got_2, self.got_z = got_c, got_1, got_2, got_z
        self.sems, self.own = Sems(send, recv), own

    def local(self):
        if self.own is None:
            return []
        return [
            pltpu.make_async_copy(
                self.grad(2 * i + self.place.at["core"]), self.held.at[i], self.own.at[i]
            )
            for i in range(self.place.size("x"))
        ]

    def copies(self, phase):
        place, at, held = self.place, self.place.at, self.held
        nx, nz = place.size("x"), place.size("z")
        base = [0, nx, 2 * nx, 3 * nx, 3 * nx + nz, 3 * nx + 2 * nz][phase]
        sems = self.sems
        if phase == 0:
            other, device = place.peer("core", 1)
            return [
                sems.copy(i, self.grad(2 * i + other), self.got_c.at[i], device) for i in range(nx)
            ]
        if phase == 1 and self.order == "xy":
            return exchange(
                place, "x", lambda k, j: held.at[j], lambda k, j: self.got_1.at[k - 1], sems, base
            )
        if phase == 2 and self.order == "xy":
            return exchange(
                place, "y", lambda k, j: held.at[at["x"], j], lambda k, j: self.got_2.at[0], sems, base
            )
        if phase == 1:
            other, device = place.peer("y", 1)
            return [
                sems.copy(base + i, held.at[i, other], self.got_1.at[i], device) for i in range(nx)
            ]
        if phase == 2:
            return exchange(
                place,
                "x",
                lambda k, j: held.at[j, at["y"]],
                lambda k, j: self.got_2.at[k - 1],
                sems,
                base,
            )
        if phase == 3:
            return exchange(
                place,
                "z",
                lambda k, j: held.at[at["x"], at["y"], j],
                lambda k, j: self.got_z.at[k - 1],
                sems,
                base,
            )
        if phase == 4:
            piece = self.out.at[at["y"], at["z"]]
            return exchange(place, "z", lambda k, j: piece, lambda k, j: piece, sems, base)
        half = self.out.at[at["y"]]
        return exchange(place, "y", lambda k, j: half, lambda k, j: half, sems, base)

    def start(self, phase):
        for copy in self.copies(phase) + (self.local() if phase == 0 else []):
            copy.start()

    def finish(self, phase):
        for copy in self.copies(phase) + (self.local() if phase == 0 else []):
            copy.wait()
        at, held = self.place.at, self.held
        nx, nz = self.place.size("x"), self.place.size("z")
        if phase == 0:
            for i in range(nx):
                for y in range(2):
                    own = held[i, y] if self.own is not None else self.grad(2 * i + at["core"])[y]
                    held[i, y] = add(own, self.got_c[i, y])
        elif phase == 1 and self.order == "xy":
            for y in range(2):
                held[at["x"], y] = add(
                    held[at["x"], y], *[self.got_1[k, y] for k in range(nx - 1)]
                )
        elif phase == 1:
            for i in range(nx):
                held[i, at["y"]] = add(held[i, at["y"]], self.got_1[i])
        elif phase == 2:
            count = 1 if self.order == "xy" else nx - 1
            held[at["x"], at["y"]] = add(
                held[at["x"], at["y"]], *[self.got_2[k] for k in range(count)]
            )
        elif phase == 3:
            self.out[at["y"], at["z"]] = add(
                held[at["x"], at["y"], at["z"]], *[self.got_z[k] for k in range(nz - 1)]
            )


def stream_scratch(sizes, order, rows, lanes):
    nx, nz = sizes["x"], sizes["z"]
    count = 3 * nx + 2 * nz + 1
    piece = (nz, rows, lanes)
    first = (nx - 1, 2) if order == "xy" else (nx,)
    second = (1,) if order == "xy" else (nx - 1,)
    return [
        pltpu.VMEM((nx, 2) + piece, BF16),
        pltpu.VMEM((nx, 2) + piece, BF16),
        pltpu.VMEM(first + piece, BF16),
        pltpu.VMEM(second + piece, BF16),
        pltpu.VMEM((nz - 1,) + piece[1:], BF16),
        pltpu.VMEM((2,) + piece, BF16),
        pltpu.SemaphoreType.DMA((count,)),
        pltpu.SemaphoreType.DMA((count,)),
        pltpu.SemaphoreType.DMA((nx,)),
    ]


class Small:
    def __init__(self, place, combine, slots, send, recv):
        self.place, self.combine, self.slots, self.sems = place, combine, slots, Sems(send, recv)

    def offsets(self, phase):
        sizes = [self.place.size(g) for g in GROUPS]
        return sum(sizes[:phase]), sum(sizes[:phase]) - phase

    def copies(self, phase):
        slot, sem = self.offsets(phase)
        return exchange(
            self.place,
            GROUPS[phase],
            lambda k, j: self.slots.at[slot],
            lambda k, j: self.slots.at[slot + k],
            self.sems,
            sem,
        )

    def start(self, phase, values):
        self.slots[self.offsets(phase)[0]] = values
        for copy in self.copies(phase):
            copy.start()

    def finish(self, phase):
        for copy in self.copies(phase):
            copy.wait()
        slot = self.offsets(phase)[0]
        count, me = self.place.size(GROUPS[phase]), self.place.at[GROUPS[phase]]
        total = None
        for member in range(count):
            term = self.slots[slot + (me + count - member) % count]
            total = term if total is None else self.combine(total, term)
        return total


def small_scratch(sizes, rows, lanes):
    total = sum(sizes[g] for g in GROUPS)
    return [
        pltpu.VMEM((total, rows, lanes), F32),
        pltpu.SemaphoreType.DMA((total - 4,)),
        pltpu.SemaphoreType.DMA((total - 4,)),
    ]


class Gather:
    def __init__(self, place, own, every, send, recv, keep):
        self.place, self.own, self.every, self.sems, self.keep = place, own, every, Sems(send, recv), keep

    def far(self):
        place = self.place
        mine = self.every.at[place.part]
        return exchange(place, "x", lambda k, j: self.own, lambda k, j: mine, self.sems, 0)

    def near(self, step):
        place = self.place
        nx = place.size("x")
        device = place.peer("core", 1)[1]
        if step == 0:
            return self.sems.copy(nx - 1, self.own, self.every.at[place.part], device)
        chip = (place.at["x"] + nx - step) % nx
        block = self.every.at[chip * 2 + place.at["core"]]
        return self.sems.copy(nx - 1 + step, block, block, device)

    def mine(self):
        return pltpu.make_async_copy(self.own, self.every.at[self.place.part], self.keep.at[0])

    def start(self):
        for copy in self.far():
            copy.start()
        self.near(0).start()
        self.mine().start()

    def forward(self):
        for copy in self.far():
            copy.wait()
        for k in range(1, self.place.size("x")):
            self.near(k).start()

    def finish(self):
        for k in range(self.place.size("x")):
            self.near(k).wait()
        self.mine().wait()


def gather_scratch(sizes):
    count = 2 * sizes["x"] - 1
    return [
        pltpu.SemaphoreType.DMA((count,)),
        pltpu.SemaphoreType.DMA((count,)),
        pltpu.SemaphoreType.DMA((1,)),
    ]


def split_rows(rows, pieces):
    return -(-rows // (pieces * 8)) * 8


def spread(values, shape):
    count = 1
    for size in shape[:-1]:
        count *= size
    if count > values.shape[0]:
        zeros = jnp.zeros((count - values.shape[0], values.shape[1]), values.dtype)
        values = jnp.concatenate([values, zeros], axis=0)
    return values.reshape(shape)


def tile_rows(rows, height, lanes):
    filled = [r if r.shape[1] == lanes else jnp.concatenate([r, jnp.zeros((1, lanes - r.shape[1]), F32)], axis=1) for r in rows]
    at = lax.broadcasted_iota(jnp.int32, (height, lanes), 0)
    total = jnp.zeros((height, lanes), F32)
    for n, r in enumerate(filled):
        total = jnp.where(at == n, r, total)
    return total


def top(values):
    peak = jnp.max(jnp.abs(values.astype(F32)), axis=0, keepdims=True)
    return jnp.max(peak, axis=1, keepdims=True)


def attend_kernel(
    sizes,
    lens,
    tok_ref,
    seg_ref,
    qkv_sh,
    qvb_sh,
    proj_sh,
    up_sh,
    down_sh,
    ub_sh,
    ints_ref,
    qkv_ref,
    probs_ref,
    ctx_ref,
    w_ref,
    step_ref,
    bias_ref,
    proj_all,
    up_all,
    down_all,
    mask_s,
    raw_all,
    bias_all,
    bias_own,
    proj_own,
    up_own,
    down_own,
    *sems,
):
    row = pl.program_id(0)
    last = pl.num_programs(0) - 1
    place = Place(sizes)
    parts = 2 * sizes["x"]
    width = D // parts
    early = [
        Gather(place, own, every, *sems[3 * n : 3 * n + 3])
        for n, (own, every) in enumerate(((qkv_sh, raw_all), (bias_own, bias_all)))
    ]
    late = [
        Gather(place, own, every, *sems[6 + 3 * n : 9 + 3 * n])
        for n, (own, every) in enumerate(
            ((up_own, up_all), (down_own, down_all), (proj_own, proj_all))
        )
    ]
    peaks = Small(place, jnp.maximum, *sems[15:18])

    @pl.when(row == 0)
    def _():
        place.greet()
        bias_own[...] = tile_rows(
            [ub_sh[...].astype(F32), qvb_sh[0:1].astype(F32), qvb_sh[1:2].astype(F32)],
            8,
            ub_sh.shape[1],
        )
        for gather in early:
            gather.start()
        tops = [top(tok_ref[...])] + [top(qkv_sh[i]) for i in range(3)]
        tops += [top(proj_sh[...]), top(up_sh[...]), top(down_sh[...])]
        total = tile_rows([jnp.broadcast_to(t, (1, LANES)) for t in tops], 8, LANES)
        for phase in range(4):
            peaks.start(phase, total)
            total = peaks.finish(phase)
        step_ref[...] = total / LEVELS
        up_own[...] = rounded(up_sh[...].astype(F32) / step_ref[5:6, 0:1]).astype(BF16)
        down_own[...] = rounded(down_sh[...].astype(F32) / step_ref[6:7, 0:1]).astype(BF16)
        proj_own[...] = rounded(proj_sh[...].astype(F32) / step_ref[4:5, 0:1]).astype(BF16)
        for gather in early:
            gather.forward()
        for gather in late:
            gather.start()
        for gather in early:
            gather.finish()
        bias_ref[...] = bias_all[...]
        for t in range(parts):
            for i in range(3):
                w_ref[i, :, t * width : (t + 1) * width] = rounded(
                    raw_all[t, i].astype(F32) / step_ref[1 + i : 2 + i, 0:1]
                ).astype(BF16)

    @pl.when(row == last)
    def _():
        for gather in late:
            gather.forward()

    step_tokens = step_ref[0:1, 0:1]
    tok = tok_ref[pl.ds(pl.multiple_of(row * SEQ, SEQ), SEQ), :]
    ints = rounded(tok.astype(F32) / step_tokens).astype(BF16)
    ints_ref[...] = ints
    biases = [
        jnp.concatenate([bias_all[t, r : r + 1, :width] for t in range(parts)], axis=1)
        for r in (1, 2)
    ]
    for i in range(3):
        raw = dot_nn(ints, w_ref[i]) * (step_tokens * step_ref[1 + i : 2 + i, 0:1])
        if i == 0:
            raw = (raw + biases[0]) * SCORE_SCALE
        if i == 2:
            raw = raw + biases[1]
        qkv_ref[:, i * D : (i + 1) * D] = raw.astype(BF16)
    seg_q = seg_ref[0].astype(F32)
    length = lens[row]
    spot = lax.broadcasted_iota(jnp.int32, (8, SEQ), 1)
    seg_k = jnp.where(spot < length, jnp.broadcast_to(seg_q, (8, SEQ)), -1.0)
    seg_k = jnp.transpose(seg_k)[:, 0:1]
    for n, (k0, k1, q0, q1) in enumerate(TILES):
        keys = lax.broadcasted_iota(jnp.int32, (k1 - k0, q1 - q0), 0) + k0
        queries = lax.broadcasted_iota(jnp.int32, (k1 - k0, q1 - q0), 1) + q0
        allowed = (seg_k[k0:k1] == seg_q[:, q0:q1]) | (keys == queries)
        mask_s[n] = jnp.where(allowed, 0.0, MASKED)

    def pair_step(p, carry):
        at = pl.multiple_of(p * LANES, LANES)
        q_pair = qkv_ref[:, pl.ds(at, LANES)]
        k_pair = qkv_ref[:, pl.ds(D + at, LANES)]
        v_pair = qkv_ref[:, pl.ds(2 * D + at, LANES)]
        v_t = jnp.transpose(v_pair)
        parts = []
        for h in range(2):
            q_head = jnp.where(head_mask(h, SEQ), q_pair, jnp.zeros_like(q_pair))
            scores = [
                dot_nt(k_pair[k0:k1], q_head[q0:q1]) + mask_s[n]
                for n, (k0, k1, q0, q1) in enumerate(TILES)
            ]
            peak = [jnp.max(s, axis=0, keepdims=True) for s in scores]
            high = jnp.concatenate(
                [
                    peak[0][:, :128],
                    jnp.maximum(peak[0][:, 128:], peak[1][:, :256]),
                    peak[1][:, 256:],
                ],
                axis=1,
            )
            weights = [
                jnp.exp2(s - high[:, q0:q1]) for s, (k0, k1, q0, q1) in zip(scores, TILES)
            ]
            totals = both(*[jnp.sum(w, axis=0, keepdims=True) for w in weights])
            inverse = 1.0 / totals
            outs = []
            for n, (k0, k1, q0, q1) in enumerate(TILES):
                probs = (weights[n] * inverse[:, q0:q1]).astype(BF16)
                probs_ref[0, 2 * p + h, n] = probs
                outs.append(dot_nn(v_t[h * 64 : h * 64 + 64, k0:k1], probs))
            parts.append(both(*outs))
        context_t = jnp.concatenate(parts, axis=0)
        ctx_ref[:, pl.ds(at, LANES)] = jnp.transpose(context_t).astype(BF16)
        return carry

    lax.fori_loop(0, PAIRS, pair_step, 0)

    @pl.when(row == last)
    def _():
        for gather in late:
            gather.finish()


def attend(sizes, lens, tokens, segments, qkv_w, qv_bias, proj_w, up_w, down_w, up_b):
    rows = tokens.shape[0] // SEQ
    parts = 2 * sizes["x"]
    hbm = pl.BlockSpec(memory_space=pl.ANY)
    gathered = [(w.shape, BF16) for w in (proj_w, up_w, down_w)]

    def whole(*shape):
        return pl.BlockSpec(shape, lambda i, *_: (0,) * len(shape))

    return pl.pallas_call(
        lambda *refs: attend_kernel(sizes, *refs),
        name="attend",
        grid_spec=pltpu.PrefetchScalarGridSpec(
            num_scalar_prefetch=1,
            grid=(rows,),
            in_specs=[
                whole(*tokens.shape),
                pl.BlockSpec((1, 1, SEQ), lambda i, *_: (i, 0, 0)),
                whole(*qkv_w.shape),
                whole(*qv_bias.shape),
                whole(*proj_w.shape),
                whole(*up_w.shape),
                whole(*down_w.shape),
                whole(*up_b.shape),
            ],
            out_specs=[
                pl.BlockSpec((SEQ, D), lambda i, *_: (i, 0)),
                pl.BlockSpec((SEQ, 3 * D), lambda i, *_: (i, 0)),
                pl.BlockSpec((1, HEADS, 2, 256, 384), lambda i, *_: (i, 0, 0, 0, 0)),
                pl.BlockSpec((SEQ, D), lambda i, *_: (i, 0)),
                whole(3, D, D),
                whole(8, LANES),
                whole(parts, 8, up_b.shape[1]),
                hbm,
                hbm,
                hbm,
            ],
            scratch_shapes=[
                pltpu.VMEM((2, 256, 384), F32),
                pltpu.VMEM((parts,) + qkv_w.shape, BF16),
                pltpu.VMEM((parts, 8, up_b.shape[1]), F32),
                pltpu.VMEM((8, up_b.shape[1]), F32),
            ]
            + [pltpu.VMEM(w.shape, BF16) for w in (proj_w, up_w, down_w)]
            + sum([gather_scratch(sizes) for _ in range(5)], [])
            + small_scratch(sizes, 8, LANES),
        ),
        out_shape=[
            jax.ShapeDtypeStruct((rows * SEQ, D), BF16),
            jax.ShapeDtypeStruct((rows * SEQ, 3 * D), BF16),
            jax.ShapeDtypeStruct((rows, HEADS, 2, 256, 384), BF16),
            jax.ShapeDtypeStruct((rows * SEQ, D), BF16),
            jax.ShapeDtypeStruct((3, D, D), BF16),
            jax.ShapeDtypeStruct((8, LANES), F32),
            jax.ShapeDtypeStruct((parts, 8, up_b.shape[1]), F32),
        ]
        + [jax.ShapeDtypeStruct((parts,) + w.shape, BF16) for w in (proj_w, up_w, down_w)],
        compiler_params=pltpu.CompilerParams(
            vmem_limit_bytes=VMEM_LIMIT, collective_id=0, has_side_effects=True
        ),
        cost_estimate=pl.CostEstimate(
            flops=rows * 3 * 10**9, bytes_accessed=rows * 6 * 10**6, transcendentals=rows * 2 * 10**6
        ),
    )(lens, tokens, segments, qkv_w, qv_bias, proj_w, up_w, down_w, up_b)

GELU_P = 0.3275911 * 0.7071067811865476
GELU_A = (0.254829592, -0.284496736, 1.421413741, -1.453152027, 1.061405429)
INV_SQRT_2PI = 0.3989422804014327


def gelu_pair(pre):
    base = 1.0 + GELU_P * jnp.abs(pre)
    t = pl.reciprocal(base, approx=True)
    t = t * (2.0 - base * t)
    bell = jnp.exp2(pre * pre * (-0.5 * LOG2E))
    poly = 0.5 * GELU_A[4]
    for a in (GELU_A[3], GELU_A[2], GELU_A[1], GELU_A[0]):
        poly = poly * t + 0.5 * a
    tail = poly * t * bell
    cdf = jnp.where(pre < 0.0, tail, 1.0 - tail)
    return pre * cdf, cdf + (pre * INV_SQRT_2PI) * bell


def fold_rows(values):
    total = values[0:8]
    for r in range(8, values.shape[0], 8):
        total = total + values[r : r + 8]
    return total


def normalize(values):
    centred = values - jnp.mean(values, axis=-1, keepdims=True)
    inverse = lax.rsqrt(jnp.mean(centred * centred, axis=-1, keepdims=True) + EPS)
    return centred * inverse, inverse


def norm_back(scaled, standard, inverse):
    return inverse * (
        scaled
        - jnp.mean(scaled, axis=-1, keepdims=True)
        - standard * jnp.mean(scaled * standard, axis=-1, keepdims=True)
    )


TB = 256


def ffn_kernel(
    step_ref,
    bias_ref,
    tok_ref,
    ctx_ref,
    og_ref,
    proj_ref,
    up_ref,
    down_ref,
    pb_ref,
    fg_ref,
    fs_ref,
    db_ref,
    sg_ref,
    ss_ref,
    out_ref,
    first_ref,
    gctx_ref,
    dproj_ref,
    dup_ref,
    ddown_ref,
    dub_ref,
    dvec_ref,
    act_s,
    slope_s,
    dproj_s,
    dup_s,
    ddown_s,
    dub_s,
    dvec_s,
):
    at = pl.program_id(0)
    last = pl.num_programs(0) - 1
    parts = up_ref.shape[0]
    step_proj, step_up, step_down = [step_ref[r : r + 1, 0:1] for r in (4, 5, 6)]

    @pl.when(at == 0)
    def _():
        dproj_s[...] = jnp.zeros_like(dproj_s)
        dup_s[...] = jnp.zeros_like(dup_s)
        ddown_s[...] = jnp.zeros_like(ddown_s)
        dub_s[...] = jnp.zeros_like(dub_s)
        dvec_s[...] = jnp.zeros_like(dvec_s)

    proj_bias, first_gain, first_shift, down_bias, second_gain, second_shift = [
        r[...].astype(F32) for r in (pb_ref, fg_ref, fs_ref, db_ref, sg_ref, ss_ref)
    ]
    ctx = ctx_ref[...]
    first_in = tok_ref[...].astype(F32) + (dot_nn(ctx, proj_ref[...]) * step_proj + proj_bias)
    n1, r1 = normalize(first_in)
    normed = n1 * first_gain + first_shift
    low = normed.astype(BF16)
    branch = None
    for t in range(parts):
        pre = dot_nn(low, up_ref[t]) * step_up + bias_ref[t, 0:1]
        act, slope = gelu_pair(pre)
        act = act.astype(BF16)
        act_s[t] = act
        slope_s[t] = slope
        term = dot_nn(act, down_ref[t])
        branch = term if branch is None else branch + term
    second_in = normed + (branch * step_down + down_bias)
    n2, r2 = normalize(second_in)
    out_ref[...] = (n2 * second_gain + second_shift).astype(BF16)
    og = og_ref[...].astype(F32)
    grad_second = norm_back(og * second_gain, n2, r2)
    dvec_s[4] += fold_rows(og * n2)
    dvec_s[5] += fold_rows(og)
    dvec_s[3] += fold_rows(grad_second)
    grad_down = (grad_second * step_down).astype(BF16)
    back = grad_second
    for t in range(parts):
        grad_pre = dot_nt(grad_down, down_ref[t]) * slope_s[t]
        dub_s[t] += fold_rows(grad_pre)
        grad_up = (grad_pre * step_up).astype(BF16)
        back = back + dot_nt(grad_up, up_ref[t])
        dup_s[t] += dot_tn(low, grad_up)
        ddown_s[t] += dot_tn(grad_down, act_s[t])
    dvec_s[1] += fold_rows(back * n1)
    dvec_s[2] += fold_rows(back)
    grad_first = norm_back(back * first_gain, n1, r1)
    dvec_s[0] += fold_rows(grad_first)
    first_ref[...] = grad_first
    grad_proj = (grad_first * step_proj).astype(BF16)
    dproj_s[...] += dot_tn(ctx, grad_proj)
    gctx_ref[...] = dot_nt(grad_proj, proj_ref[...]).astype(BF16)

    @pl.when(at == last)
    def _():
        width = D // parts
        for t in range(parts):
            rows = dproj_s[t * width : (t + 1) * width]
            dproj_ref[t] = spread(rows.astype(BF16), dproj_ref.shape[1:])
            dup_ref[t] = spread(dup_s[t].astype(BF16), dup_ref.shape[1:])
            ddown_ref[t] = spread(ddown_s[t].astype(BF16), ddown_ref.shape[1:])
            dub_ref[t] = jnp.sum(dub_s[t], axis=0, keepdims=True)
        dvec_ref[...] = jnp.sum(dvec_s[...], axis=1)


def feed_forward(sizes, steps, biases, tokens, ctx, out_grad, proj, up, down, vecs):
    count = tokens.shape[0]
    parts, nz = 2 * sizes["x"], sizes["z"]
    wide = FF // parts
    split = (parts, 2, 2, nz, split_rows(D, 4 * nz), wide)
    split_proj = (parts, 2, nz, split_rows(D // parts, 2 * nz), D)
    block = pl.BlockSpec((TB, D), lambda i, *_: (i, 0))

    def whole(*shape):
        return pl.BlockSpec(shape, lambda i, *_: (0,) * len(shape))

    return pl.pallas_call(
        ffn_kernel,
        name="feed_forward",
        grid=(count // TB,),
        in_specs=[
            whole(8, LANES),
            whole(parts, 8, wide),
            block,
            block,
            block,
            whole(D, D),
            whole(parts, D, wide),
            whole(parts, wide, D),
        ]
        + [whole(1, D)] * 6,
        out_specs=[
            block,
            block,
            block,
            whole(*split_proj),
            whole(*split),
            whole(*split),
            whole(parts, 1, wide),
            whole(6, D),
        ],
        scratch_shapes=[
            pltpu.VMEM((parts, TB, wide), BF16),
            pltpu.VMEM((parts, TB, wide), F32),
            pltpu.VMEM((D, D), F32),
            pltpu.VMEM((parts, D, wide), F32),
            pltpu.VMEM((parts, D, wide), F32),
            pltpu.VMEM((parts, 8, wide), F32),
            pltpu.VMEM((6, 8, D), F32),
        ],
        out_shape=[
            jax.ShapeDtypeStruct((count, D), BF16),
            jax.ShapeDtypeStruct((count, D), F32),
            jax.ShapeDtypeStruct((count, D), BF16),
            jax.ShapeDtypeStruct(split_proj, BF16),
            jax.ShapeDtypeStruct(split, BF16),
            jax.ShapeDtypeStruct(split, BF16),
            jax.ShapeDtypeStruct((parts, 1, wide), F32),
            jax.ShapeDtypeStruct((6, D), F32),
        ],
        compiler_params=pltpu.CompilerParams(vmem_limit_bytes=VMEM_LIMIT),
        cost_estimate=pl.CostEstimate(
            flops=count * 14 * 10**6, bytes_accessed=count * 12000, transcendentals=count * 4096
        ),
    )(steps, biases, tokens, ctx, out_grad, proj, up, down, *[v.reshape(1, D) for v in vecs])


PLANS = (
    ((0, 2), (2, 5), (5, 7), (7, 9), (9, 12), (12, 14)),
    ((0, 2), (2, 5), (5, 7), (7, 10), (10, 12), (12, 14)),
    ((0, 2), (4, 7), (7, 9), (9, 11), (11, 14), (14, 16)),
    ((0, 2), (4, 7), (7, 9), (9, 12), (12, 14), (14, 16)),
    ((0, 2), (6, 8), (8, 10), (10, 12), (12, 14), (14, 16)),
)
ORDERS = ("xy", "yx", "xy", "yx", "xy", "xy", "yx")


def passing(grads, weights, step):
    return jnp.where(weights.astype(F32) == 0.0, 0.0, grads.astype(F32)) / step


def back_kernel(
    sizes,
    step_ref,
    tok_ref,
    ints_ref,
    qkv_ref,
    probs_ref,
    ctx_ref,
    gctx_ref,
    first_ref,
    w_ref,
    dproj_hbm,
    dup_hbm,
    ddown_hbm,
    dub_ref,
    dvec_ref,
    qkv_sh,
    proj_sh,
    up_sh,
    down_sh,
    tg_ref,
    dqkv_out,
    dqv_out,
    dproj_out,
    dup_out,
    dub_out,
    ddown_out,
    vec_out,
    grad_s,
    dqkv_s,
    dqv_s,
    part_s,
    *scratch,
):
    step = pl.program_id(0)
    rows = grad_s.shape[0]
    place = Place(sizes)
    parts = 2 * sizes["x"]
    width = D // parts
    step_tokens = step_ref[0:1, 0:1]
    sources = [
        lambda t: dup_hbm.at[t, 0],
        lambda t: ddown_hbm.at[t, 0],
        lambda t: dup_hbm.at[t, 1],
        lambda t: ddown_hbm.at[t, 1],
        lambda t: dproj_hbm.at[t],
        lambda t: part_s.at[t, 0],
        lambda t: part_s.at[t, 1],
    ]
    streams = []
    for n, source in enumerate(sources):
        refs = scratch[9 * n : 9 * n + 9]
        own = refs[8] if n < 5 else None
        streams.append(Stream(place, ORDERS[n], source, *refs[:8], own))
    sums = Small(place, jnp.add, *scratch[63:66])

    @pl.when(step == 0)
    def _():
        dqkv_s[...] = jnp.zeros_like(dqkv_s)
        dqv_s[...] = jnp.zeros_like(dqv_s)
        place.greet()

    def advance(tick):
        for now in range(16):
            done = [(s, k) for s, plan in enumerate(PLANS) for k, p in enumerate(plan) if p[1] == now]
            begun = [(s, k) for s, plan in enumerate(PLANS) for k, p in enumerate(plan) if p[0] == now]
            if done or begun:

                @pl.when(tick == now)
                def _():
                    for s, k in done:
                        streams[s].finish(k)
                    for s, k in begun:
                        streams[s].start(k)

    def pair_step(p, carry):
        for n in range(16 // (PAIRS * rows)):
            advance((step * PAIRS + p) * (16 // (PAIRS * rows)) + n)
        at = pl.multiple_of(p * LANES, LANES)
        q_pair = qkv_ref[:, pl.ds(at, LANES)]
        k_pair = qkv_ref[:, pl.ds(D + at, LANES)]
        v_pair = qkv_ref[:, pl.ds(2 * D + at, LANES)]
        g_pair = gctx_ref[:, pl.ds(at, LANES)]
        c_pair = ctx_ref[:, pl.ds(at, LANES)]
        k_t = jnp.transpose(k_pair)
        product = (g_pair.astype(F32) * c_pair.astype(F32)).astype(BF16)
        d_keys = [None, None]
        d_values = [None, None]
        parts = []
        for h in range(2):
            mask = head_mask(h, SEQ)
            q_head = jnp.where(mask, q_pair, jnp.zeros_like(q_pair))
            g_head = jnp.where(mask, g_pair, jnp.zeros_like(g_pair))
            ones = jnp.where(head_mask(h, 8), 1.0, 0.0).astype(BF16)
            centre = dot_nt(ones, product)[0:1]
            outs = []
            for n, (k0, k1, q0, q1) in enumerate(TILES):
                probs = probs_ref[0, 2 * p + h, n]
                gp = dot_nt(v_pair[k0:k1], g_head[q0:q1])
                gs = (probs.astype(F32) * (gp - centre[:, q0:q1])).astype(BF16)
                dv = dot_nn(probs, g_head[q0:q1])
                dk = dot_nn(gs, q_head[q0:q1])
                d_values[n] = dv if h == 0 else d_values[n] + dv
                d_keys[n] = dk if h == 0 else d_keys[n] + dk
                outs.append(dot_nn(k_t[h * 64 : h * 64 + 64, k0:k1], gs))
            parts.append(both(*outs))
        d_q = jnp.transpose(jnp.concatenate(parts, axis=0)) * 0.125
        dqv_s[0, :, pl.ds(at, LANES)] += fold_rows(d_q)
        grad_s[step, :, pl.ds(at, LANES)] = (d_q * (step_tokens * step_ref[1:2, 0:1])).astype(BF16)
        for n, (k0, k1, q0, q1) in enumerate(TILES):
            grad_s[step, k0:k1, pl.ds(D + at, LANES)] = (
                d_keys[n] * (step_tokens * step_ref[2:3, 0:1] * (1.0 / LOG2E))
            ).astype(BF16)
            dqv_s[1, :, pl.ds(at, LANES)] += fold_rows(d_values[n])
            grad_s[step, k0:k1, pl.ds(2 * D + at, LANES)] = (
                d_values[n] * (step_tokens * step_ref[3:4, 0:1])
            ).astype(BF16)
        return carry

    @pl.when(step < rows)
    def _():
        lax.fori_loop(0, PAIRS, pair_step, 0)
        for i in range(3):
            dqkv_s[i] += dot_tn(grad_s[step, :, i * D : (i + 1) * D], ints_ref[...])

    @pl.when(step == rows)
    def _():
        for t in range(parts):
            piece = jnp.concatenate(
                [dqkv_s[i, t * width : (t + 1) * width] for i in range(3)], axis=0
            )
            part_s[t] = spread(piece.astype(BF16), part_s.shape[1:])
        for stream in streams[5:]:
            stream.start(0)
        dqv = jnp.sum(dqv_s[...], axis=1)
        vec = [dvec_ref[r : r + 1] for r in range(6)] + [dqv[0:1], dqv[1:2]]
        dub = jnp.concatenate([dub_ref[t] for t in range(parts)], axis=1)
        vec += [dub[:, r * D : (r + 1) * D] for r in range(4)]
        sums.start(0, tile_rows(vec, 16, D))
        for s, plan in enumerate(PLANS):
            for k, p in enumerate(plan):
                if p[1] == 16:
                    streams[s].finish(k)

    def settle(tick):
        for stream in streams[5:]:
            stream.finish(tick)
        if tick < 5:
            for stream in streams[5:]:
                stream.start(tick + 1)
        if tick < 3:
            sums.start(tick + 1, sums.finish(tick))
        if tick == 3:
            total = sums.finish(tick)
            for n, r in enumerate((0, 1, 2, 3, 4, 5)):
                vec_out[n] = total[r : r + 1]
            for t in range(parts):

                @pl.when(place.part == t)
                def _():
                    dqv_out[...] = total[6:8, t * width : (t + 1) * width]
                    wide = FF // parts
                    dub_out[...] = total[
                        8 + t * wide // D : 9 + t * wide // D, t * wide % D : t * wide % D + wide
                    ]

    @pl.when(step == rows + 1)
    def _():
        settle(0)

    @pl.when(step >= rows)
    def _():
        grads = grad_s[step - rows]
        total = None
        for i in range(3):
            term = dot_nt(grads[:, i * D : (i + 1) * D], w_ref[i])
            total = term if total is None else total + term
        tg_ref[...] = first_ref[...] + passing(total, tok_ref[...], step_tokens)

    @pl.when(step == 2 * rows - 1)
    def _():
        settle(1)
        halves = [
            jnp.concatenate([streams[n + h].out[...].reshape(D // 2, FF // parts) for h in (0, 2)], axis=0)
            for n in range(2)
        ]
        dup_out[...] = passing(halves[0], up_sh[...], step_ref[5:6, 0:1])
        ddown_out[...] = passing(
            jnp.transpose(halves[1].astype(F32)), down_sh[...], step_ref[6:7, 0:1]
        )
        settle(2)
        settle(3)
        settle(4)
        dproj = streams[4].out[...].reshape(-1, D)[:width]
        dproj_out[...] = passing(dproj, proj_sh[...], step_ref[4:5, 0:1])
        settle(5)
        whole = jnp.concatenate(
            [streams[5 + h].out[...].reshape(-1, D) for h in range(2)], axis=0
        ).astype(F32)
        for i in range(3):
            dqkv_out[i] = passing(
                jnp.transpose(whole[i * width : (i + 1) * width]),
                qkv_sh[i],
                step_ref[1 + i : 2 + i, 0:1],
            )


def attend_back(
    sizes, steps, tokens, ints, qkv, probs, ctx, gctx, first, qkv_full, dproj, dup, ddown, dub, dvec,
    qkv_w, proj_w, up_w, down_w,
):
    rows = tokens.shape[0] // SEQ
    parts, nz = 2 * sizes["x"], sizes["z"]
    width, wide = D // parts, FF // parts
    part = (parts, 2, 2, nz, split_rows(3 * width, 4 * nz), D)
    pieces = [dup.shape[-2:], ddown.shape[-2:], dup.shape[-2:], ddown.shape[-2:], dproj.shape[-2:]]
    pieces += [part[-2:]] * 2
    early = lambda i: (jnp.minimum(i, rows - 1), 0)
    late = lambda i: (jnp.maximum(i - rows, 0), 0)
    hbm = pl.BlockSpec(memory_space=pl.ANY)

    def whole(*shape):
        return pl.BlockSpec(shape, lambda i: (0,) * len(shape))

    outs = [
        ((3, D, width), F32),
        ((2, width), F32),
        ((width, D), F32),
        ((D, wide), F32),
        ((1, wide), F32),
        ((wide, D), F32),
        ((6, 1, D), F32),
    ]
    return pl.pallas_call(
        lambda *refs: back_kernel(sizes, *refs),
        name="attend_back",
        grid=(2 * rows,),
        in_specs=[
            whole(8, LANES),
            pl.BlockSpec((SEQ, D), late),
            pl.BlockSpec((SEQ, D), early),
            pl.BlockSpec((SEQ, 3 * D), early),
            pl.BlockSpec(
                (1, HEADS, 2, 256, 384), lambda i: (jnp.minimum(i, rows - 1), 0, 0, 0, 0)
            ),
            pl.BlockSpec((SEQ, D), early),
            pl.BlockSpec((SEQ, D), early),
            pl.BlockSpec((SEQ, D), late),
            whole(3, D, D),
            hbm,
            hbm,
            hbm,
            whole(*dub.shape),
            whole(*dvec.shape),
            whole(*qkv_w.shape),
            whole(*proj_w.shape),
            whole(*up_w.shape),
            whole(*down_w.shape),
        ],
        out_specs=[pl.BlockSpec((SEQ, D), late)] + [whole(*shape) for shape, _ in outs],
        scratch_shapes=[
            pltpu.VMEM((rows, SEQ, 3 * D), BF16),
            pltpu.VMEM((3, D, D), F32),
            pltpu.VMEM((2, 8, D), F32),
            pltpu.VMEM(part, BF16),
        ]
        + sum([stream_scratch(sizes, o, *p) for o, p in zip(ORDERS, pieces)], [])
        + small_scratch(sizes, 16, D),
        out_shape=[jax.ShapeDtypeStruct((rows * SEQ, D), F32)]
        + [jax.ShapeDtypeStruct(shape, kind) for shape, kind in outs],
        compiler_params=pltpu.CompilerParams(
            vmem_limit_bytes=VMEM_LIMIT, collective_id=1, has_side_effects=True
        ),
        cost_estimate=pl.CostEstimate(
            flops=rows * 6 * 10**9, bytes_accessed=rows * 8 * 10**6, transcendentals=0
        ),
    )(
        steps, tokens, ints, qkv, probs, ctx, gctx, first, qkv_full, dproj, dup, ddown, dub, dvec,
        qkv_w, proj_w, up_w, down_w,
    )

def local(
    tokens,
    segment_ids,
    row_lengths,
    qkv_weight,
    qv_bias,
    proj_weight,
    proj_bias,
    first_gain,
    first_shift,
    up_weight,
    up_bias,
    down_weight,
    down_bias,
    second_gain,
    second_shift,
    out_grad,
):
    rows = tokens.shape[0] // SEQ
    place = lax.axis_index("tensor")
    sizes = group_sizes(lax.axis_size("tensor"), lax.axis_size("dp"))
    segments = lax.dynamic_slice(segment_ids, (place * rows, 0), (rows, SEQ))
    lengths = lax.dynamic_slice(row_lengths, (place * rows,), (rows,))
    ints, qkv, probs, ctx, qkv_full, steps, biases, proj_full, up_full, down_full = attend(
        sizes,
        lengths,
        tokens,
        segments[:, None, :],
        qkv_weight,
        qv_bias,
        proj_weight,
        up_weight,
        down_weight,
        up_bias[None],
    )
    vecs = (proj_bias, first_gain, first_shift, down_bias, second_gain, second_shift)
    layer_out, grad_first, grad_ctx, dproj, dup, ddown, dub, dvec = feed_forward(
        sizes, steps, biases, tokens, ctx, out_grad, proj_full.reshape(D, D), up_full, down_full, vecs
    )
    tokens_grad, dqkv, dqv, dproj, dup, dub, ddown, vec = attend_back(
        sizes, steps, tokens, ints, qkv, probs, ctx, grad_ctx, grad_first, qkv_full,
        dproj, dup, ddown, dub, dvec, qkv_weight, proj_weight, up_weight, down_weight,
    )
    vec = [vec[n, 0] for n in range(6)]
    return (
        layer_out, tokens_grad, dqkv, dqv, dproj, vec[0], vec[1], vec[2], dup, dub[0], ddown,
        vec[3], vec[4], vec[5],
    )


def solution(mesh):
    in_specs = (
        P(("dp", "tensor"), None),
        P("dp", None),
        P("dp"),
        P(None, None, "tensor"),
        P(None, "tensor"),
        P("tensor", None),
        P(),
        P(),
        P(),
        P(None, "tensor"),
        P("tensor"),
        P("tensor", None),
        P(),
        P(),
        P(),
        P(("dp", "tensor"), None),
    )
    out_specs = (
        P(("dp", "tensor"), None),
        P(("dp", "tensor"), None),
        P(None, None, "tensor"),
        P(None, "tensor"),
        P("tensor", None),
        P(),
        P(),
        P(),
        P(None, "tensor"),
        P("tensor"),
        P("tensor", None),
        P(),
        P(),
        P(),
    )
    return jax.shard_map(local, mesh=mesh, in_specs=in_specs, out_specs=out_specs, check_vma=False)
```

```python
import jax
import jax.numpy as jnp
from jax import lax
from jax.experimental import pallas as pl
from jax.experimental.pallas import tpu as pltpu
from jax.sharding import PartitionSpec as P

D = 512
HEADS = 8
HEAD_DIM = 64
FF = 2048
SEQ = 512
PAIRS = 4
LANES = 128
LEVELS = 127.0
EPS = 1e-12
MASKED = -1e30
LOG2E = 1.4426950408889634
SCORE_SCALE = 0.125 * LOG2E
VMEM_LIMIT = 58 << 20
F32 = jnp.float32
BF16 = jnp.bfloat16
TILES = ((0, 256, 0, 384), (256, 512, 128, 512))


def rounded(scaled):
    magnitude = jnp.floor(jnp.abs(scaled) + 0.5)
    return jnp.where(scaled < 0.0, -magnitude, magnitude)


def dot_nn(a, b):
    return lax.dot_general(a, b, (((1,), (0,)), ((), ())), preferred_element_type=F32)


def dot_nt(a, b):
    return lax.dot_general(a, b, (((1,), (1,)), ((), ())), preferred_element_type=F32)


def dot_tn(a, b):
    return lax.dot_general(a, b, (((0,), (0,)), ((), ())), preferred_element_type=F32)


def head_mask(head, rows):
    lane = lax.broadcasted_iota(jnp.int32, (rows, LANES), 1)
    return (lane < HEAD_DIM) if head == 0 else (lane >= HEAD_DIM)


def both(left, right):
    return jnp.concatenate(
        [left[:, :128], left[:, 128:] + right[:, :256], right[:, 256:]], axis=1
    )


MESH = pl.DeviceIdType.MESH
MESH_AXES = ("tensor", "dp")


def group_sizes(tensor_size, dp_size):
    return {
        "core": 2,
        "x": tensor_size // 2,
        "y": 2,
        "z": dp_size // 2,
        "tensor": tensor_size,
        "dp": dp_size,
    }


class Place:
    def __init__(self, sizes):
        t, d = lax.axis_index("tensor"), lax.axis_index("dp")
        self.sizes = sizes
        self.part = t
        self.at = {"core": t % 2, "x": t // 2, "y": d % 2, "z": d // 2, "tensor": t, "dp": d}

    def size(self, group):
        return self.sizes[group]

    def peer(self, group, k):
        if group in MESH_AXES:
            at = {axis: lax.axis_index(axis) for axis in MESH_AXES}
            at[group] = (at[group] + k) % self.sizes[group]
            return at[group], (at["dp"], at["tensor"])
        at = dict(self.at)
        at[group] = (at[group] + k) % self.sizes[group]
        return at[group], (at["z"] * 2 + at["y"], at["x"] * 2 + at["core"])

    def greet(self):
        barrier = pltpu.get_barrier_semaphore()
        count = 0
        for group in MESH_AXES:
            for k in range(1, self.sizes[group]):
                pl.semaphore_signal(
                    barrier, inc=1, device_id=self.peer(group, k)[1], device_id_type=MESH
                )
                count += 1
        pl.semaphore_wait(barrier, count)


class Sems:
    def __init__(self, send, recv):
        self.send, self.recv = send, recv

    def copy(self, at, source, target, device):
        return pltpu.make_async_remote_copy(
            src_ref=source,
            dst_ref=target,
            send_sem=self.send.at[at],
            recv_sem=self.recv.at[at],
            device_id=device,
            device_id_type=MESH,
        )


def exchange(place, group, source, target, sems, base):
    copies = []
    for k in range(1, place.size(group)):
        index, device = place.peer(group, k)
        copies.append(sems.copy(base + k - 1, source(k, index), target(k, index), device))
    return copies


def add(first, *others):
    total = first.astype(F32)
    for other in others:
        total = total + other.astype(F32)
    return total.astype(BF16)


class Stream:
    phases = 6

    def __init__(self, place, order, grad, held, got_c, got_1, got_2, got_z, out, send, recv, own):
        self.place, self.order, self.grad, self.held, self.out = place, order, grad, held, out
        self.got_c, self.got_1, self.got_2, self.got_z = got_c, got_1, got_2, got_z
        self.sems, self.own = Sems(send, recv), own

    def local(self):
        if self.own is None:
            return []
        return [
            pltpu.make_async_copy(
                self.grad(2 * i + self.place.at["core"]), self.held.at[i], self.own.at[i]
            )
            for i in range(self.place.size("x"))
        ]

    def copies(self, phase):
        place, at, held = self.place, self.place.at, self.held
        nx, nz = place.size("x"), place.size("z")
        base = [0, nx, 2 * nx, 3 * nx, 3 * nx + nz, 3 * nx + 2 * nz][phase]
        sems = self.sems
        if phase == 0:
            other, device = place.peer("core", 1)
            return [
                sems.copy(i, self.grad(2 * i + other), self.got_c.at[i], device) for i in range(nx)
            ]
        if phase == 1 and self.order == "xy":
            return exchange(
                place, "x", lambda k, j: held.at[j], lambda k, j: self.got_1.at[k - 1], sems, base
            )
        if phase == 2 and self.order == "xy":
            return exchange(
                place, "y", lambda k, j: held.at[at["x"], j], lambda k, j: self.got_2.at[0], sems, base
            )
        if phase == 1:
            other, device = place.peer("y", 1)
            return [
                sems.copy(base + i, held.at[i, other], self.got_1.at[i], device) for i in range(nx)
            ]
        if phase == 2:
            return exchange(
                place,
                "x",
                lambda k, j: held.at[j, at["y"]],
                lambda k, j: self.got_2.at[k - 1],
                sems,
                base,
            )
        if phase == 3:
            return exchange(
                place,
                "z",
                lambda k, j: held.at[at["x"], at["y"], j],
                lambda k, j: self.got_z.at[k - 1],
                sems,
                base,
            )
        if phase == 4:
            piece = self.out.at[at["y"], at["z"]]
            return exchange(place, "z", lambda k, j: piece, lambda k, j: piece, sems, base)
        half = self.out.at[at["y"]]
        return exchange(place, "y", lambda k, j: half, lambda k, j: half, sems, base)

    def start(self, phase):
        for copy in self.copies(phase) + (self.local() if phase == 0 else []):
            copy.start()

    def finish(self, phase):
        for copy in self.copies(phase) + (self.local() if phase == 0 else []):
            copy.wait()
        at, held = self.place.at, self.held
        nx, nz = self.place.size("x"), self.place.size("z")
        if phase == 0:
            for i in range(nx):
                for y in range(2):
                    own = held[i, y] if self.own is not None else self.grad(2 * i + at["core"])[y]
                    held[i, y] = add(own, self.got_c[i, y])
        elif phase == 1 and self.order == "xy":
            for y in range(2):
                held[at["x"], y] = add(
                    held[at["x"], y], *[self.got_1[k, y] for k in range(nx - 1)]
                )
        elif phase == 1:
            for i in range(nx):
                held[i, at["y"]] = add(held[i, at["y"]], self.got_1[i])
        elif phase == 2:
            count = 1 if self.order == "xy" else nx - 1
            held[at["x"], at["y"]] = add(
                held[at["x"], at["y"]], *[self.got_2[k] for k in range(count)]
            )
        elif phase == 3:
            self.out[at["y"], at["z"]] = add(
                held[at["x"], at["y"], at["z"]], *[self.got_z[k] for k in range(nz - 1)]
            )


def stream_scratch(sizes, order, rows, lanes):
    nx, nz = sizes["x"], sizes["z"]
    count = 3 * nx + 2 * nz + 1
    piece = (nz, rows, lanes)
    first = (nx - 1, 2) if order == "xy" else (nx,)
    second = (1,) if order == "xy" else (nx - 1,)
    return [
        pltpu.VMEM((nx, 2) + piece, BF16),
        pltpu.VMEM((nx, 2) + piece, BF16),
        pltpu.VMEM(first + piece, BF16),
        pltpu.VMEM(second + piece, BF16),
        pltpu.VMEM((nz - 1,) + piece[1:], BF16),
        pltpu.VMEM((2,) + piece, BF16),
        pltpu.SemaphoreType.DMA((count,)),
        pltpu.SemaphoreType.DMA((count,)),
        pltpu.SemaphoreType.DMA((nx,)),
    ]


class Small:
    def __init__(self, place, combine, slots, send, recv):
        self.place, self.combine, self.slots, self.sems = place, combine, slots, Sems(send, recv)

    def offsets(self, phase):
        sizes = [self.place.size(g) for g in MESH_AXES]
        return sum(sizes[:phase]), sum(sizes[:phase]) - phase

    def copies(self, phase):
        slot, sem = self.offsets(phase)
        return exchange(
            self.place,
            MESH_AXES[phase],
            lambda k, j: self.slots.at[slot],
            lambda k, j: self.slots.at[slot + k],
            self.sems,
            sem,
        )

    def start(self, phase, values):
        self.slots[self.offsets(phase)[0]] = values
        for copy in self.copies(phase):
            copy.start()

    def finish(self, phase):
        for copy in self.copies(phase):
            copy.wait()
        slot = self.offsets(phase)[0]
        count, me = self.place.size(MESH_AXES[phase]), self.place.at[MESH_AXES[phase]]
        total = None
        for member in range(count):
            term = self.slots[slot + (me + count - member) % count]
            total = term if total is None else self.combine(total, term)
        return total


def small_scratch(sizes, rows, lanes):
    total = sum(sizes[g] for g in MESH_AXES)
    return [
        pltpu.VMEM((total, rows, lanes), F32),
        pltpu.SemaphoreType.DMA((total - 2,)),
        pltpu.SemaphoreType.DMA((total - 2,)),
    ]


class Gather:
    def __init__(self, place, own, every, send, recv, keep):
        self.place, self.own, self.every, self.sems, self.keep = place, own, every, Sems(send, recv), keep

    def far(self):
        place = self.place
        mine = self.every.at[place.part]
        return exchange(place, "x", lambda k, j: self.own, lambda k, j: mine, self.sems, 0)

    def near(self, step):
        place = self.place
        nx = place.size("x")
        device = place.peer("core", 1)[1]
        if step == 0:
            return self.sems.copy(nx - 1, self.own, self.every.at[place.part], device)
        chip = (place.at["x"] + nx - step) % nx
        block = self.every.at[chip * 2 + place.at["core"]]
        return self.sems.copy(nx - 1 + step, block, block, device)

    def mine(self):
        return pltpu.make_async_copy(self.own, self.every.at[self.place.part], self.keep.at[0])

    def start(self):
        for copy in self.far():
            copy.start()
        self.near(0).start()
        self.mine().start()

    def forward(self):
        for copy in self.far():
            copy.wait()
        for k in range(1, self.place.size("x")):
            self.near(k).start()

    def finish(self):
        for k in range(self.place.size("x")):
            self.near(k).wait()
        self.mine().wait()


def gather_scratch(sizes):
    count = 2 * sizes["x"] - 1
    return [
        pltpu.SemaphoreType.DMA((count,)),
        pltpu.SemaphoreType.DMA((count,)),
        pltpu.SemaphoreType.DMA((1,)),
    ]


def split_rows(rows, pieces):
    return -(-rows // (pieces * 8)) * 8


def spread(values, shape):
    count = 1
    for size in shape[:-1]:
        count *= size
    if count > values.shape[0]:
        zeros = jnp.zeros((count - values.shape[0], values.shape[1]), values.dtype)
        values = jnp.concatenate([values, zeros], axis=0)
    return values.reshape(shape)


def tile_rows(rows, height, lanes):
    filled = [r if r.shape[1] == lanes else jnp.concatenate([r, jnp.zeros((1, lanes - r.shape[1]), F32)], axis=1) for r in rows]
    at = lax.broadcasted_iota(jnp.int32, (height, lanes), 0)
    total = jnp.zeros((height, lanes), F32)
    for n, r in enumerate(filled):
        total = jnp.where(at == n, r, total)
    return total


def top(values):
    peak = jnp.max(jnp.abs(values.astype(F32)), axis=0, keepdims=True)
    return jnp.max(peak, axis=1, keepdims=True)


def attend_kernel(
    sizes,
    len_ref,
    tok_ref,
    seg_ref,
    qkv_sh,
    qvb_sh,
    proj_sh,
    up_sh,
    down_sh,
    ub_sh,
    ints_ref,
    qkv_ref,
    probs_ref,
    ctx_ref,
    w_ref,
    step_ref,
    bias_ref,
    proj_all,
    up_all,
    down_all,
    mask_s,
    raw_all,
    bias_all,
    bias_own,
    proj_own,
    up_own,
    down_own,
    *sems,
):
    row = pl.program_id(0)
    last = pl.num_programs(0) - 1
    place = Place(sizes)
    parts = 2 * sizes["x"]
    width = D // parts
    early = [
        Gather(place, own, every, *sems[3 * n : 3 * n + 3])
        for n, (own, every) in enumerate(((qkv_sh, raw_all), (bias_own, bias_all)))
    ]
    late = [
        Gather(place, own, every, *sems[6 + 3 * n : 9 + 3 * n])
        for n, (own, every) in enumerate(
            ((up_own, up_all), (down_own, down_all), (proj_own, proj_all))
        )
    ]
    peaks = Small(place, jnp.maximum, *sems[15:18])

    @pl.when(row == 0)
    def _():
        place.greet()
        bias_own[...] = tile_rows(
            [ub_sh[...].astype(F32)[None], qvb_sh[0:1].astype(F32), qvb_sh[1:2].astype(F32)],
            8,
            ub_sh.shape[0],
        )
        for gather in early:
            gather.start()
        tops = [top(tok_ref[...])] + [top(qkv_sh[i]) for i in range(3)]
        tops += [top(proj_sh[...]), top(up_sh[...]), top(down_sh[...])]
        total = tile_rows([jnp.broadcast_to(t, (1, LANES)) for t in tops], 8, LANES)
        for phase in range(2):
            peaks.start(phase, total)
            total = peaks.finish(phase)
        step_ref[...] = total / LEVELS
        up_own[...] = rounded(up_sh[...].astype(F32) / step_ref[5:6, 0:1]).astype(BF16)
        down_own[...] = rounded(down_sh[...].astype(F32) / step_ref[6:7, 0:1]).astype(BF16)
        proj_own[...] = rounded(proj_sh[...].astype(F32) / step_ref[4:5, 0:1]).astype(BF16)
        for gather in early:
            gather.forward()
        for gather in late:
            gather.start()
        for gather in early:
            gather.finish()
        bias_ref[...] = bias_all[...]
        for t in range(parts):
            for i in range(3):
                w_ref[i, :, t * width : (t + 1) * width] = rounded(
                    raw_all[t, i].astype(F32) / step_ref[1 + i : 2 + i, 0:1]
                ).astype(BF16)

    @pl.when(row == last)
    def _():
        for gather in late:
            gather.forward()

    step_tokens = step_ref[0:1, 0:1]
    tok = tok_ref[pl.ds(pl.multiple_of(row * SEQ, SEQ), SEQ), :]
    ints = rounded(tok.astype(F32) / step_tokens).astype(BF16)
    ints_ref[...] = ints
    biases = [
        jnp.concatenate([bias_all[t, r : r + 1, :width] for t in range(parts)], axis=1)
        for r in (1, 2)
    ]
    for i in range(3):
        raw = dot_nn(ints, w_ref[i]) * (step_tokens * step_ref[1 + i : 2 + i, 0:1])
        if i == 0:
            raw = (raw + biases[0]) * SCORE_SCALE
        if i == 2:
            raw = raw + biases[1]
        qkv_ref[:, i * D : (i + 1) * D] = raw.astype(BF16)
    here = place.part * pl.num_programs(0) + row
    seg_q = seg_ref[pl.ds(here, 1), :].astype(F32)
    length = len_ref[here]
    spot = lax.broadcasted_iota(jnp.int32, (8, SEQ), 1)
    seg_k = jnp.where(spot < length, jnp.broadcast_to(seg_q, (8, SEQ)), -1.0)
    seg_k = jnp.transpose(seg_k)[:, 0:1]
    for n, (k0, k1, q0, q1) in enumerate(TILES):
        keys = lax.broadcasted_iota(jnp.int32, (k1 - k0, q1 - q0), 0) + k0
        queries = lax.broadcasted_iota(jnp.int32, (k1 - k0, q1 - q0), 1) + q0
        allowed = (seg_k[k0:k1] == seg_q[:, q0:q1]) | (keys == queries)
        mask_s[n] = jnp.where(allowed, 0.0, MASKED)

    def pair_step(p, carry):
        at = pl.multiple_of(p * LANES, LANES)
        q_pair = qkv_ref[:, pl.ds(at, LANES)]
        k_pair = qkv_ref[:, pl.ds(D + at, LANES)]
        v_pair = qkv_ref[:, pl.ds(2 * D + at, LANES)]
        v_t = jnp.transpose(v_pair)
        parts = []
        for h in range(2):
            q_head = jnp.where(head_mask(h, SEQ), q_pair, jnp.zeros_like(q_pair))
            scores = [
                dot_nt(k_pair[k0:k1], q_head[q0:q1]) + mask_s[n]
                for n, (k0, k1, q0, q1) in enumerate(TILES)
            ]
            peak = [jnp.max(s, axis=0, keepdims=True) for s in scores]
            high = jnp.concatenate(
                [
                    peak[0][:, :128],
                    jnp.maximum(peak[0][:, 128:], peak[1][:, :256]),
                    peak[1][:, 256:],
                ],
                axis=1,
            )
            weights = [
                jnp.exp2(s - high[:, q0:q1]) for s, (k0, k1, q0, q1) in zip(scores, TILES)
            ]
            totals = both(*[jnp.sum(w, axis=0, keepdims=True) for w in weights])
            inverse = 1.0 / totals
            outs = []
            for n, (k0, k1, q0, q1) in enumerate(TILES):
                probs = (weights[n] * inverse[:, q0:q1]).astype(BF16)
                probs_ref[0, 2 * p + h, n] = probs
                outs.append(dot_nn(v_t[h * 64 : h * 64 + 64, k0:k1], probs))
            parts.append(both(*outs))
        context_t = jnp.concatenate(parts, axis=0)
        ctx_ref[:, pl.ds(at, LANES)] = jnp.transpose(context_t).astype(BF16)
        return carry

    lax.fori_loop(0, PAIRS, pair_step, 0)

    @pl.when(row == last)
    def _():
        for gather in late:
            gather.finish()


def attend(sizes, lens, tokens, segments, qkv_w, qv_bias, proj_w, up_w, down_w, up_b):
    rows = tokens.shape[0] // SEQ
    parts = 2 * sizes["x"]
    hbm = pl.BlockSpec(memory_space=pl.ANY)
    gathered = [(w.shape, BF16) for w in (proj_w, up_w, down_w)]

    def whole(*shape):
        return pl.BlockSpec(shape, lambda i, *_: (0,) * len(shape))

    return pl.pallas_call(
        lambda *refs: attend_kernel(sizes, *refs),
        name="attend",
        grid_spec=pltpu.PrefetchScalarGridSpec(
            num_scalar_prefetch=0,
            grid=(rows,),
            in_specs=[
                pl.BlockSpec(memory_space=pltpu.SMEM),
                whole(*tokens.shape),
                whole(*segments.shape),
                whole(*qkv_w.shape),
                whole(*qv_bias.shape),
                whole(*proj_w.shape),
                whole(*up_w.shape),
                whole(*down_w.shape),
                whole(*up_b.shape),
            ],
            out_specs=[
                pl.BlockSpec((SEQ, D), lambda i, *_: (i, 0)),
                pl.BlockSpec((SEQ, 3 * D), lambda i, *_: (i, 0)),
                pl.BlockSpec((1, HEADS, 2, 256, 384), lambda i, *_: (i, 0, 0, 0, 0)),
                pl.BlockSpec((SEQ, D), lambda i, *_: (i, 0)),
                whole(3, D, D),
                whole(8, LANES),
                whole(parts, 8, up_b.shape[0]),
                hbm,
                hbm,
                hbm,
            ],
            scratch_shapes=[
                pltpu.VMEM((2, 256, 384), F32),
                pltpu.VMEM((parts,) + qkv_w.shape, BF16),
                pltpu.VMEM((parts, 8, up_b.shape[0]), F32),
                pltpu.VMEM((8, up_b.shape[0]), F32),
            ]
            + [pltpu.VMEM(w.shape, BF16) for w in (proj_w, up_w, down_w)]
            + sum([gather_scratch(sizes) for _ in range(5)], [])
            + small_scratch(sizes, 8, LANES),
        ),
        out_shape=[
            jax.ShapeDtypeStruct((rows * SEQ, D), BF16),
            jax.ShapeDtypeStruct((rows * SEQ, 3 * D), BF16),
            jax.ShapeDtypeStruct((rows, HEADS, 2, 256, 384), BF16),
            jax.ShapeDtypeStruct((rows * SEQ, D), BF16),
            jax.ShapeDtypeStruct((3, D, D), BF16),
            jax.ShapeDtypeStruct((8, LANES), F32),
            jax.ShapeDtypeStruct((parts, 8, up_b.shape[0]), F32),
        ]
        + [jax.ShapeDtypeStruct((parts,) + w.shape, BF16) for w in (proj_w, up_w, down_w)],
        compiler_params=pltpu.CompilerParams(
            vmem_limit_bytes=VMEM_LIMIT, collective_id=0, has_side_effects=True
        ),
        cost_estimate=pl.CostEstimate(
            flops=rows * 3 * 10**9, bytes_accessed=rows * 6 * 10**6, transcendentals=rows * 2 * 10**6
        ),
    )(lens, tokens, segments, qkv_w, qv_bias, proj_w, up_w, down_w, up_b)

INV_SQRT_2PI = 0.3989422804014327


def gelu_pair(pre):
    cdf = 0.5 + 0.5 * lax.erf(pre * 0.7071067811865476)
    bell = jnp.exp2(pre * pre * (-0.5 * LOG2E))
    return pre * cdf, cdf + (pre * INV_SQRT_2PI) * bell


def fold_rows(values):
    total = values[0:8]
    for r in range(8, values.shape[0], 8):
        total = total + values[r : r + 8]
    return total


def normalize(values):
    centred = values - jnp.mean(values, axis=-1, keepdims=True)
    inverse = lax.rsqrt(jnp.mean(centred * centred, axis=-1, keepdims=True) + EPS)
    return centred * inverse, inverse


def norm_back(scaled, standard, inverse):
    return inverse * (
        scaled
        - jnp.mean(scaled, axis=-1, keepdims=True)
        - standard * jnp.mean(scaled * standard, axis=-1, keepdims=True)
    )


TB = 512


def ffn_kernel(
    step_ref,
    bias_ref,
    tok_ref,
    ctx_ref,
    og_ref,
    proj_ref,
    up_ref,
    down_ref,
    pb_ref,
    fg_ref,
    fs_ref,
    db_ref,
    sg_ref,
    ss_ref,
    out_ref,
    first_ref,
    gctx_ref,
    dproj_ref,
    dup_ref,
    ddown_ref,
    dub_ref,
    dvec_ref,
    act_s,
    slope_s,
    dproj_s,
    dup_s,
    ddown_s,
    dub_s,
    dvec_s,
):
    at = pl.program_id(0)
    last = pl.num_programs(0) - 1
    parts = up_ref.shape[0]
    step_proj, step_up, step_down = [step_ref[r : r + 1, 0:1] for r in (4, 5, 6)]

    @pl.when(at == 0)
    def _():
        dproj_s[...] = jnp.zeros_like(dproj_s)
        dup_s[...] = jnp.zeros_like(dup_s)
        ddown_s[...] = jnp.zeros_like(ddown_s)
        dub_s[...] = jnp.zeros_like(dub_s)
        dvec_s[...] = jnp.zeros_like(dvec_s)

    proj_bias, first_gain, first_shift, down_bias, second_gain, second_shift = [
        r[...].astype(F32)[None] for r in (pb_ref, fg_ref, fs_ref, db_ref, sg_ref, ss_ref)
    ]
    ctx = ctx_ref[...]
    first_in = tok_ref[...].astype(F32) + (dot_nn(ctx, proj_ref[...]) * step_proj + proj_bias)
    n1, r1 = normalize(first_in)
    normed = n1 * first_gain + first_shift
    low = normed.astype(BF16)
    branch = None
    pre = dot_nn(low, up_ref[0])
    for t in range(parts):
        follow = dot_nn(low, up_ref[t + 1]) if t + 1 < parts else None
        act, slope = gelu_pair(pre * step_up + bias_ref[t, 0:1])
        pre = follow
        act = act.astype(BF16)
        act_s[t] = act
        slope_s[t] = slope
        term = dot_nn(act, down_ref[t])
        branch = term if branch is None else branch + term
    second_in = normed + (branch * step_down + down_bias)
    n2, r2 = normalize(second_in)
    out_ref[...] = (n2 * second_gain + second_shift).astype(BF16)
    og = og_ref[...].astype(F32)
    grad_second = norm_back(og * second_gain, n2, r2)
    dvec_s[4] += fold_rows(og * n2)
    dvec_s[5] += fold_rows(og)
    dvec_s[3] += fold_rows(grad_second)
    grad_down = (grad_second * step_down).astype(BF16)
    back = grad_second
    grad_act = dot_nt(grad_down, down_ref[0])
    for t in range(parts):
        follow = dot_nt(grad_down, down_ref[t + 1]) if t + 1 < parts else None
        grad_pre = grad_act * slope_s[t]
        grad_act = follow
        dub_s[t] += fold_rows(grad_pre)
        grad_up = (grad_pre * step_up).astype(BF16)
        back = back + dot_nt(grad_up, up_ref[t])
        dup_s[t] += dot_tn(low, grad_up)
        ddown_s[t] += dot_tn(grad_down, act_s[t])
    dvec_s[1] += fold_rows(back * n1)
    dvec_s[2] += fold_rows(back)
    grad_first = norm_back(back * first_gain, n1, r1)
    dvec_s[0] += fold_rows(grad_first)
    first_ref[...] = grad_first
    grad_proj = (grad_first * step_proj).astype(BF16)
    dproj_s[...] += dot_tn(ctx, grad_proj)
    gctx_ref[...] = dot_nt(grad_proj, proj_ref[...]).astype(BF16)

    @pl.when(at == last)
    def _():
        width = D // parts
        for t in range(parts):
            rows = dproj_s[t * width : (t + 1) * width]
            dproj_ref[t] = spread(rows.astype(BF16), dproj_ref.shape[1:])
            dup_ref[t] = spread(dup_s[t].astype(BF16), dup_ref.shape[1:])
            ddown_ref[t] = spread(ddown_s[t].astype(BF16), ddown_ref.shape[1:])
            dub_ref[t] = jnp.sum(dub_s[t], axis=0, keepdims=True)
        dvec_ref[...] = jnp.sum(dvec_s[...], axis=1)


def feed_forward(sizes, steps, biases, tokens, ctx, out_grad, proj, up, down, vecs):
    count = tokens.shape[0]
    parts, nz = 2 * sizes["x"], sizes["z"]
    wide = FF // parts
    split = (parts, 2, 2, nz, split_rows(D, 4 * nz), wide)
    split_proj = (parts, 2, nz, split_rows(D // parts, 2 * nz), D)
    block = pl.BlockSpec((TB, D), lambda i, *_: (i, 0))

    def whole(*shape):
        return pl.BlockSpec(shape, lambda i, *_: (0,) * len(shape))

    return pl.pallas_call(
        ffn_kernel,
        name="feed_forward",
        grid=(count // TB,),
        in_specs=[
            whole(8, LANES),
            whole(parts, 8, wide),
            block,
            block,
            block,
            whole(D, D),
            whole(parts, D, wide),
            whole(parts, wide, D),
        ]
        + [whole(D)] * 6,
        out_specs=[
            block,
            block,
            block,
            whole(*split_proj),
            whole(*split),
            whole(*split),
            whole(parts, 1, wide),
            whole(6, D),
        ],
        scratch_shapes=[
            pltpu.VMEM((parts, TB, wide), BF16),
            pltpu.VMEM((parts, TB, wide), F32),
            pltpu.VMEM((D, D), F32),
            pltpu.VMEM((parts, D, wide), F32),
            pltpu.VMEM((parts, D, wide), F32),
            pltpu.VMEM((parts, 8, wide), F32),
            pltpu.VMEM((6, 8, D), F32),
        ],
        out_shape=[
            jax.ShapeDtypeStruct((count, D), BF16),
            jax.ShapeDtypeStruct((count, D), F32),
            jax.ShapeDtypeStruct((count, D), BF16),
            jax.ShapeDtypeStruct(split_proj, BF16),
            jax.ShapeDtypeStruct(split, BF16),
            jax.ShapeDtypeStruct(split, BF16),
            jax.ShapeDtypeStruct((parts, 1, wide), F32),
            jax.ShapeDtypeStruct((6, D), F32),
        ],
        compiler_params=pltpu.CompilerParams(vmem_limit_bytes=VMEM_LIMIT),
        cost_estimate=pl.CostEstimate(
            flops=count * 14 * 10**6, bytes_accessed=count * 12000, transcendentals=count * 4096
        ),
    )(steps, biases, tokens, ctx, out_grad, proj, up, down, *vecs)


PLANS = (
    ((0, 2), (2, 6), (6, 9), (9, 11), (11, 13), (13, 16)),
    ((0, 2), (4, 8), (8, 11), (12, 14), (14, 16), (16, 20)),
    ((0, 2), (7, 11), (11, 14), (15, 18), (18, 21), (21, 27)),
    ((0, 3), (9, 13), (14, 17), (17, 20), (20, 24), (24, 31)),
    ((0, 3), (12, 15), (15, 18), (18, 22), (22, 26), (28, 35)),
    ((16, 19), (19, 23), (23, 29), (29, 32), (32, 36), (36, 39)),
    ((16, 19), (19, 23), (23, 28), (28, 30), (30, 34), (34, 38)),
    ((16, 19), (19, 25), (25, 33), (33, 37), (37, 40), (40, 41)),
)
ORDERS = ('xy', 'xy', 'xy', 'xy', 'xy', 'xy', 'yx', 'xy')
THIRDS = 3


def passing(grads, weights, step):
    return jnp.where(weights.astype(F32) == 0.0, 0.0, grads.astype(F32)) / step


def back_kernel(
    sizes,
    step_ref,
    tok_ref,
    ints_ref,
    qkv_ref,
    probs_ref,
    ctx_ref,
    gctx_ref,
    first_ref,
    w_ref,
    dproj_hbm,
    dup_hbm,
    ddown_hbm,
    dub_ref,
    dvec_ref,
    qkv_sh,
    proj_sh,
    up_sh,
    down_sh,
    tg_ref,
    dqkv_out,
    dqv_out,
    dproj_out,
    dup_out,
    dub_out,
    ddown_out,
    vec_out,
    grad_s,
    dqkv_s,
    dqv_s,
    part_s,
    *scratch,
):
    step = pl.program_id(0)
    rows = grad_s.shape[0]
    place = Place(sizes)
    parts = 2 * sizes["x"]
    width = D // parts
    step_tokens = step_ref[0:1, 0:1]
    sources = [
        lambda t: dup_hbm.at[t, 0],
        lambda t: ddown_hbm.at[t, 0],
        lambda t: dup_hbm.at[t, 1],
        lambda t: ddown_hbm.at[t, 1],
        lambda t: dproj_hbm.at[t],
    ]
    sources += [lambda t, q=q: part_s.at[t, q] for q in range(THIRDS)]
    streams = []
    for n, source in enumerate(sources):
        refs = scratch[9 * n : 9 * n + 9]
        own = refs[8] if n < 5 else None
        streams.append(Stream(place, ORDERS[n], source, *refs[:8], own))
    sums = Small(place, jnp.add, *scratch[9 * len(sources) :])

    @pl.when(step == 0)
    def _():
        dqkv_s[...] = jnp.zeros_like(dqkv_s)
        dqv_s[...] = jnp.zeros_like(dqv_s)
        place.greet()

    def events(now):
        for s, plan in enumerate(PLANS):
            for k, p in enumerate(plan):
                if p[1] == now:
                    streams[s].finish(k)
        for s, plan in enumerate(PLANS):
            for k, p in enumerate(plan):
                if p[0] == now:
                    streams[s].start(k)

    def advance(tick, ticks):
        for now in ticks:
            if any(now in p for plan in PLANS for p in plan):
                pl.when(tick == now)(lambda: events(now))

    def pair_step(p, carry):
        for n in range(16 // (PAIRS * rows)):
            advance((step * PAIRS + p) * (16 // (PAIRS * rows)) + n, range(16))
        at = pl.multiple_of(p * LANES, LANES)
        q_pair = qkv_ref[:, pl.ds(at, LANES)]
        k_pair = qkv_ref[:, pl.ds(D + at, LANES)]
        v_pair = qkv_ref[:, pl.ds(2 * D + at, LANES)]
        g_pair = gctx_ref[:, pl.ds(at, LANES)]
        c_pair = ctx_ref[:, pl.ds(at, LANES)]
        k_t = jnp.transpose(k_pair)
        product = (g_pair.astype(F32) * c_pair.astype(F32)).astype(BF16)
        d_keys = [None, None]
        d_values = [None, None]
        parts = []
        for h in range(2):
            mask = head_mask(h, SEQ)
            q_head = jnp.where(mask, q_pair, jnp.zeros_like(q_pair))
            g_head = jnp.where(mask, g_pair, jnp.zeros_like(g_pair))
            ones = jnp.where(head_mask(h, 8), 1.0, 0.0).astype(BF16)
            centre = dot_nt(ones, product)[0:1]
            outs = []
            for n, (k0, k1, q0, q1) in enumerate(TILES):
                probs = probs_ref[0, 2 * p + h, n]
                gp = dot_nt(v_pair[k0:k1], g_head[q0:q1])
                gs = (probs.astype(F32) * (gp - centre[:, q0:q1])).astype(BF16)
                dv = dot_nn(probs, g_head[q0:q1])
                dk = dot_nn(gs, q_head[q0:q1])
                d_values[n] = dv if h == 0 else d_values[n] + dv
                d_keys[n] = dk if h == 0 else d_keys[n] + dk
                outs.append(dot_nn(k_t[h * 64 : h * 64 + 64, k0:k1], gs))
            parts.append(both(*outs))
        d_q = jnp.transpose(jnp.concatenate(parts, axis=0)) * 0.125
        dqv_s[0, :, pl.ds(at, LANES)] += fold_rows(d_q)
        grad_s[step, :, pl.ds(at, LANES)] = (d_q * (step_tokens * step_ref[1:2, 0:1])).astype(BF16)
        for n, (k0, k1, q0, q1) in enumerate(TILES):
            grad_s[step, k0:k1, pl.ds(D + at, LANES)] = (
                d_keys[n] * (step_tokens * step_ref[2:3, 0:1] * (1.0 / LOG2E))
            ).astype(BF16)
            dqv_s[1, :, pl.ds(at, LANES)] += fold_rows(d_values[n])
            grad_s[step, k0:k1, pl.ds(2 * D + at, LANES)] = (
                d_values[n] * (step_tokens * step_ref[3:4, 0:1])
            ).astype(BF16)
        return carry

    @pl.when(step < rows)
    def _():
        lax.fori_loop(0, PAIRS, pair_step, 0)
        for i in range(3):
            dqkv_s[i] += dot_tn(grad_s[step, :, i * D : (i + 1) * D], ints_ref[...])

    @pl.when(step == rows)
    def _():
        for t in range(parts):
            piece = jnp.concatenate(
                [dqkv_s[i, t * width : (t + 1) * width] for i in range(3)], axis=0
            )
            part_s[t] = spread(piece.astype(BF16), part_s.shape[1:])
        dqv = jnp.sum(dqv_s[...], axis=1)
        vec = [dvec_ref[r : r + 1] for r in range(6)] + [dqv[0:1], dqv[1:2]]
        dub = jnp.concatenate([dub_ref[t] for t in range(parts)], axis=1)
        vec += [dub[:, r * D : (r + 1) * D] for r in range(4)]
        sums.start(0, tile_rows(vec, 16, D))

    @pl.when(step >= rows)
    def _():
        for n in range(4 // rows):
            advance(16 + (step - rows) * (4 // rows) + n, range(16, 20))

    def vectors():
        total = sums.finish(1)
        for n in range(6):
            vec_out[n] = total[n : n + 1]
        for t in range(parts):

            @pl.when(place.part == t)
            def _():
                dqv_out[...] = total[6:8, t * width : (t + 1) * width]
                wide = FF // parts
                dub_out[...] = total[
                    8 + t * wide // D : 9 + t * wide // D, t * wide % D : t * wide % D + wide
                ]

    @pl.when(step == rows + 1)
    def _():
        sums.start(1, sums.finish(0))

    @pl.when(step >= rows)
    def _():
        grads = grad_s[step - rows]
        total = None
        for i in range(3):
            term = dot_nt(grads[:, i * D : (i + 1) * D], w_ref[i])
            total = term if total is None else total + term
        tg_ref[...] = (first_ref[...] + passing(total, tok_ref[...], step_tokens)).astype(BF16)

    def joined(*group):
        halves = [streams[n].out[...].reshape(D // 2, FF // parts) for n in group]
        return jnp.concatenate(halves, axis=0)

    @pl.when(step == 2 * rows - 1)
    def _():
        ticks = sorted({n for plan in PLANS for p in plan for n in p if n >= 20})
        ended = [max(PLANS[s][5][1] for s in group) for group in ((0, 2), (1, 3), (4,))]
        for now in [19] + ticks:
            if now > 19:
                events(now)
            if now == ticks[len(ticks) // 3]:
                vectors()
            if now == max(19, ended[0]):
                dup_out[...] = passing(joined(0, 2), up_sh[...], step_ref[5:6, 0:1])
            if now == max(19, ended[1]):
                ddown_out[...] = passing(
                    jnp.transpose(joined(1, 3).astype(F32)), down_sh[...], step_ref[6:7, 0:1]
                )
            if now == max(19, ended[2]):
                dproj = streams[4].out[...].reshape(-1, D)[:width]
                dproj_out[...] = passing(dproj, proj_sh[...], step_ref[4:5, 0:1])
        whole = jnp.concatenate(
            [streams[5 + q].out[...].reshape(-1, D) for q in range(THIRDS)], axis=0
        ).astype(F32)
        for i in range(3):
            dqkv_out[i] = passing(
                jnp.transpose(whole[i * width : (i + 1) * width]),
                qkv_sh[i],
                step_ref[1 + i : 2 + i, 0:1],
            )


def attend_back(
    sizes, steps, tokens, ints, qkv, probs, ctx, gctx, first, qkv_full, dproj, dup, ddown, dub, dvec,
    qkv_w, proj_w, up_w, down_w,
):
    rows = tokens.shape[0] // SEQ
    parts, nz = 2 * sizes["x"], sizes["z"]
    width, wide = D // parts, FF // parts
    part = (parts, THIRDS, 2, nz, split_rows(3 * width, 2 * THIRDS * nz), D)
    pieces = [dup.shape[-2:], ddown.shape[-2:], dup.shape[-2:], ddown.shape[-2:], dproj.shape[-2:]]
    pieces += [part[-2:]] * THIRDS
    early = lambda i: (jnp.minimum(i, rows - 1), 0)
    late = lambda i: (jnp.maximum(i - rows, 0), 0)
    hbm = pl.BlockSpec(memory_space=pl.ANY)

    def whole(*shape):
        return pl.BlockSpec(shape, lambda i: (0,) * len(shape))

    outs = [
        ((3, D, width), F32),
        ((2, width), F32),
        ((width, D), F32),
        ((D, wide), F32),
        ((1, wide), F32),
        ((wide, D), F32),
        ((6, 1, D), F32),
    ]
    return pl.pallas_call(
        lambda *refs: back_kernel(sizes, *refs),
        name="attend_back",
        grid=(2 * rows,),
        in_specs=[
            whole(8, LANES),
            pl.BlockSpec((SEQ, D), late),
            pl.BlockSpec((SEQ, D), early),
            pl.BlockSpec((SEQ, 3 * D), early),
            pl.BlockSpec(
                (1, HEADS, 2, 256, 384), lambda i: (jnp.minimum(i, rows - 1), 0, 0, 0, 0)
            ),
            pl.BlockSpec((SEQ, D), early),
            pl.BlockSpec((SEQ, D), early),
            pl.BlockSpec((SEQ, D), late),
            whole(3, D, D),
            hbm,
            hbm,
            hbm,
            whole(*dub.shape),
            whole(*dvec.shape),
            whole(*qkv_w.shape),
            whole(*proj_w.shape),
            whole(*up_w.shape),
            whole(*down_w.shape),
        ],
        out_specs=[pl.BlockSpec((SEQ, D), late)] + [whole(*shape) for shape, _ in outs],
        scratch_shapes=[
            pltpu.VMEM((rows, SEQ, 3 * D), BF16),
            pltpu.VMEM((3, D, D), F32),
            pltpu.VMEM((2, 8, D), F32),
            pltpu.VMEM(part, BF16),
        ]
        + sum([stream_scratch(sizes, o, *p) for o, p in zip(ORDERS, pieces)], [])
        + small_scratch(sizes, 16, D),
        out_shape=[jax.ShapeDtypeStruct((rows * SEQ, D), BF16)]
        + [jax.ShapeDtypeStruct(shape, kind) for shape, kind in outs],
        compiler_params=pltpu.CompilerParams(
            vmem_limit_bytes=VMEM_LIMIT, collective_id=1, has_side_effects=True
        ),
        cost_estimate=pl.CostEstimate(
            flops=rows * 6 * 10**9, bytes_accessed=rows * 8 * 10**6, transcendentals=0
        ),
    )(
        steps, tokens, ints, qkv, probs, ctx, gctx, first, qkv_full, dproj, dup, ddown, dub, dvec,
        qkv_w, proj_w, up_w, down_w,
    )

def local(
    tokens,
    segment_ids,
    row_lengths,
    qkv_weight,
    qv_bias,
    proj_weight,
    proj_bias,
    first_gain,
    first_shift,
    up_weight,
    up_bias,
    down_weight,
    down_bias,
    second_gain,
    second_shift,
    out_grad,
):
    rows = tokens.shape[0] // SEQ
    sizes = group_sizes(lax.axis_size("tensor"), lax.axis_size("dp"))
    ints, qkv, probs, ctx, qkv_full, steps, biases, proj_full, up_full, down_full = attend(
        sizes,
        row_lengths,
        tokens,
        segment_ids,
        qkv_weight,
        qv_bias,
        proj_weight,
        up_weight,
        down_weight,
        up_bias,
    )
    vecs = (proj_bias, first_gain, first_shift, down_bias, second_gain, second_shift)
    layer_out, grad_first, grad_ctx, dproj, dup, ddown, dub, dvec = feed_forward(
        sizes, steps, biases, tokens, ctx, out_grad, proj_full.reshape(D, D), up_full, down_full, vecs
    )
    tokens_grad, dqkv, dqv, dproj, dup, dub, ddown, vec = attend_back(
        sizes, steps, tokens, ints, qkv, probs, ctx, grad_ctx, grad_first, qkv_full,
        dproj, dup, ddown, dub, dvec, qkv_weight, proj_weight, up_weight, down_weight,
    )
    vec = [vec[n, 0] for n in range(6)]
    return (
        layer_out, tokens_grad.astype(F32), dqkv, dqv, dproj, vec[0], vec[1], vec[2], dup, dub[0], ddown,
        vec[3], vec[4], vec[5],
    )


def solution(mesh):
    in_specs = (
        P(("dp", "tensor"), None),
        P("dp", None),
        P("dp"),
        P(None, None, "tensor"),
        P(None, "tensor"),
        P("tensor", None),
        P(),
        P(),
        P(),
        P(None, "tensor"),
        P("tensor"),
        P("tensor", None),
        P(),
        P(),
        P(),
        P(("dp", "tensor"), None),
    )
    out_specs = (
        P(("dp", "tensor"), None),
        P(("dp", "tensor"), None),
        P(None, None, "tensor"),
        P(None, "tensor"),
        P("tensor", None),
        P(),
        P(),
        P(),
        P(None, "tensor"),
        P("tensor"),
        P("tensor", None),
        P(),
        P(),
        P(),
    )
    return jax.shard_map(local, mesh=mesh, in_specs=in_specs, out_specs=out_specs, check_vma=False)
```

```python
import jax
import jax.numpy as jnp
from jax import lax
from jax.experimental import pallas as pl
from jax.experimental.pallas import tpu as pltpu
from jax.sharding import PartitionSpec as P

D = 512
HEADS = 8
HEAD_DIM = 64
FF = 2048
SEQ = 512
PAIRS = 4
LANES = 128
LEVELS = 127.0
EPS = 1e-12
MASKED = -1e30
LOG2E = 1.4426950408889634
SCORE_SCALE = 0.125 * LOG2E
VMEM_LIMIT = 58 << 20
F32 = jnp.float32
BF16 = jnp.bfloat16
TILES = ((0, 256, 0, 384), (256, 512, 128, 512))


def rounded(scaled):
    magnitude = jnp.floor(jnp.abs(scaled) + 0.5)
    return jnp.where(scaled < 0.0, -magnitude, magnitude)


def dot_nn(a, b):
    return lax.dot_general(a, b, (((1,), (0,)), ((), ())), preferred_element_type=F32)


def dot_nt(a, b):
    return lax.dot_general(a, b, (((1,), (1,)), ((), ())), preferred_element_type=F32)


def dot_tn(a, b):
    return lax.dot_general(a, b, (((0,), (0,)), ((), ())), preferred_element_type=F32)


def head_mask(head, rows):
    lane = lax.broadcasted_iota(jnp.int32, (rows, LANES), 1)
    return (lane < HEAD_DIM) if head == 0 else (lane >= HEAD_DIM)


def stacked(pair):
    zeros = jnp.zeros_like(pair)
    return jnp.concatenate(
        [jnp.where(head_mask(h, pair.shape[0]), pair, zeros) for h in range(2)], axis=0
    )


def unstacked(blocks):
    rows = blocks.shape[0] // 2
    return jnp.where(head_mask(0, rows), blocks[:rows], blocks[rows:])


def both(left, right):
    return jnp.concatenate([left[:128], left[128:] + right[:256], right[256:]], axis=0)


MESH = pl.DeviceIdType.MESH
MESH_AXES = ("tensor", "dp")


def group_sizes(tensor_size, dp_size):
    return {
        "core": 2,
        "x": tensor_size // 2,
        "y": 2,
        "z": dp_size // 2,
        "tensor": tensor_size,
        "dp": dp_size,
    }


class Place:
    def __init__(self, sizes):
        t, d = lax.axis_index("tensor"), lax.axis_index("dp")
        self.sizes = sizes
        self.part = t
        self.at = {"core": t % 2, "x": t // 2, "y": d % 2, "z": d // 2, "tensor": t, "dp": d}

    def size(self, group):
        return self.sizes[group]

    def peer(self, group, k):
        if group in MESH_AXES:
            at = {axis: lax.axis_index(axis) for axis in MESH_AXES}
            at[group] = (at[group] + k) % self.sizes[group]
            return at[group], (at["dp"], at["tensor"])
        at = dict(self.at)
        at[group] = (at[group] + k) % self.sizes[group]
        return at[group], (at["z"] * 2 + at["y"], at["x"] * 2 + at["core"])

    def greet(self):
        barrier = pltpu.get_barrier_semaphore()
        count = 0
        for group in MESH_AXES:
            for k in range(1, self.sizes[group]):
                pl.semaphore_signal(
                    barrier, inc=1, device_id=self.peer(group, k)[1], device_id_type=MESH
                )
                count += 1
        pl.semaphore_wait(barrier, count)


class Sems:
    def __init__(self, send, recv):
        self.send, self.recv = send, recv

    def copy(self, at, source, target, device):
        return pltpu.make_async_remote_copy(
            src_ref=source,
            dst_ref=target,
            send_sem=self.send.at[at],
            recv_sem=self.recv.at[at],
            device_id=device,
            device_id_type=MESH,
        )


def exchange(place, group, source, target, sems, base):
    copies = []
    for k in range(1, place.size(group)):
        index, device = place.peer(group, k)
        copies.append(sems.copy(base + k - 1, source(k, index), target(k, index), device))
    return copies


def add(first, *others):
    total = first.astype(F32)
    for other in others:
        total = total + other.astype(F32)
    return total.astype(BF16)


class Stream:
    phases = 6

    def __init__(self, place, order, grad, held, got_c, got_1, got_2, got_z, out, send, recv, own):
        self.place, self.order, self.grad, self.held, self.out = place, order, grad, held, out
        self.got_c, self.got_1, self.got_2, self.got_z = got_c, got_1, got_2, got_z
        self.sems, self.own = Sems(send, recv), own

    def local(self):
        if self.own is None:
            return []
        return [
            pltpu.make_async_copy(
                self.grad(2 * i + self.place.at["core"]), self.held.at[i], self.own.at[i]
            )
            for i in range(self.place.size("x"))
        ]

    def copies(self, phase):
        place, at, held = self.place, self.place.at, self.held
        nx, nz = place.size("x"), place.size("z")
        base = [0, nx, 2 * nx, 3 * nx, 3 * nx + nz, 3 * nx + 2 * nz][phase]
        sems = self.sems
        if phase == 0:
            other, device = place.peer("core", 1)
            return [
                sems.copy(i, self.grad(2 * i + other), self.got_c.at[i], device) for i in range(nx)
            ]
        if phase == 1 and self.order == "xy":
            return exchange(
                place, "x", lambda k, j: held.at[j], lambda k, j: self.got_1.at[k - 1], sems, base
            )
        if phase == 2 and self.order == "xy":
            return exchange(
                place, "y", lambda k, j: held.at[at["x"], j], lambda k, j: self.got_2.at[0], sems, base
            )
        if phase == 1:
            other, device = place.peer("y", 1)
            return [
                sems.copy(base + i, held.at[i, other], self.got_1.at[i], device) for i in range(nx)
            ]
        if phase == 2:
            return exchange(
                place,
                "x",
                lambda k, j: held.at[j, at["y"]],
                lambda k, j: self.got_2.at[k - 1],
                sems,
                base,
            )
        if phase == 3:
            return exchange(
                place,
                "z",
                lambda k, j: held.at[at["x"], at["y"], j],
                lambda k, j: self.got_z.at[k - 1],
                sems,
                base,
            )
        if phase == 4:
            piece = self.out.at[at["y"], at["z"]]
            return exchange(place, "z", lambda k, j: piece, lambda k, j: piece, sems, base)
        half = self.out.at[at["y"]]
        return exchange(place, "y", lambda k, j: half, lambda k, j: half, sems, base)

    def start(self, phase):
        for copy in self.copies(phase) + (self.local() if phase == 0 else []):
            copy.start()

    def finish(self, phase):
        for copy in self.copies(phase) + (self.local() if phase == 0 else []):
            copy.wait()
        at, held = self.place.at, self.held
        nx, nz = self.place.size("x"), self.place.size("z")
        if phase == 0:
            for i in range(nx):
                for y in range(2):
                    own = held[i, y] if self.own is not None else self.grad(2 * i + at["core"])[y]
                    held[i, y] = add(own, self.got_c[i, y])
        elif phase == 1 and self.order == "xy":
            for y in range(2):
                held[at["x"], y] = add(
                    held[at["x"], y], *[self.got_1[k, y] for k in range(nx - 1)]
                )
        elif phase == 1:
            for i in range(nx):
                held[i, at["y"]] = add(held[i, at["y"]], self.got_1[i])
        elif phase == 2:
            count = 1 if self.order == "xy" else nx - 1
            held[at["x"], at["y"]] = add(
                held[at["x"], at["y"]], *[self.got_2[k] for k in range(count)]
            )
        elif phase == 3:
            self.out[at["y"], at["z"]] = add(
                held[at["x"], at["y"], at["z"]], *[self.got_z[k] for k in range(nz - 1)]
            )


def stream_scratch(sizes, order, rows, lanes):
    nx, nz = sizes["x"], sizes["z"]
    count = 3 * nx + 2 * nz + 1
    piece = (nz, rows, lanes)
    first = (nx - 1, 2) if order == "xy" else (nx,)
    second = (1,) if order == "xy" else (nx - 1,)
    return [
        pltpu.VMEM((nx, 2) + piece, BF16),
        pltpu.VMEM((nx, 2) + piece, BF16),
        pltpu.VMEM(first + piece, BF16),
        pltpu.VMEM(second + piece, BF16),
        pltpu.VMEM((nz - 1,) + piece[1:], BF16),
        pltpu.VMEM((2,) + piece, BF16),
        pltpu.SemaphoreType.DMA((count,)),
        pltpu.SemaphoreType.DMA((count,)),
        pltpu.SemaphoreType.DMA((nx,)),
    ]


class Small:
    def __init__(self, place, combine, slots, send, recv):
        self.place, self.combine, self.slots, self.sems = place, combine, slots, Sems(send, recv)

    def offsets(self, phase):
        sizes = [self.place.size(g) for g in MESH_AXES]
        return sum(sizes[:phase]), sum(sizes[:phase]) - phase

    def copies(self, phase):
        slot, sem = self.offsets(phase)
        return exchange(
            self.place,
            MESH_AXES[phase],
            lambda k, j: self.slots.at[slot],
            lambda k, j: self.slots.at[slot + k],
            self.sems,
            sem,
        )

    def start(self, phase, values):
        self.slots[self.offsets(phase)[0]] = values
        for copy in self.copies(phase):
            copy.start()

    def finish(self, phase):
        for copy in self.copies(phase):
            copy.wait()
        slot = self.offsets(phase)[0]
        count, me = self.place.size(MESH_AXES[phase]), self.place.at[MESH_AXES[phase]]
        total = None
        for member in range(count):
            term = self.slots[slot + (me + count - member) % count]
            total = term if total is None else self.combine(total, term)
        return total


def small_scratch(sizes, rows, lanes):
    total = sum(sizes[g] for g in MESH_AXES)
    return [
        pltpu.VMEM((total, rows, lanes), F32),
        pltpu.SemaphoreType.DMA((total - 2,)),
        pltpu.SemaphoreType.DMA((total - 2,)),
    ]


class Gather:
    def __init__(self, place, own, every, send, recv, keep):
        self.place, self.own, self.every, self.sems, self.keep = place, own, every, Sems(send, recv), keep

    def far(self):
        place = self.place
        mine = self.every.at[place.part]
        return exchange(place, "x", lambda k, j: self.own, lambda k, j: mine, self.sems, 0)

    def near(self, step):
        place = self.place
        nx = place.size("x")
        device = place.peer("core", 1)[1]
        if step == 0:
            return self.sems.copy(nx - 1, self.own, self.every.at[place.part], device)
        chip = (place.at["x"] + nx - step) % nx
        block = self.every.at[chip * 2 + place.at["core"]]
        return self.sems.copy(nx - 1 + step, block, block, device)

    def mine(self):
        return pltpu.make_async_copy(self.own, self.every.at[self.place.part], self.keep.at[0])

    def start(self):
        for copy in self.far():
            copy.start()
        self.near(0).start()
        self.mine().start()

    def forward(self):
        for copy in self.far():
            copy.wait()
        for k in range(1, self.place.size("x")):
            self.near(k).start()

    def finish(self):
        for k in range(self.place.size("x")):
            self.near(k).wait()
        self.mine().wait()


def gather_scratch(sizes):
    count = 2 * sizes["x"] - 1
    return [
        pltpu.SemaphoreType.DMA((count,)),
        pltpu.SemaphoreType.DMA((count,)),
        pltpu.SemaphoreType.DMA((1,)),
    ]


def split_rows(rows, pieces):
    return -(-rows // (pieces * 8)) * 8


def spread(values, shape):
    count = 1
    for size in shape[:-1]:
        count *= size
    if count > values.shape[0]:
        zeros = jnp.zeros((count - values.shape[0], values.shape[1]), values.dtype)
        values = jnp.concatenate([values, zeros], axis=0)
    return values.reshape(shape)


def tile_rows(rows, height, lanes):
    filled = [r if r.shape[1] == lanes else jnp.concatenate([r, jnp.zeros((1, lanes - r.shape[1]), F32)], axis=1) for r in rows]
    at = lax.broadcasted_iota(jnp.int32, (height, lanes), 0)
    total = jnp.zeros((height, lanes), F32)
    for n, r in enumerate(filled):
        total = jnp.where(at == n, r, total)
    return total


def top(values):
    peak = jnp.max(jnp.abs(values.astype(F32)), axis=0, keepdims=True)
    return jnp.max(peak, axis=1, keepdims=True)


def attend_kernel(
    sizes,
    len_ref,
    tok_ref,
    seg_ref,
    qkv_sh,
    qvb_sh,
    proj_sh,
    up_sh,
    down_sh,
    ub_sh,
    ints_ref,
    qkv_ref,
    probs_ref,
    ctx_ref,
    w_ref,
    step_ref,
    bias_ref,
    proj_all,
    up_all,
    down_all,
    mask_s,
    raw_all,
    bias_all,
    bias_own,
    proj_own,
    up_own,
    down_own,
    *sems,
):
    row = pl.program_id(0)
    last = pl.num_programs(0) - 1
    place = Place(sizes)
    parts = 2 * sizes["x"]
    width = D // parts
    early = [
        Gather(place, own, every, *sems[3 * n : 3 * n + 3])
        for n, (own, every) in enumerate(((qkv_sh, raw_all), (bias_own, bias_all)))
    ]
    late = [
        Gather(place, own, every, *sems[6 + 3 * n : 9 + 3 * n])
        for n, (own, every) in enumerate(
            ((up_own, up_all), (down_own, down_all), (proj_own, proj_all))
        )
    ]
    peaks = Small(place, jnp.maximum, *sems[15:18])

    @pl.when(row == 0)
    def _():
        bias_own[...] = tile_rows(
            [ub_sh[...].astype(F32)[None], qvb_sh[0:1].astype(F32), qvb_sh[1:2].astype(F32)],
            8,
            ub_sh.shape[0],
        )
        tops = [top(tok_ref[...])] + [top(qkv_sh[i]) for i in range(3)]
        tops += [top(proj_sh[...]), top(up_sh[...]), top(down_sh[...])]
        total = tile_rows([jnp.broadcast_to(t, (1, LANES)) for t in tops], 8, LANES)
        place.greet()
        peaks.start(0, total)
        for gather in early:
            gather.start()
        peaks.start(1, peaks.finish(0))
        step_ref[...] = peaks.finish(1) / LEVELS
        proj_own[...] = rounded(proj_sh[...].astype(F32) / step_ref[4:5, 0:1]).astype(BF16)
        up_own[...] = rounded(up_sh[...].astype(F32) / step_ref[5:6, 0:1]).astype(BF16)
        down_own[...] = rounded(down_sh[...].astype(F32) / step_ref[6:7, 0:1]).astype(BF16)
        for gather in late:
            gather.start()
        for gather in early:
            gather.forward()
        for gather in early:
            gather.finish()
        bias_ref[...] = bias_all[...]
        for t in range(parts):
            for i in range(3):
                w_ref[i, :, t * width : (t + 1) * width] = rounded(
                    raw_all[t, i].astype(F32) / step_ref[1 + i : 2 + i, 0:1]
                ).astype(BF16)

    @pl.when(row == last)
    def _():
        for gather in late:
            gather.forward()

    step_tokens = step_ref[0:1, 0:1]
    tok = tok_ref[pl.ds(pl.multiple_of(row * SEQ, SEQ), SEQ), :]
    ints = rounded(tok.astype(F32) / step_tokens).astype(BF16)
    ints_ref[...] = ints
    biases = [
        jnp.concatenate([bias_all[t, r : r + 1, :width] for t in range(parts)], axis=1)
        for r in (1, 2)
    ]
    for i in range(3):
        raw = dot_nn(ints, w_ref[i]) * (step_tokens * step_ref[1 + i : 2 + i, 0:1])
        if i == 0:
            raw = (raw + biases[0]) * SCORE_SCALE
        if i == 2:
            raw = raw + biases[1]
        qkv_ref[:, i * D : (i + 1) * D] = raw.astype(BF16)
    here = place.part * pl.num_programs(0) + row
    seg_q = seg_ref[pl.ds(here, 1), :].astype(F32)
    length = len_ref[here]
    spot = lax.broadcasted_iota(jnp.int32, (8, SEQ), 1)
    seg_k = jnp.where(spot < length, jnp.broadcast_to(seg_q, (8, SEQ)), -1.0)
    seg_k = jnp.transpose(seg_k)[:, 0:1]
    for n, (k0, k1, q0, q1) in enumerate(TILES):
        keys = lax.broadcasted_iota(jnp.int32, (k1 - k0, q1 - q0), 0) + k0
        queries = lax.broadcasted_iota(jnp.int32, (k1 - k0, q1 - q0), 1) + q0
        allowed = (seg_k[k0:k1] == seg_q[:, q0:q1]) | (keys == queries)
        mask_s[n] = jnp.where(allowed, 0.0, MASKED)

    def pair_step(p, carry):
        at = pl.multiple_of(p * LANES, LANES)
        q_pair = qkv_ref[:, pl.ds(at, LANES)]
        k_pair = qkv_ref[:, pl.ds(D + at, LANES)]
        v_pair = qkv_ref[:, pl.ds(2 * D + at, LANES)]
        scores = []
        for n, (k0, k1, q0, q1) in enumerate(TILES):
            s = dot_nt(stacked(k_pair[k0:k1]), q_pair[q0:q1])
            scores.append(s.reshape(2, 256, 384) + mask_s[n])
        peak = [jnp.max(s, axis=1, keepdims=True) for s in scores]
        high = jnp.concatenate(
            [
                peak[0][:, :, :128],
                jnp.maximum(peak[0][:, :, 128:], peak[1][:, :, :256]),
                peak[1][:, :, 256:],
            ],
            axis=2,
        )
        weights = [jnp.exp2(s - high[:, :, q0:q1]) for s, (k0, k1, q0, q1) in zip(scores, TILES)]
        sums = [jnp.sum(w, axis=1, keepdims=True) for w in weights]
        totals = jnp.concatenate(
            [
                sums[0][:, :, :128],
                sums[0][:, :, 128:] + sums[1][:, :, :256],
                sums[1][:, :, 256:],
            ],
            axis=2,
        )
        inverse = 1.0 / totals
        outs = []
        for n, (k0, k1, q0, q1) in enumerate(TILES):
            probs = (weights[n] * inverse[:, :, q0:q1]).astype(BF16)
            probs_ref[0, pl.ds(2 * p, 2), n] = probs
            outs.append(dot_tn(probs.reshape(512, 384), stacked(v_pair[k0:k1])))
        ctx_ref[:, pl.ds(at, LANES)] = both(*outs).astype(BF16)
        return carry

    lax.fori_loop(0, PAIRS, pair_step, 0)

    @pl.when(row == last)
    def _():
        for gather in late:
            gather.finish()


def attend(sizes, lens, tokens, segments, qkv_w, qv_bias, proj_w, up_w, down_w, up_b):
    rows = tokens.shape[0] // SEQ
    parts = 2 * sizes["x"]
    hbm = pl.BlockSpec(memory_space=pl.ANY)
    gathered = [(w.shape, BF16) for w in (proj_w, up_w, down_w)]

    def whole(*shape):
        return pl.BlockSpec(shape, lambda i, *_: (0,) * len(shape))

    return pl.pallas_call(
        lambda *refs: attend_kernel(sizes, *refs),
        name="attend",
        grid_spec=pltpu.PrefetchScalarGridSpec(
            num_scalar_prefetch=0,
            grid=(rows,),
            in_specs=[
                pl.BlockSpec(memory_space=pltpu.SMEM),
                whole(*tokens.shape),
                whole(*segments.shape),
                whole(*qkv_w.shape),
                whole(*qv_bias.shape),
                whole(*proj_w.shape),
                whole(*up_w.shape),
                whole(*down_w.shape),
                whole(*up_b.shape),
            ],
            out_specs=[
                pl.BlockSpec((SEQ, D), lambda i, *_: (i, 0)),
                pl.BlockSpec((SEQ, 3 * D), lambda i, *_: (i, 0)),
                pl.BlockSpec((1, HEADS, 2, 256, 384), lambda i, *_: (i, 0, 0, 0, 0)),
                pl.BlockSpec((SEQ, D), lambda i, *_: (i, 0)),
                whole(3, D, D),
                whole(8, LANES),
                whole(parts, 8, up_b.shape[0]),
                hbm,
                hbm,
                hbm,
            ],
            scratch_shapes=[
                pltpu.VMEM((2, 256, 384), F32),
                pltpu.VMEM((parts,) + qkv_w.shape, BF16),
                pltpu.VMEM((parts, 8, up_b.shape[0]), F32),
                pltpu.VMEM((8, up_b.shape[0]), F32),
            ]
            + [pltpu.VMEM(w.shape, BF16) for w in (proj_w, up_w, down_w)]
            + sum([gather_scratch(sizes) for _ in range(5)], [])
            + small_scratch(sizes, 8, LANES),
        ),
        out_shape=[
            jax.ShapeDtypeStruct((rows * SEQ, D), BF16),
            jax.ShapeDtypeStruct((rows * SEQ, 3 * D), BF16),
            jax.ShapeDtypeStruct((rows, HEADS, 2, 256, 384), BF16),
            jax.ShapeDtypeStruct((rows * SEQ, D), BF16),
            jax.ShapeDtypeStruct((3, D, D), BF16),
            jax.ShapeDtypeStruct((8, LANES), F32),
            jax.ShapeDtypeStruct((parts, 8, up_b.shape[0]), F32),
        ]
        + [jax.ShapeDtypeStruct((parts,) + w.shape, BF16) for w in (proj_w, up_w, down_w)],
        compiler_params=pltpu.CompilerParams(
            vmem_limit_bytes=VMEM_LIMIT, collective_id=0, has_side_effects=True
        ),
        cost_estimate=pl.CostEstimate(
            flops=rows * 3 * 10**9, bytes_accessed=rows * 6 * 10**6, transcendentals=rows * 2 * 10**6
        ),
    )(lens, tokens, segments, qkv_w, qv_bias, proj_w, up_w, down_w, up_b)

INV_SQRT_2PI = 0.3989422804014327


def gelu_pair(pre):
    cdf = 0.5 + 0.5 * lax.erf(pre * 0.7071067811865476)
    bell = jnp.exp2(pre * pre * (-0.5 * LOG2E))
    return pre * cdf, cdf + (pre * INV_SQRT_2PI) * bell


def fold_rows(values):
    total = values[0:8]
    for r in range(8, values.shape[0], 8):
        total = total + values[r : r + 8]
    return total


def normalize(values):
    centred = values - jnp.mean(values, axis=-1, keepdims=True)
    inverse = lax.rsqrt(jnp.mean(centred * centred, axis=-1, keepdims=True) + EPS)
    return centred * inverse, inverse


def norm_back(scaled, standard, inverse):
    return inverse * (
        scaled
        - jnp.mean(scaled, axis=-1, keepdims=True)
        - standard * jnp.mean(scaled * standard, axis=-1, keepdims=True)
    )


TB = 512


def ffn_kernel(
    step_ref,
    bias_ref,
    tok_ref,
    ctx_ref,
    og_ref,
    proj_ref,
    up_ref,
    down_ref,
    pb_ref,
    fg_ref,
    fs_ref,
    db_ref,
    sg_ref,
    ss_ref,
    out_ref,
    first_ref,
    gctx_ref,
    dproj_ref,
    dup_ref,
    ddown_ref,
    dub_ref,
    dvec_ref,
    act_s,
    slope_s,
    dproj_s,
    dup_s,
    ddown_s,
    dub_s,
    dvec_s,
):
    at = pl.program_id(0)
    last = pl.num_programs(0) - 1
    parts = up_ref.shape[0]
    step_proj, step_up, step_down = [step_ref[r : r + 1, 0:1] for r in (4, 5, 6)]

    @pl.when(at == 0)
    def _():
        dproj_s[...] = jnp.zeros_like(dproj_s)
        dup_s[...] = jnp.zeros_like(dup_s)
        ddown_s[...] = jnp.zeros_like(ddown_s)
        dub_s[...] = jnp.zeros_like(dub_s)
        dvec_s[...] = jnp.zeros_like(dvec_s)

    proj_bias, first_gain, first_shift, down_bias, second_gain, second_shift = [
        r[...].astype(F32)[None] for r in (pb_ref, fg_ref, fs_ref, db_ref, sg_ref, ss_ref)
    ]
    ctx = ctx_ref[...]
    first_in = tok_ref[...].astype(F32) + (dot_nn(ctx, proj_ref[...]) * step_proj + proj_bias)
    n1, r1 = normalize(first_in)
    normed = n1 * first_gain + first_shift
    low = normed.astype(BF16)
    branch = None
    pre = dot_nn(low, up_ref[0])
    for t in range(parts):
        follow = dot_nn(low, up_ref[t + 1]) if t + 1 < parts else None
        act, slope = gelu_pair(pre * step_up + bias_ref[t, 0:1])
        pre = follow
        act = act.astype(BF16)
        act_s[t] = act
        slope_s[t] = slope
        term = dot_nn(act, down_ref[t])
        branch = term if branch is None else branch + term
    second_in = normed + (branch * step_down + down_bias)
    n2, r2 = normalize(second_in)
    out_ref[...] = (n2 * second_gain + second_shift).astype(BF16)
    og = og_ref[...].astype(F32)
    grad_second = norm_back(og * second_gain, n2, r2)
    dvec_s[4] += fold_rows(og * n2)
    dvec_s[5] += fold_rows(og)
    dvec_s[3] += fold_rows(grad_second)
    grad_down = (grad_second * step_down).astype(BF16)
    back = grad_second
    grad_act = dot_nt(grad_down, down_ref[0])
    for t in range(parts):
        follow = dot_nt(grad_down, down_ref[t + 1]) if t + 1 < parts else None
        grad_pre = grad_act * slope_s[t]
        grad_act = follow
        dub_s[t] += fold_rows(grad_pre)
        grad_up = (grad_pre * step_up).astype(BF16)
        back = back + dot_nt(grad_up, up_ref[t])
        dup_s[t] += dot_tn(low, grad_up)
        ddown_s[t] += dot_tn(grad_down, act_s[t])
    dvec_s[1] += fold_rows(back * n1)
    dvec_s[2] += fold_rows(back)
    grad_first = norm_back(back * first_gain, n1, r1)
    dvec_s[0] += fold_rows(grad_first)
    first_ref[...] = grad_first
    grad_proj = (grad_first * step_proj).astype(BF16)
    dproj_s[...] += dot_tn(ctx, grad_proj)
    gctx_ref[...] = dot_nt(grad_proj, proj_ref[...]).astype(BF16)

    @pl.when(at == last)
    def _():
        width = D // parts
        for t in range(parts):
            rows = dproj_s[t * width : (t + 1) * width]
            dproj_ref[t] = spread(rows.astype(BF16), dproj_ref.shape[1:])
            dup_ref[t] = spread(dup_s[t].astype(BF16), dup_ref.shape[1:])
            ddown_ref[t] = spread(ddown_s[t].astype(BF16), ddown_ref.shape[1:])
            dub_ref[t] = jnp.sum(dub_s[t], axis=0, keepdims=True)
        dvec_ref[...] = jnp.sum(dvec_s[...], axis=1)


def feed_forward(sizes, steps, biases, tokens, ctx, out_grad, proj, up, down, vecs):
    count = tokens.shape[0]
    parts, nz = 2 * sizes["x"], sizes["z"]
    wide = FF // parts
    split = (parts, 2, 2, nz, split_rows(D, 4 * nz), wide)
    split_proj = (parts, 2, nz, split_rows(D // parts, 2 * nz), D)
    block = pl.BlockSpec((TB, D), lambda i, *_: (i, 0))

    def whole(*shape):
        return pl.BlockSpec(shape, lambda i, *_: (0,) * len(shape))

    return pl.pallas_call(
        ffn_kernel,
        name="feed_forward",
        grid=(count // TB,),
        in_specs=[
            whole(8, LANES),
            whole(parts, 8, wide),
            block,
            block,
            block,
            whole(D, D),
            whole(parts, D, wide),
            whole(parts, wide, D),
        ]
        + [whole(D)] * 6,
        out_specs=[
            block,
            block,
            block,
            whole(*split_proj),
            whole(*split),
            whole(*split),
            whole(parts, 1, wide),
            whole(6, D),
        ],
        scratch_shapes=[
            pltpu.VMEM((parts, TB, wide), BF16),
            pltpu.VMEM((parts, TB, wide), F32),
            pltpu.VMEM((D, D), F32),
            pltpu.VMEM((parts, D, wide), F32),
            pltpu.VMEM((parts, D, wide), F32),
            pltpu.VMEM((parts, 8, wide), F32),
            pltpu.VMEM((6, 8, D), F32),
        ],
        out_shape=[
            jax.ShapeDtypeStruct((count, D), BF16),
            jax.ShapeDtypeStruct((count, D), F32),
            jax.ShapeDtypeStruct((count, D), BF16),
            jax.ShapeDtypeStruct(split_proj, BF16),
            jax.ShapeDtypeStruct(split, BF16),
            jax.ShapeDtypeStruct(split, BF16),
            jax.ShapeDtypeStruct((parts, 1, wide), F32),
            jax.ShapeDtypeStruct((6, D), F32),
        ],
        compiler_params=pltpu.CompilerParams(vmem_limit_bytes=VMEM_LIMIT),
        cost_estimate=pl.CostEstimate(
            flops=count * 14 * 10**6, bytes_accessed=count * 12000, transcendentals=count * 4096
        ),
    )(steps, biases, tokens, ctx, out_grad, proj, up, down, *vecs)


PLANS = (
    ((0, 2), (2, 6), (7, 10), (10, 13), (13, 16), (16, 20)),
    ((0, 2), (2, 6), (7, 10), (11, 14), (15, 19), (19, 22)),
    ((0, 3), (4, 8), (8, 11), (12, 15), (16, 20), (21, 27)),
    ((0, 3), (4, 8), (8, 11), (17, 21), (21, 25), (25, 33)),
    ((0, 3), (9, 12), (12, 14), (19, 23), (23, 26), (29, 35)),
    ((16, 19), (19, 22), (23, 29), (29, 32), (32, 37), (37, 40)),
    ((16, 19), (19, 24), (24, 28), (28, 31), (31, 36), (36, 39)),
    ((16, 19), (19, 24), (24, 30), (30, 34), (34, 38), (38, 41)),
)
ORDERS = ('xy', 'yx', 'xy', 'yx', 'xy', 'xy', 'yx', 'xy')
THIRDS = 3


def passing(grads, weights, step):
    return jnp.where(weights.astype(F32) == 0.0, 0.0, grads.astype(F32)) / step


def back_kernel(
    sizes,
    step_ref,
    tok_ref,
    ints_ref,
    qkv_ref,
    probs_ref,
    ctx_ref,
    gctx_ref,
    first_ref,
    w_ref,
    dproj_hbm,
    dup_hbm,
    ddown_hbm,
    dub_ref,
    dvec_ref,
    tg_ref,
    dqkv_out,
    dqv_out,
    dproj_out,
    dup_out,
    dub_out,
    ddown_out,
    vec_out,
    grad_s,
    dqkv_s,
    dqv_s,
    part_s,
    *scratch,
):
    step = pl.program_id(0)
    rows = grad_s.shape[0]
    place = Place(sizes)
    parts = 2 * sizes["x"]
    width = D // parts
    step_tokens = step_ref[0:1, 0:1]
    sources = [
        lambda t: dup_hbm.at[t, 0],
        lambda t: ddown_hbm.at[t, 0],
        lambda t: dup_hbm.at[t, 1],
        lambda t: ddown_hbm.at[t, 1],
        lambda t: dproj_hbm.at[t],
    ]
    sources += [lambda t, q=q: part_s.at[t, q] for q in range(THIRDS)]
    streams = []
    for n, source in enumerate(sources):
        refs = scratch[9 * n : 9 * n + 9]
        own = refs[8] if n < 5 else None
        streams.append(Stream(place, ORDERS[n], source, *refs[:8], own))
    sums = Small(place, jnp.add, *scratch[9 * len(sources) :])

    @pl.when(step == 0)
    def _():
        dqkv_s[...] = jnp.zeros_like(dqkv_s)
        dqv_s[...] = jnp.zeros_like(dqv_s)
        place.greet()

    def events(now):
        for s, plan in enumerate(PLANS):
            for k, p in enumerate(plan):
                if p[1] == now:
                    streams[s].finish(k)
        for s, plan in enumerate(PLANS):
            for k, p in enumerate(plan):
                if p[0] == now:
                    streams[s].start(k)

    def advance(tick, ticks):
        for now in ticks:
            if any(now in p for plan in PLANS for p in plan):
                pl.when(tick == now)(lambda: events(now))

    def pair_step(p, carry):
        for n in range(16 // (PAIRS * rows)):
            advance((step * PAIRS + p) * (16 // (PAIRS * rows)) + n, range(16))
        at = pl.multiple_of(p * LANES, LANES)
        q_pair = qkv_ref[:, pl.ds(at, LANES)]
        k_pair = qkv_ref[:, pl.ds(D + at, LANES)]
        v_pair = qkv_ref[:, pl.ds(2 * D + at, LANES)]
        g_pair = gctx_ref[:, pl.ds(at, LANES)]
        c_pair = ctx_ref[:, pl.ds(at, LANES)]
        product = (g_pair.astype(F32) * c_pair.astype(F32)).astype(BF16)
        lane = lax.broadcasted_iota(jnp.int32, (8, LANES), 1)
        line = lax.broadcasted_iota(jnp.int32, (8, LANES), 0)
        ones = jnp.where(lane // HEAD_DIM == line, 1.0, 0.0).astype(BF16)
        centre = dot_nt(ones, product)
        outs = []
        for n, (k0, k1, q0, q1) in enumerate(TILES):
            probs = probs_ref[0, pl.ds(2 * p, 2), n]
            gp = dot_nt(stacked(v_pair[k0:k1]), g_pair[q0:q1])
            gs = jnp.concatenate(
                [
                    (probs[h].astype(F32) * (gp[256 * h : 256 * h + 256] - centre[h : h + 1, q0:q1])).astype(BF16)
                    for h in range(2)
                ],
                axis=0,
            )
            d_values = unstacked(dot_nn(probs.reshape(512, 384), g_pair[q0:q1]))
            d_keys = unstacked(dot_nn(gs, q_pair[q0:q1]))
            outs.append(dot_tn(gs, stacked(k_pair[k0:k1])))
            grad_s[step, k0:k1, pl.ds(D + at, LANES)] = (
                d_keys * (step_tokens * step_ref[2:3, 0:1] * (1.0 / LOG2E))
            ).astype(BF16)
            dqv_s[1, :, pl.ds(at, LANES)] += fold_rows(d_values)
            grad_s[step, k0:k1, pl.ds(2 * D + at, LANES)] = (
                d_values * (step_tokens * step_ref[3:4, 0:1])
            ).astype(BF16)
        d_q = both(*outs) * 0.125
        dqv_s[0, :, pl.ds(at, LANES)] += fold_rows(d_q)
        grad_s[step, :, pl.ds(at, LANES)] = (d_q * (step_tokens * step_ref[1:2, 0:1])).astype(BF16)
        return carry

    @pl.when(step < rows)
    def _():
        lax.fori_loop(0, PAIRS, pair_step, 0)
        for i in range(3):
            dqkv_s[i] += dot_tn(grad_s[step, :, i * D : (i + 1) * D], ints_ref[...])

    @pl.when(step == rows)
    def _():
        for t in range(parts):
            piece = jnp.concatenate(
                [dqkv_s[i, t * width : (t + 1) * width] for i in range(3)], axis=0
            )
            part_s[t] = spread(piece.astype(BF16), part_s.shape[1:])
        dqv = jnp.sum(dqv_s[...], axis=1)
        vec = [dvec_ref[r : r + 1] for r in range(6)] + [dqv[0:1], dqv[1:2]]
        dub = jnp.concatenate([dub_ref[t] for t in range(parts)], axis=1)
        vec += [dub[:, r * D : (r + 1) * D] for r in range(4)]
        sums.start(0, tile_rows(vec, 16, D))

    @pl.when(step >= rows)
    def _():
        for n in range(4 // rows):
            advance(16 + (step - rows) * (4 // rows) + n, range(16, 20))

    def vectors():
        total = sums.finish(1)
        for n in range(6):
            vec_out[n] = total[n : n + 1]
        for t in range(parts):

            @pl.when(place.part == t)
            def _():
                dqv_out[...] = total[6:8, t * width : (t + 1) * width]
                wide = FF // parts
                dub_out[...] = total[
                    8 + t * wide // D : 9 + t * wide // D, t * wide % D : t * wide % D + wide
                ]

    @pl.when(step == rows + 1)
    def _():
        sums.start(1, sums.finish(0))

    @pl.when(step >= rows)
    def _():
        grads = grad_s[step - rows]
        total = None
        for i in range(3):
            term = dot_nt(grads[:, i * D : (i + 1) * D], w_ref[i])
            total = term if total is None else total + term
        tg_ref[...] = (first_ref[...] + passing(total, tok_ref[...], step_tokens)).astype(BF16)

    def joined(*group):
        halves = [streams[n].out[...].reshape(D // 2, FF // parts) for n in group]
        return jnp.concatenate(halves, axis=0)

    @pl.when(step == 2 * rows - 1)
    def _():
        ticks = sorted({n for plan in PLANS for p in plan for n in p if n >= 20})
        ended = [max(PLANS[s][5][1] for s in group) for group in ((0, 2), (1, 3), (4,))]
        for now in [19] + ticks:
            if now > 19:
                events(now)
            if now == ticks[len(ticks) // 3]:
                vectors()
            if now == max(19, ended[0]):
                dup_out[...] = joined(0, 2)
            if now == max(19, ended[1]):
                ddown_out[...] = joined(1, 3)
            if now == max(19, ended[2]):
                dproj_out[...] = streams[4].out[...].reshape(-1, D)[:width]
        whole = jnp.concatenate(
            [streams[5 + q].out[...].reshape(-1, D) for q in range(THIRDS)], axis=0
        )
        dqkv_out[...] = whole[: 3 * width]


def deliver_kernel(
    step_ref,
    tg_ref,
    dqkv_ref,
    dqv_ref,
    dproj_ref,
    dup_ref,
    dub_ref,
    ddown_ref,
    vec_ref,
    qkv_ref,
    proj_ref,
    up_ref,
    down_ref,
    tg_out,
    dqkv_out,
    dqv_out,
    dproj_out,
    dup_out,
    dub_out,
    ddown_out,
    *vec_outs,
):
    width = dqkv_out.shape[-1]
    tg_out[...] = tg_ref[...].astype(F32)
    for i in range(3):
        grad = jnp.transpose(dqkv_ref[i * width : (i + 1) * width].astype(F32))
        dqkv_out[i] = passing(grad, qkv_ref[i], step_ref[1 + i : 2 + i, 0:1])
    dproj_out[...] = passing(dproj_ref[...], proj_ref[...], step_ref[4:5, 0:1])
    dup_out[...] = passing(dup_ref[...], up_ref[...], step_ref[5:6, 0:1])
    grad = jnp.transpose(ddown_ref[...].astype(F32))
    ddown_out[...] = passing(grad, down_ref[...], step_ref[6:7, 0:1])
    dqv_out[...] = dqv_ref[...]
    dub_out[...] = dub_ref[0]
    for n, out in enumerate(vec_outs):
        out[...] = vec_ref[n, 0]


def deliver(steps, tokens_grad, dqkv, dqv, dproj, dup, dub, ddown, vec, qkv_w, proj_w, up_w, down_w):
    rows = tokens_grad.shape[0] // SEQ
    width, wide = qkv_w.shape[2], up_w.shape[1]

    def whole(*shape):
        return pl.BlockSpec(shape, lambda i: (0,) * len(shape))

    def down_rows(*shape):
        return pl.BlockSpec((shape[0] // rows,) + shape[1:], lambda i: (i, 0))

    def along(*shape):
        return pl.BlockSpec((shape[0], shape[1] // rows), lambda i: (0, i))

    qkv_block = pl.BlockSpec((3, D // rows, width), lambda i: (0, i, 0))
    outs = [
        (tokens_grad.shape, down_rows(*tokens_grad.shape)),
        (qkv_w.shape, qkv_block),
        ((2, width), whole(2, width)),
        (proj_w.shape, down_rows(*proj_w.shape)),
        (up_w.shape, down_rows(*up_w.shape)),
        ((wide,), whole(wide)),
        (down_w.shape, down_rows(*down_w.shape)),
    ] + [((D,), whole(D))] * 6
    return pl.pallas_call(
        deliver_kernel,
        name="deliver",
        grid=(rows,),
        in_specs=[
            whole(8, LANES),
            down_rows(*tokens_grad.shape),
            along(*dqkv.shape),
            whole(2, width),
            down_rows(*dproj.shape),
            down_rows(*dup.shape),
            whole(1, wide),
            along(*ddown.shape),
            whole(6, 1, D),
            qkv_block,
            down_rows(*proj_w.shape),
            down_rows(*up_w.shape),
            down_rows(*down_w.shape),
        ],
        out_specs=[spec for _, spec in outs],
        out_shape=[jax.ShapeDtypeStruct(shape, F32) for shape, _ in outs],
        compiler_params=pltpu.CompilerParams(vmem_limit_bytes=VMEM_LIMIT),
    )(steps, tokens_grad, dqkv, dqv, dproj, dup, dub, ddown, vec, qkv_w, proj_w, up_w, down_w)


def attend_back(
    sizes, steps, tokens, ints, qkv, probs, ctx, gctx, first, qkv_full, dproj, dup, ddown, dub, dvec
):
    rows = tokens.shape[0] // SEQ
    parts, nz = 2 * sizes["x"], sizes["z"]
    width, wide = D // parts, FF // parts
    part = (parts, THIRDS, 2, nz, split_rows(3 * width, 2 * THIRDS * nz), D)
    pieces = [dup.shape[-2:], ddown.shape[-2:], dup.shape[-2:], ddown.shape[-2:], dproj.shape[-2:]]
    pieces += [part[-2:]] * THIRDS
    early = lambda i: (jnp.minimum(i, rows - 1), 0)
    late = lambda i: (jnp.maximum(i - rows, 0), 0)
    hbm = pl.BlockSpec(memory_space=pl.ANY)

    def whole(*shape):
        return pl.BlockSpec(shape, lambda i: (0,) * len(shape))

    outs = [
        ((3 * width, D), BF16),
        ((2, width), F32),
        ((width, D), BF16),
        ((D, wide), BF16),
        ((1, wide), F32),
        ((D, wide), BF16),
        ((6, 1, D), F32),
    ]
    return pl.pallas_call(
        lambda *refs: back_kernel(sizes, *refs),
        name="attend_back",
        grid=(2 * rows,),
        in_specs=[
            whole(8, LANES),
            pl.BlockSpec((SEQ, D), late),
            pl.BlockSpec((SEQ, D), early),
            pl.BlockSpec((SEQ, 3 * D), early),
            pl.BlockSpec(
                (1, HEADS, 2, 256, 384), lambda i: (jnp.minimum(i, rows - 1), 0, 0, 0, 0)
            ),
            pl.BlockSpec((SEQ, D), early),
            pl.BlockSpec((SEQ, D), early),
            pl.BlockSpec((SEQ, D), late),
            whole(3, D, D),
            hbm,
            hbm,
            hbm,
            whole(*dub.shape),
            whole(*dvec.shape),
        ],
        out_specs=[pl.BlockSpec((SEQ, D), late)] + [whole(*shape) for shape, _ in outs],
        scratch_shapes=[
            pltpu.VMEM((rows, SEQ, 3 * D), BF16),
            pltpu.VMEM((3, D, D), F32),
            pltpu.VMEM((2, 8, D), F32),
            pltpu.VMEM(part, BF16),
        ]
        + sum([stream_scratch(sizes, o, *p) for o, p in zip(ORDERS, pieces)], [])
        + small_scratch(sizes, 16, D),
        out_shape=[jax.ShapeDtypeStruct((rows * SEQ, D), BF16)]
        + [jax.ShapeDtypeStruct(shape, kind) for shape, kind in outs],
        compiler_params=pltpu.CompilerParams(
            vmem_limit_bytes=VMEM_LIMIT, collective_id=1, has_side_effects=True
        ),
        cost_estimate=pl.CostEstimate(
            flops=rows * 6 * 10**9, bytes_accessed=rows * 8 * 10**6, transcendentals=0
        ),
    )(
        steps, tokens, ints, qkv, probs, ctx, gctx, first, qkv_full, dproj, dup, ddown, dub, dvec
    )

def local(
    tokens,
    segment_ids,
    row_lengths,
    qkv_weight,
    qv_bias,
    proj_weight,
    proj_bias,
    first_gain,
    first_shift,
    up_weight,
    up_bias,
    down_weight,
    down_bias,
    second_gain,
    second_shift,
    out_grad,
):
    rows = tokens.shape[0] // SEQ
    sizes = group_sizes(lax.axis_size("tensor"), lax.axis_size("dp"))
    ints, qkv, probs, ctx, qkv_full, steps, biases, proj_full, up_full, down_full = attend(
        sizes,
        row_lengths,
        tokens,
        segment_ids,
        qkv_weight,
        qv_bias,
        proj_weight,
        up_weight,
        down_weight,
        up_bias,
    )
    vecs = (proj_bias, first_gain, first_shift, down_bias, second_gain, second_shift)
    layer_out, grad_first, grad_ctx, dproj, dup, ddown, dub, dvec = feed_forward(
        sizes, steps, biases, tokens, ctx, out_grad, proj_full.reshape(D, D), up_full, down_full, vecs
    )
    sums = attend_back(
        sizes, steps, tokens, ints, qkv, probs, ctx, grad_ctx, grad_first, qkv_full,
        dproj, dup, ddown, dub, dvec,
    )
    tokens_grad, dqkv, dqv, dproj, dup, dub, ddown, *vec = deliver(
        steps, *sums, qkv_weight, proj_weight, up_weight, down_weight
    )
    return (
        layer_out, tokens_grad, dqkv, dqv, dproj, vec[0], vec[1], vec[2], dup, dub, ddown,
        vec[3], vec[4], vec[5],
    )


def solution(mesh):
    in_specs = (
        P(("dp", "tensor"), None),
        P("dp", None),
        P("dp"),
        P(None, None, "tensor"),
        P(None, "tensor"),
        P("tensor", None),
        P(),
        P(),
        P(),
        P(None, "tensor"),
        P("tensor"),
        P("tensor", None),
        P(),
        P(),
        P(),
        P(("dp", "tensor"), None),
    )
    out_specs = (
        P(("dp", "tensor"), None),
        P(("dp", "tensor"), None),
        P(None, None, "tensor"),
        P(None, "tensor"),
        P("tensor", None),
        P(),
        P(),
        P(),
        P(None, "tensor"),
        P("tensor"),
        P("tensor", None),
        P(),
        P(),
        P(),
    )
    return jax.shard_map(local, mesh=mesh, in_specs=in_specs, out_specs=out_specs, check_vma=False)
```

```python
import jax
import jax.numpy as jnp
from jax import lax
from jax.experimental import pallas as pl
from jax.experimental.pallas import tpu as pltpu
from jax.sharding import PartitionSpec as P

D = 512
HEADS = 8
HEAD_DIM = 64
FF = 2048
SEQ = 512
PAIRS = 4
LANES = 128
LEVELS = 127.0
EPS = 1e-12
MASKED = -1e30
LOG2E = 1.4426950408889634
SCORE_SCALE = 0.125 * LOG2E
VMEM_LIMIT = 58 << 20
F32 = jnp.float32
BF16 = jnp.bfloat16
TILES = ((0, 256, 0, 384), (256, 512, 128, 512))


def rounded(scaled):
    magnitude = jnp.floor(jnp.abs(scaled) + 0.5)
    return jnp.where(scaled < 0.0, -magnitude, magnitude)


def dot_nn(a, b):
    return lax.dot_general(a, b, (((1,), (0,)), ((), ())), preferred_element_type=F32)


def dot_nt(a, b):
    return lax.dot_general(a, b, (((1,), (1,)), ((), ())), preferred_element_type=F32)


def dot_tn(a, b):
    return lax.dot_general(a, b, (((0,), (0,)), ((), ())), preferred_element_type=F32)


def head_mask(head, rows):
    lane = lax.broadcasted_iota(jnp.int32, (rows, LANES), 1)
    return (lane < HEAD_DIM) if head == 0 else (lane >= HEAD_DIM)


def stacked(pair):
    zeros = jnp.zeros_like(pair)
    return jnp.concatenate(
        [jnp.where(head_mask(h, pair.shape[0]), pair, zeros) for h in range(2)], axis=0
    )


def unstacked(blocks):
    rows = blocks.shape[0] // 2
    return jnp.where(head_mask(0, rows), blocks[:rows], blocks[rows:])


def both(left, right):
    return jnp.concatenate([left[:128], left[128:] + right[:256], right[256:]], axis=0)


MESH = pl.DeviceIdType.MESH
MESH_AXES = ("tensor", "dp")


def group_sizes(tensor_size, dp_size):
    return {
        "core": 2,
        "x": tensor_size // 2,
        "y": 2,
        "z": dp_size // 2,
        "tensor": tensor_size,
        "dp": dp_size,
    }


class Place:
    def __init__(self, sizes):
        t, d = lax.axis_index("tensor"), lax.axis_index("dp")
        self.sizes = sizes
        self.part = t
        self.at = {"core": t % 2, "x": t // 2, "y": d % 2, "z": d // 2, "tensor": t, "dp": d}

    def size(self, group):
        return self.sizes[group]

    def peer(self, group, k):
        if group in MESH_AXES:
            at = {axis: lax.axis_index(axis) for axis in MESH_AXES}
            at[group] = (at[group] + k) % self.sizes[group]
            return at[group], (at["dp"], at["tensor"])
        at = dict(self.at)
        at[group] = (at[group] + k) % self.sizes[group]
        return at[group], (at["z"] * 2 + at["y"], at["x"] * 2 + at["core"])

    def greet(self):
        self.hello()
        self.welcome()

    def welcome(self, others=0):
        count = sum(self.sizes[group] - 1 for group in MESH_AXES) + others
        pl.semaphore_wait(pltpu.get_barrier_semaphore(), count)

    def plane(self):
        members = []
        for k in range(self.sizes["x"]):
            for side in range(2):
                if k or side:
                    at = dict(self.at)
                    at["x"] = (at["x"] + k) % self.sizes["x"]
                    at["y"] = (at["y"] + side) % 2
                    device = (at["z"] * 2 + at["y"], at["x"] * 2 + at["core"])
                    members.append((at["x"], at["y"], device))
        return members

    def hello(self, *others):
        barrier = pltpu.get_barrier_semaphore()
        for device in others:
            pl.semaphore_signal(barrier, inc=1, device_id=device, device_id_type=MESH)
        for group in MESH_AXES:
            for k in range(1, self.sizes[group]):
                pl.semaphore_signal(
                    barrier, inc=1, device_id=self.peer(group, k)[1], device_id_type=MESH
                )


class Sems:
    def __init__(self, send, recv):
        self.send, self.recv = send, recv

    def copy(self, at, source, target, device):
        return pltpu.make_async_remote_copy(
            src_ref=source,
            dst_ref=target,
            send_sem=self.send.at[at],
            recv_sem=self.recv.at[at],
            device_id=device,
            device_id_type=MESH,
        )


def exchange(place, group, source, target, sems, base):
    copies = []
    for k in range(1, place.size(group)):
        index, device = place.peer(group, k)
        copies.append(sems.copy(base + k - 1, source(k, index), target(k, index), device))
    return copies


def add(first, *others):
    total = first.astype(F32)
    for other in others:
        total = total + other.astype(F32)
    return total.astype(BF16)


class Stream:
    phases = 6

    def __init__(self, place, order, grad, held, got_c, got_1, got_2, got_z, out, send, recv, own):
        self.place, self.order, self.grad, self.held, self.out = place, order, grad, held, out
        self.got_c, self.got_1, self.got_2, self.got_z = got_c, got_1, got_2, got_z
        self.sems, self.own = Sems(send, recv), own

    def local(self):
        if self.own is None:
            return []
        return [
            pltpu.make_async_copy(
                self.grad(2 * i + self.place.at["core"]), self.held.at[i], self.own.at[i]
            )
            for i in range(self.place.size("x"))
        ]

    def copies(self, phase):
        place, at, held = self.place, self.place.at, self.held
        nx, nz = place.size("x"), place.size("z")
        base = [0, nx, 2 * nx, 3 * nx, 3 * nx + nz, 3 * nx + 2 * nz][phase]
        sems = self.sems
        if phase == 0:
            other, device = place.peer("core", 1)
            return [
                sems.copy(i, self.grad(2 * i + other), self.got_c.at[i], device) for i in range(nx)
            ]
        if self.order == "plane":
            if phase == 2:
                return []
            if phase == 1:
                return [
                    sems.copy(base + n, held.at[x, y], self.got_1.at[n], device)
                    for n, (x, y, device) in enumerate(place.plane())
                ]
        if phase == 1 and self.order == "xy":
            return exchange(
                place, "x", lambda k, j: held.at[j], lambda k, j: self.got_1.at[k - 1], sems, base
            )
        if phase == 2 and self.order == "xy":
            return exchange(
                place, "y", lambda k, j: held.at[at["x"], j], lambda k, j: self.got_2.at[0], sems, base
            )
        if phase == 1:
            other, device = place.peer("y", 1)
            return [
                sems.copy(base + i, held.at[i, other], self.got_1.at[i], device) for i in range(nx)
            ]
        if phase == 2:
            return exchange(
                place,
                "x",
                lambda k, j: held.at[j, at["y"]],
                lambda k, j: self.got_2.at[k - 1],
                sems,
                base,
            )
        if phase == 3:
            return exchange(
                place,
                "z",
                lambda k, j: held.at[at["x"], at["y"], j],
                lambda k, j: self.got_z.at[k - 1],
                sems,
                base,
            )
        if phase == 4:
            piece = self.out.at[at["y"], at["z"]]
            return exchange(place, "z", lambda k, j: piece, lambda k, j: piece, sems, base)
        half = self.out.at[at["y"]]
        return exchange(place, "y", lambda k, j: half, lambda k, j: half, sems, base)

    def start(self, phase):
        for copy in self.copies(phase) + (self.local() if phase == 0 else []):
            copy.start()

    def finish(self, phase):
        for copy in self.copies(phase) + (self.local() if phase == 0 else []):
            copy.wait()
        at, held = self.place.at, self.held
        nx, nz = self.place.size("x"), self.place.size("z")
        if phase == 0:
            for i in range(nx):
                for y in range(2):
                    own = held[i, y] if self.own is not None else self.grad(2 * i + at["core"])[y]
                    held[i, y] = add(own, self.got_c[i, y])
        elif phase == 1 and self.order == "xy":
            for y in range(2):
                held[at["x"], y] = add(
                    held[at["x"], y], *[self.got_1[k, y] for k in range(nx - 1)]
                )
        elif phase == 1 and self.order == "plane":
            held[at["x"], at["y"]] = add(
                held[at["x"], at["y"]], *[self.got_1[n] for n in range(2 * nx - 1)]
            )
        elif phase == 1:
            for i in range(nx):
                held[i, at["y"]] = add(held[i, at["y"]], self.got_1[i])
        elif phase == 2 and self.order != "plane":
            count = 1 if self.order == "xy" else nx - 1
            held[at["x"], at["y"]] = add(
                held[at["x"], at["y"]], *[self.got_2[k] for k in range(count)]
            )
        elif phase == 3:
            self.out[at["y"], at["z"]] = add(
                held[at["x"], at["y"], at["z"]], *[self.got_z[k] for k in range(nz - 1)]
            )


def stream_scratch(sizes, order, rows, lanes):
    nx, nz = sizes["x"], sizes["z"]
    count = 3 * nx + 2 * nz + 1
    piece = (nz, rows, lanes)
    first = {"xy": (nx - 1, 2), "yx": (nx,), "plane": (2 * nx - 1,)}[order]
    second = (nx - 1,) if order == "yx" else (1,)
    return [
        pltpu.VMEM((nx, 2) + piece, BF16),
        pltpu.VMEM((nx, 2) + piece, BF16),
        pltpu.VMEM(first + piece, BF16),
        pltpu.VMEM(second + piece, BF16),
        pltpu.VMEM((nz - 1,) + piece[1:], BF16),
        pltpu.VMEM((2,) + piece, BF16),
        pltpu.SemaphoreType.DMA((count,)),
        pltpu.SemaphoreType.DMA((count,)),
        pltpu.SemaphoreType.DMA((nx,)),
    ]


class Small:
    def __init__(self, place, combine, slots, send, recv):
        self.place, self.combine, self.slots, self.sems = place, combine, slots, Sems(send, recv)

    def offsets(self, phase):
        sizes = [self.place.size(g) for g in MESH_AXES]
        return sum(sizes[:phase]), sum(sizes[:phase]) - phase

    def copies(self, phase):
        slot, sem = self.offsets(phase)
        return exchange(
            self.place,
            MESH_AXES[phase],
            lambda k, j: self.slots.at[slot],
            lambda k, j: self.slots.at[slot + k],
            self.sems,
            sem,
        )

    def start(self, phase, values):
        self.slots[self.offsets(phase)[0]] = values
        for copy in self.copies(phase):
            copy.start()

    def finish(self, phase):
        for copy in self.copies(phase):
            copy.wait()
        slot = self.offsets(phase)[0]
        count, me = self.place.size(MESH_AXES[phase]), self.place.at[MESH_AXES[phase]]
        total = None
        for member in range(count):
            term = self.slots[slot + (me + count - member) % count]
            total = term if total is None else self.combine(total, term)
        return total


def small_scratch(sizes, rows, lanes):
    total = sum(sizes[g] for g in MESH_AXES)
    return [
        pltpu.VMEM((total, rows, lanes), F32),
        pltpu.SemaphoreType.DMA((total - 2,)),
        pltpu.SemaphoreType.DMA((total - 2,)),
    ]


class Gather:
    def __init__(self, place, own, every, send, recv, keep):
        self.place, self.own, self.every, self.sems, self.keep = place, own, every, Sems(send, recv), keep

    def far(self):
        place = self.place
        mine = self.every.at[place.part]
        return exchange(place, "x", lambda k, j: self.own, lambda k, j: mine, self.sems, 0)

    def near(self, step):
        place = self.place
        nx = place.size("x")
        device = place.peer("core", 1)[1]
        if step == 0:
            return self.sems.copy(nx - 1, self.own, self.every.at[place.part], device)
        chip = (place.at["x"] + nx - step) % nx
        block = self.every.at[chip * 2 + place.at["core"]]
        return self.sems.copy(nx - 1 + step, block, block, device)

    def mine(self):
        return pltpu.make_async_copy(self.own, self.every.at[self.place.part], self.keep.at[0])

    def start(self):
        for copy in self.far():
            copy.start()
        self.near(0).start()
        self.mine().start()

    def forward(self):
        for copy in self.far():
            copy.wait()
        for k in range(1, self.place.size("x")):
            self.near(k).start()

    def finish(self):
        for k in range(self.place.size("x")):
            self.near(k).wait()
        self.mine().wait()


class SplitGather(Gather):
    def far(self):
        place, y = self.place, self.place.at["y"]
        mine, half = self.every.at[place.part, y], self.own.at[y]
        return exchange(place, "x", lambda k, j: half, lambda k, j: mine, self.sems, 0)

    def side(self):
        place = self.place
        nx, y = place.size("x"), place.at["y"]
        copies = []
        for k in range(1, nx):
            chip = (place.at["x"] + nx - k) % nx
            half = self.every.at[chip * 2 + place.at["core"], y]
            copies.append(self.sems.copy(2 * nx - 2 + k, half, half, place.peer("y", 1)[1]))
        return copies

    def cross(self):
        for copy in self.far():
            copy.wait()
        for copy in self.side():
            copy.start()

    def forward(self):
        for copy in self.side():
            copy.wait()
        for k in range(1, self.place.size("x")):
            self.near(k).start()


def gather_scratch(sizes):
    count = 3 * sizes["x"] - 2
    return [
        pltpu.SemaphoreType.DMA((count,)),
        pltpu.SemaphoreType.DMA((count,)),
        pltpu.SemaphoreType.DMA((1,)),
    ]


def split_rows(rows, pieces):
    return -(-rows // (pieces * 8)) * 8


def spread(values, shape):
    count = 1
    for size in shape[:-1]:
        count *= size
    if count > values.shape[0]:
        zeros = jnp.zeros((count - values.shape[0], values.shape[1]), values.dtype)
        values = jnp.concatenate([values, zeros], axis=0)
    return values.reshape(shape)


def tile_rows(rows, height, lanes):
    filled = [r if r.shape[1] == lanes else jnp.concatenate([r, jnp.zeros((1, lanes - r.shape[1]), F32)], axis=1) for r in rows]
    at = lax.broadcasted_iota(jnp.int32, (height, lanes), 0)
    total = jnp.zeros((height, lanes), F32)
    for n, r in enumerate(filled):
        total = jnp.where(at == n, r, total)
    return total


def top(values):
    peak = jnp.max(jnp.abs(values.astype(F32)), axis=0, keepdims=True)
    return jnp.max(peak, axis=1, keepdims=True)


def attend_kernel(
    sizes,
    len_ref,
    tok_ref,
    seg_ref,
    qkv_sh,
    qvb_sh,
    proj_sh,
    up_sh,
    down_sh,
    ub_sh,
    ints_ref,
    qkv_ref,
    probs_ref,
    ctx_ref,
    w_ref,
    step_ref,
    bias_ref,
    proj_all,
    up_all,
    down_all,
    mask_s,
    ints_s,
    raw_all,
    bias_all,
    bias_own,
    proj_own,
    up_own,
    down_own,
    *sems,
):
    row = pl.program_id(0)
    last = pl.num_programs(0) - 1
    place = Place(sizes)
    parts = 2 * sizes["x"]
    width = D // parts
    early = [
        Gather(place, own, every, *sems[3 * n : 3 * n + 3])
        for n, (own, every) in enumerate(((qkv_sh, raw_all), (bias_own, bias_all)))
    ]
    late = [
        SplitGather(place, own, every, *sems[6 + 3 * n : 9 + 3 * n])
        for n, (own, every) in enumerate(
            ((proj_own, proj_all), (up_own, up_all), (down_own, down_all))
        )
    ]
    peaks = Small(place, jnp.maximum, *sems[15:18])

    @pl.when(row == 0)
    def _():
        place.hello()
        bias_own[...] = tile_rows(
            [ub_sh[...].astype(F32)[None], qvb_sh[0:1].astype(F32), qvb_sh[1:2].astype(F32)],
            8,
            ub_sh.shape[0],
        )
        tops = [top(tok_ref[...])] + [top(qkv_sh[i]) for i in range(3)]
        tops += [top(proj_sh[...]), top(up_sh[...]), top(down_sh[...])]
        total = tile_rows([jnp.broadcast_to(t, (1, LANES)) for t in tops], 8, LANES)
        place.welcome()
        peaks.start(0, total)
        for gather in early:
            gather.start()
        peaks.start(1, peaks.finish(0))
        step_ref[...] = peaks.finish(1) / LEVELS
        for own, shard, r in ((proj_own, proj_sh, 4), (up_own, up_sh, 5), (down_own, down_sh, 6)):
            for h in range(2):
                half = shard[h * own.shape[1] : (h + 1) * own.shape[1]]
                own[h] = rounded(half.astype(F32) / step_ref[r : r + 1, 0:1]).astype(BF16)
        for r in range(ints_s.shape[0] // SEQ):
            rows = slice(r * SEQ, (r + 1) * SEQ)
            ints_s[rows] = rounded(tok_ref[rows].astype(F32) / step_ref[0:1, 0:1]).astype(BF16)
            if r == 0:
                for gather in early:
                    gather.forward()
        for gather in early:
            gather.finish()
        for gather in late:
            gather.start()
        bias_ref[...] = bias_all[...]
        for t in range(parts):
            for i in range(3):
                w_ref[i, :, t * width : (t + 1) * width] = rounded(
                    raw_all[t, i].astype(F32) / step_ref[1 + i : 2 + i, 0:1]
                ).astype(BF16)

    for n, gather in enumerate(late):
        pl.when(row == jnp.minimum((1, 1, 2)[n], last))(gather.cross)

    @pl.when(row == last)
    def _():
        for gather in late:
            gather.forward()

    step_tokens = step_ref[0:1, 0:1]
    ints = ints_s[pl.ds(pl.multiple_of(row * SEQ, SEQ), SEQ), :]
    ints_ref[...] = ints
    biases = [
        jnp.concatenate([bias_all[t, r : r + 1, :width] for t in range(parts)], axis=1)
        for r in (1, 2)
    ]
    for i in range(3):
        raw = dot_nn(ints, w_ref[i]) * (step_tokens * step_ref[1 + i : 2 + i, 0:1])
        if i == 0:
            raw = (raw + biases[0]) * SCORE_SCALE
        if i == 2:
            raw = raw + biases[1]
        qkv_ref[:, i * D : (i + 1) * D] = raw.astype(BF16)
    here = place.part * pl.num_programs(0) + row
    seg_q = seg_ref[pl.ds(here, 1), :].astype(F32)
    length = len_ref[here]
    spot = lax.broadcasted_iota(jnp.int32, (8, SEQ), 1)
    seg_k = jnp.where(spot < length, jnp.broadcast_to(seg_q, (8, SEQ)), -1.0)
    seg_k = jnp.transpose(seg_k)[:, 0:1]
    for n, (k0, k1, q0, q1) in enumerate(TILES):
        keys = lax.broadcasted_iota(jnp.int32, (k1 - k0, q1 - q0), 0) + k0
        queries = lax.broadcasted_iota(jnp.int32, (k1 - k0, q1 - q0), 1) + q0
        allowed = (seg_k[k0:k1] == seg_q[:, q0:q1]) | (keys == queries)
        mask_s[n] = jnp.where(allowed, 0.0, MASKED)

    def pair_step(p, carry):
        at = pl.multiple_of(p * LANES, LANES)
        q_pair = qkv_ref[:, pl.ds(at, LANES)]
        k_pair = qkv_ref[:, pl.ds(D + at, LANES)]
        v_pair = qkv_ref[:, pl.ds(2 * D + at, LANES)]
        scores = []
        for n, (k0, k1, q0, q1) in enumerate(TILES):
            s = dot_nt(stacked(k_pair[k0:k1]), q_pair[q0:q1])
            scores.append(s.reshape(2, 256, 384) + mask_s[n])
        peak = [jnp.max(s, axis=1, keepdims=True) for s in scores]
        high = jnp.concatenate(
            [
                peak[0][:, :, :128],
                jnp.maximum(peak[0][:, :, 128:], peak[1][:, :, :256]),
                peak[1][:, :, 256:],
            ],
            axis=2,
        )
        weights = [jnp.exp2(s - high[:, :, q0:q1]) for s, (k0, k1, q0, q1) in zip(scores, TILES)]
        sums = [jnp.sum(w, axis=1, keepdims=True) for w in weights]
        totals = jnp.concatenate(
            [
                sums[0][:, :, :128],
                sums[0][:, :, 128:] + sums[1][:, :, :256],
                sums[1][:, :, 256:],
            ],
            axis=2,
        )
        inverse = 1.0 / totals
        outs = []
        for n, (k0, k1, q0, q1) in enumerate(TILES):
            probs = (weights[n] * inverse[:, :, q0:q1]).astype(BF16)
            probs_ref[0, pl.ds(2 * p, 2), n] = probs
            outs.append(dot_tn(probs.reshape(512, 384), stacked(v_pair[k0:k1])))
        ctx_ref[:, pl.ds(at, LANES)] = both(*outs).astype(BF16)
        return carry

    lax.fori_loop(0, PAIRS, pair_step, 0)

    @pl.when(row == last)
    def _():
        for gather in late:
            gather.finish()


def attend(sizes, lens, tokens, segments, qkv_w, qv_bias, proj_w, up_w, down_w, up_b):
    rows = tokens.shape[0] // SEQ
    parts = 2 * sizes["x"]
    hbm = pl.BlockSpec(memory_space=pl.ANY)
    halves = [(2, w.shape[0] // 2, w.shape[1]) for w in (proj_w, up_w, down_w)]

    def whole(*shape):
        return pl.BlockSpec(shape, lambda i, *_: (0,) * len(shape))

    return pl.pallas_call(
        lambda *refs: attend_kernel(sizes, *refs),
        name="attend",
        grid_spec=pltpu.PrefetchScalarGridSpec(
            num_scalar_prefetch=0,
            grid=(rows,),
            in_specs=[
                pl.BlockSpec(memory_space=pltpu.SMEM),
                whole(*tokens.shape),
                whole(*segments.shape),
                whole(*qkv_w.shape),
                whole(*qv_bias.shape),
                whole(*proj_w.shape),
                whole(*up_w.shape),
                whole(*down_w.shape),
                whole(*up_b.shape),
            ],
            out_specs=[
                pl.BlockSpec((SEQ, D), lambda i, *_: (i, 0)),
                pl.BlockSpec((SEQ, 3 * D), lambda i, *_: (i, 0)),
                pl.BlockSpec((1, HEADS, 2, 256, 384), lambda i, *_: (i, 0, 0, 0, 0)),
                pl.BlockSpec((SEQ, D), lambda i, *_: (i, 0)),
                whole(3, D, D),
                whole(8, LANES),
                whole(parts, 8, up_b.shape[0]),
                hbm,
                hbm,
                hbm,
            ],
            scratch_shapes=[
                pltpu.VMEM((2, 256, 384), F32),
                pltpu.VMEM(tokens.shape, BF16),
                pltpu.VMEM((parts,) + qkv_w.shape, BF16),
                pltpu.VMEM((parts, 8, up_b.shape[0]), F32),
                pltpu.VMEM((8, up_b.shape[0]), F32),
            ]
            + [pltpu.VMEM(shape, BF16) for shape in halves]
            + sum([gather_scratch(sizes) for _ in range(5)], [])
            + small_scratch(sizes, 8, LANES),
        ),
        out_shape=[
            jax.ShapeDtypeStruct((rows * SEQ, D), BF16),
            jax.ShapeDtypeStruct((rows * SEQ, 3 * D), BF16),
            jax.ShapeDtypeStruct((rows, HEADS, 2, 256, 384), BF16),
            jax.ShapeDtypeStruct((rows * SEQ, D), BF16),
            jax.ShapeDtypeStruct((3, D, D), BF16),
            jax.ShapeDtypeStruct((8, LANES), F32),
            jax.ShapeDtypeStruct((parts, 8, up_b.shape[0]), F32),
        ]
        + [jax.ShapeDtypeStruct((parts,) + shape, BF16) for shape in halves],
        compiler_params=pltpu.CompilerParams(
            vmem_limit_bytes=VMEM_LIMIT, collective_id=0, has_side_effects=True
        ),
        cost_estimate=pl.CostEstimate(
            flops=rows * 3 * 10**9, bytes_accessed=rows * 6 * 10**6, transcendentals=rows * 2 * 10**6
        ),
    )(lens, tokens, segments, qkv_w, qv_bias, proj_w, up_w, down_w, up_b)

INV_SQRT_2PI = 0.3989422804014327


def gelu_pair(pre):
    cdf = 0.5 + 0.5 * lax.erf(pre * 0.7071067811865476)
    bell = jnp.exp2(pre * pre * (-0.5 * LOG2E))
    return pre * cdf, cdf + (pre * INV_SQRT_2PI) * bell


def fold_rows(values):
    total = values[0:8]
    for r in range(8, values.shape[0], 8):
        total = total + values[r : r + 8]
    return total


def normalize(values):
    centred = values - jnp.mean(values, axis=-1, keepdims=True)
    inverse = lax.rsqrt(jnp.mean(centred * centred, axis=-1, keepdims=True) + EPS)
    return centred * inverse, inverse


def norm_back(scaled, standard, inverse):
    return inverse * (
        scaled
        - jnp.mean(scaled, axis=-1, keepdims=True)
        - standard * jnp.mean(scaled * standard, axis=-1, keepdims=True)
    )


TB = 512


def ffn_kernel(
    step_ref,
    bias_ref,
    tok_ref,
    ctx_ref,
    og_ref,
    proj_ref,
    up_ref,
    down_ref,
    pb_ref,
    fg_ref,
    fs_ref,
    db_ref,
    sg_ref,
    ss_ref,
    out_ref,
    first_ref,
    gctx_ref,
    dproj_ref,
    dup_ref,
    ddown_ref,
    dub_ref,
    dvec_ref,
    act_s,
    slope_s,
    dproj_s,
    dup_s,
    ddown_s,
    dub_s,
    dvec_s,
):
    at = pl.program_id(0)
    last = pl.num_programs(0) - 1
    parts = up_ref.shape[0]
    step_proj, step_up, step_down = [step_ref[r : r + 1, 0:1] for r in (4, 5, 6)]

    @pl.when(at == 0)
    def _():
        dproj_s[...] = jnp.zeros_like(dproj_s)
        dup_s[...] = jnp.zeros_like(dup_s)
        ddown_s[...] = jnp.zeros_like(ddown_s)
        dub_s[...] = jnp.zeros_like(dub_s)
        dvec_s[...] = jnp.zeros_like(dvec_s)

    proj_bias, first_gain, first_shift, down_bias, second_gain, second_shift = [
        r[...].astype(F32)[None] for r in (pb_ref, fg_ref, fs_ref, db_ref, sg_ref, ss_ref)
    ]
    ctx = ctx_ref[...]
    first_in = tok_ref[...].astype(F32) + (dot_nn(ctx, proj_ref[...]) * step_proj + proj_bias)
    n1, r1 = normalize(first_in)
    normed = n1 * first_gain + first_shift
    low = normed.astype(BF16)
    branch = None
    pre = dot_nn(low, up_ref[0])
    for t in range(parts):
        follow = dot_nn(low, up_ref[t + 1]) if t + 1 < parts else None
        act, slope = gelu_pair(pre * step_up + bias_ref[t, 0:1])
        pre = follow
        act = act.astype(BF16)
        act_s[t] = act
        slope_s[t] = slope
        term = dot_nn(act, down_ref[t])
        branch = term if branch is None else branch + term
    second_in = normed + (branch * step_down + down_bias)
    n2, r2 = normalize(second_in)
    out_ref[...] = (n2 * second_gain + second_shift).astype(BF16)
    og = og_ref[...].astype(F32)
    grad_second = norm_back(og * second_gain, n2, r2)
    dvec_s[4] += fold_rows(og * n2)
    dvec_s[5] += fold_rows(og)
    dvec_s[3] += fold_rows(grad_second)
    grad_down = (grad_second * step_down).astype(BF16)
    back = grad_second
    grad_act = dot_nt(grad_down, down_ref[0])
    for t in range(parts):
        follow = dot_nt(grad_down, down_ref[t + 1]) if t + 1 < parts else None
        grad_pre = grad_act * slope_s[t]
        grad_act = follow
        dub_s[t] += fold_rows(grad_pre)
        grad_up = (grad_pre * step_up).astype(BF16)
        back = back + dot_nt(grad_up, up_ref[t])
        dup_s[t] += dot_tn(low, grad_up)
        ddown_s[t] += dot_tn(grad_down, act_s[t])
    dvec_s[1] += fold_rows(back * n1)
    dvec_s[2] += fold_rows(back)
    grad_first = norm_back(back * first_gain, n1, r1)
    dvec_s[0] += fold_rows(grad_first)
    first_ref[...] = grad_first
    grad_proj = (grad_first * step_proj).astype(BF16)
    dproj_s[...] += dot_tn(ctx, grad_proj)
    gctx_ref[...] = dot_nt(grad_proj, proj_ref[...]).astype(BF16)

    @pl.when(at == last)
    def _():
        width = D // parts
        for t in range(parts):
            rows = dproj_s[t * width : (t + 1) * width]
            dproj_ref[t] = spread(rows.astype(BF16), dproj_ref.shape[1:])
            dup_ref[t] = spread(dup_s[t].astype(BF16), dup_ref.shape[1:])
            ddown_ref[t] = spread(ddown_s[t].astype(BF16), ddown_ref.shape[1:])
            dub_ref[t] = jnp.sum(dub_s[t], axis=0, keepdims=True)
        dvec_ref[...] = jnp.sum(dvec_s[...], axis=1)


def feed_forward(sizes, steps, biases, tokens, ctx, out_grad, proj, up, down, vecs):
    count = tokens.shape[0]
    parts, nz = 2 * sizes["x"], sizes["z"]
    wide = FF // parts
    proj, up, down = proj.reshape(D, D), up.reshape(parts, D, wide), down.reshape(parts, wide, D)
    split = (parts, 2, 2, nz, split_rows(D, 4 * nz), wide)
    split_proj = (parts, 2, nz, split_rows(D // parts, 2 * nz), D)
    block = pl.BlockSpec((TB, D), lambda i, *_: (i, 0))

    def whole(*shape):
        return pl.BlockSpec(shape, lambda i, *_: (0,) * len(shape))

    return pl.pallas_call(
        ffn_kernel,
        name="feed_forward",
        grid=(count // TB,),
        in_specs=[
            whole(8, LANES),
            whole(parts, 8, wide),
            block,
            block,
            block,
            whole(D, D),
            whole(parts, D, wide),
            whole(parts, wide, D),
        ]
        + [whole(D)] * 6,
        out_specs=[
            block,
            block,
            block,
            whole(*split_proj),
            whole(*split),
            whole(*split),
            whole(parts, 1, wide),
            whole(6, D),
        ],
        scratch_shapes=[
            pltpu.VMEM((parts, TB, wide), BF16),
            pltpu.VMEM((parts, TB, wide), F32),
            pltpu.VMEM((D, D), F32),
            pltpu.VMEM((parts, D, wide), F32),
            pltpu.VMEM((parts, D, wide), F32),
            pltpu.VMEM((parts, 8, wide), F32),
            pltpu.VMEM((6, 8, D), F32),
        ],
        out_shape=[
            jax.ShapeDtypeStruct((count, D), BF16),
            jax.ShapeDtypeStruct((count, D), F32),
            jax.ShapeDtypeStruct((count, D), BF16),
            jax.ShapeDtypeStruct(split_proj, BF16),
            jax.ShapeDtypeStruct(split, BF16),
            jax.ShapeDtypeStruct(split, BF16),
            jax.ShapeDtypeStruct((parts, 1, wide), F32),
            jax.ShapeDtypeStruct((6, D), F32),
        ],
        compiler_params=pltpu.CompilerParams(vmem_limit_bytes=VMEM_LIMIT),
        cost_estimate=pl.CostEstimate(
            flops=count * 14 * 10**6, bytes_accessed=count * 12000, transcendentals=count * 4096
        ),
    )(steps, biases, tokens, ctx, out_grad, proj, up, down, *vecs)


PLANS = (
    ((0, 2), (2, 6), (6, 9), (9, 12), (12, 15), (15, 19)),
    ((0, 2), (4, 8), (8, 11), (11, 14), (14, 17), (17, 21)),
    ((0, 3), (6, 11), (11, 14), (14, 19), (19, 24), (24, 31)),
    ((0, 3), (8, 13), (13, 16), (16, 20), (20, 26), (26, 34)),
    ((0, 3), (11, 14), (14, 16), (17, 22), (23, 27), (29, 36)),
    ((16, 19), (19, 23), (-1, -1), (24, 29), (29, 33), (33, 38)),
    ((16, 19), (19, 25), (-1, -1), (25, 30), (30, 35), (35, 39)),
    ((16, 19), (22, 28), (-1, -1), (28, 32), (32, 37), (37, 40)),
)
ORDERS = ('xy', 'xy', 'xy', 'xy', 'xy', 'plane', 'plane', 'plane')
THIRDS = 3


def passing(grads, weights, step):
    return jnp.where(weights.astype(F32) == 0.0, 0.0, grads.astype(F32)) / step


def back_kernel(
    sizes,
    step_ref,
    tok_ref,
    ints_ref,
    qkv_ref,
    probs_ref,
    ctx_ref,
    gctx_ref,
    first_ref,
    w_ref,
    dproj_hbm,
    dup_hbm,
    ddown_hbm,
    dub_ref,
    dvec_ref,
    tg_ref,
    dqkv_out,
    dqv_out,
    dproj_out,
    dup_out,
    dub_out,
    ddown_out,
    vec_out,
    grad_s,
    dqkv_s,
    dqv_s,
    part_s,
    *scratch,
):
    step = pl.program_id(0)
    rows = grad_s.shape[0]
    place = Place(sizes)
    parts = 2 * sizes["x"]
    width = D // parts
    step_tokens = step_ref[0:1, 0:1]
    sources = [
        lambda t: dup_hbm.at[t, 0],
        lambda t: ddown_hbm.at[t, 0],
        lambda t: dup_hbm.at[t, 1],
        lambda t: ddown_hbm.at[t, 1],
        lambda t: dproj_hbm.at[t],
    ]
    sources += [lambda t, q=q: part_s.at[t, q] for q in range(THIRDS)]
    streams = []
    for n, source in enumerate(sources):
        refs = scratch[9 * n : 9 * n + 9]
        own = refs[8] if n < 5 else None
        streams.append(Stream(place, ORDERS[n], source, *refs[:8], own))
    sums = Small(place, jnp.add, *scratch[9 * len(sources) :])

    @pl.when(step == 0)
    def _():
        dqkv_s[...] = jnp.zeros_like(dqkv_s)
        dqv_s[...] = jnp.zeros_like(dqv_s)
        corners = [device for n, (_, _, device) in enumerate(place.plane()) if n > 1 and n % 2 == 0]
        place.hello(*corners)
        place.welcome(len(corners))

    def events(now):
        for s, plan in enumerate(PLANS):
            for k, p in enumerate(plan):
                if p[1] == now:
                    streams[s].finish(k)
        for s, plan in enumerate(PLANS):
            for k, p in enumerate(plan):
                if p[0] == now:
                    streams[s].start(k)

    def advance(tick, ticks):
        for now in ticks:
            if any(now in p for plan in PLANS for p in plan):
                pl.when(tick == now)(lambda: events(now))

    def pair_step(p, carry):
        for n in range(16 // (PAIRS * rows)):
            advance((step * PAIRS + p) * (16 // (PAIRS * rows)) + n, range(16))
        at = pl.multiple_of(p * LANES, LANES)
        q_pair = qkv_ref[:, pl.ds(at, LANES)]
        k_pair = qkv_ref[:, pl.ds(D + at, LANES)]
        v_pair = qkv_ref[:, pl.ds(2 * D + at, LANES)]
        g_pair = gctx_ref[:, pl.ds(at, LANES)]
        c_pair = ctx_ref[:, pl.ds(at, LANES)]
        product = (g_pair.astype(F32) * c_pair.astype(F32)).astype(BF16)
        lane = lax.broadcasted_iota(jnp.int32, (8, LANES), 1)
        line = lax.broadcasted_iota(jnp.int32, (8, LANES), 0)
        ones = jnp.where(lane // HEAD_DIM == line, 1.0, 0.0).astype(BF16)
        centre = dot_nt(ones, product)
        outs = []
        for n, (k0, k1, q0, q1) in enumerate(TILES):
            probs = probs_ref[0, pl.ds(2 * p, 2), n]
            gp = dot_nt(stacked(v_pair[k0:k1]), g_pair[q0:q1])
            gs = jnp.concatenate(
                [
                    (probs[h].astype(F32) * (gp[256 * h : 256 * h + 256] - centre[h : h + 1, q0:q1])).astype(BF16)
                    for h in range(2)
                ],
                axis=0,
            )
            d_values = unstacked(dot_nn(probs.reshape(512, 384), g_pair[q0:q1]))
            d_keys = unstacked(dot_nn(gs, q_pair[q0:q1]))
            outs.append(dot_tn(gs, stacked(k_pair[k0:k1])))
            grad_s[step, k0:k1, pl.ds(D + at, LANES)] = (
                d_keys * (step_tokens * step_ref[2:3, 0:1] * (1.0 / LOG2E))
            ).astype(BF16)
            dqv_s[1, :, pl.ds(at, LANES)] += fold_rows(d_values)
            grad_s[step, k0:k1, pl.ds(2 * D + at, LANES)] = (
                d_values * (step_tokens * step_ref[3:4, 0:1])
            ).astype(BF16)
        d_q = both(*outs) * 0.125
        dqv_s[0, :, pl.ds(at, LANES)] += fold_rows(d_q)
        grad_s[step, :, pl.ds(at, LANES)] = (d_q * (step_tokens * step_ref[1:2, 0:1])).astype(BF16)
        return carry

    @pl.when(step < rows)
    def _():
        lax.fori_loop(0, PAIRS, pair_step, 0)
        for i in range(3):
            dqkv_s[i] += dot_tn(grad_s[step, :, i * D : (i + 1) * D], ints_ref[...])

    @pl.when(step == rows)
    def _():
        for t in range(parts):
            piece = jnp.concatenate(
                [dqkv_s[i, t * width : (t + 1) * width] for i in range(3)], axis=0
            )
            part_s[t] = spread(piece.astype(BF16), part_s.shape[1:])
        dqv = jnp.sum(dqv_s[...], axis=1)
        vec = [dvec_ref[r : r + 1] for r in range(6)] + [dqv[0:1], dqv[1:2]]
        dub = jnp.concatenate([dub_ref[t] for t in range(parts)], axis=1)
        vec += [dub[:, r * D : (r + 1) * D] for r in range(4)]
        sums.start(0, tile_rows(vec, 16, D))

    @pl.when(step >= rows)
    def _():
        for n in range(4 // rows):
            advance(16 + (step - rows) * (4 // rows) + n, range(16, 20))

    def vectors():
        total = sums.finish(1)
        for n in range(6):
            vec_out[n] = total[n : n + 1]
        for t in range(parts):

            @pl.when(place.part == t)
            def _():
                dqv_out[...] = total[6:8, t * width : (t + 1) * width]
                wide = FF // parts
                dub_out[...] = total[
                    8 + t * wide // D : 9 + t * wide // D, t * wide % D : t * wide % D + wide
                ]

    @pl.when(step == rows + 1)
    def _():
        sums.start(1, sums.finish(0))

    @pl.when(step >= rows)
    def _():
        grads = grad_s[step - rows]
        total = None
        for i in range(3):
            term = dot_nt(grads[:, i * D : (i + 1) * D], w_ref[i])
            total = term if total is None else total + term
        tg_ref[...] = (first_ref[...] + passing(total, tok_ref[...], step_tokens)).astype(BF16)

    def joined(*group):
        halves = [streams[n].out[...].reshape(D // 2, FF // parts) for n in group]
        return jnp.concatenate(halves, axis=0)

    @pl.when(step == 2 * rows - 1)
    def _():
        ticks = sorted({n for plan in PLANS for p in plan for n in p if n >= 20})
        ended = [max(PLANS[s][5][1] for s in group) for group in ((0, 2), (1, 3), (4,))]
        for now in [19] + ticks:
            if now > 19:
                events(now)
            if now == ticks[len(ticks) // 3]:
                vectors()
            if now == max(19, ended[0]):
                dup_out[...] = joined(0, 2)
            if now == max(19, ended[1]):
                ddown_out[...] = joined(1, 3)
            if now == max(19, ended[2]):
                dproj_out[...] = streams[4].out[...].reshape(-1, D)[:width]
        whole = jnp.concatenate(
            [streams[5 + q].out[...].reshape(-1, D) for q in range(THIRDS)], axis=0
        )
        dqkv_out[...] = whole[: 3 * width]


def deliver_kernel(
    step_ref,
    tg_ref,
    dqkv_ref,
    dqv_ref,
    dproj_ref,
    dup_ref,
    dub_ref,
    ddown_ref,
    vec_ref,
    qkv_ref,
    proj_ref,
    up_ref,
    down_ref,
    tg_out,
    dqkv_out,
    dqv_out,
    dproj_out,
    dup_out,
    dub_out,
    ddown_out,
    *vec_outs,
):
    width = dqkv_out.shape[-1]
    tg_out[...] = tg_ref[...].astype(F32)
    for i in range(3):
        grad = jnp.transpose(dqkv_ref[i * width : (i + 1) * width].astype(F32))
        dqkv_out[i] = passing(grad, qkv_ref[i], step_ref[1 + i : 2 + i, 0:1])
    dproj_out[...] = passing(dproj_ref[...], proj_ref[...], step_ref[4:5, 0:1])
    dup_out[...] = passing(dup_ref[...], up_ref[...], step_ref[5:6, 0:1])
    grad = jnp.transpose(ddown_ref[...].astype(F32))
    ddown_out[...] = passing(grad, down_ref[...], step_ref[6:7, 0:1])
    dqv_out[...] = dqv_ref[...]
    dub_out[...] = dub_ref[0]
    for n, out in enumerate(vec_outs):
        out[...] = vec_ref[n, 0]


def deliver(steps, tokens_grad, dqkv, dqv, dproj, dup, dub, ddown, vec, qkv_w, proj_w, up_w, down_w):
    rows = tokens_grad.shape[0] // SEQ
    width, wide = qkv_w.shape[2], up_w.shape[1]

    def whole(*shape):
        return pl.BlockSpec(shape, lambda i: (0,) * len(shape))

    def down_rows(*shape):
        return pl.BlockSpec((shape[0] // rows,) + shape[1:], lambda i: (i, 0))

    def along(*shape):
        return pl.BlockSpec((shape[0], shape[1] // rows), lambda i: (0, i))

    qkv_block = pl.BlockSpec((3, D // rows, width), lambda i: (0, i, 0))
    outs = [
        (tokens_grad.shape, down_rows(*tokens_grad.shape)),
        (qkv_w.shape, qkv_block),
        ((2, width), whole(2, width)),
        (proj_w.shape, down_rows(*proj_w.shape)),
        (up_w.shape, down_rows(*up_w.shape)),
        ((wide,), whole(wide)),
        (down_w.shape, down_rows(*down_w.shape)),
    ] + [((D,), whole(D))] * 6
    return pl.pallas_call(
        deliver_kernel,
        name="deliver",
        grid=(rows,),
        in_specs=[
            whole(8, LANES),
            down_rows(*tokens_grad.shape),
            along(*dqkv.shape),
            whole(2, width),
            down_rows(*dproj.shape),
            down_rows(*dup.shape),
            whole(1, wide),
            along(*ddown.shape),
            whole(6, 1, D),
            qkv_block,
            down_rows(*proj_w.shape),
            down_rows(*up_w.shape),
            down_rows(*down_w.shape),
        ],
        out_specs=[spec for _, spec in outs],
        out_shape=[jax.ShapeDtypeStruct(shape, F32) for shape, _ in outs],
        compiler_params=pltpu.CompilerParams(vmem_limit_bytes=VMEM_LIMIT),
    )(steps, tokens_grad, dqkv, dqv, dproj, dup, dub, ddown, vec, qkv_w, proj_w, up_w, down_w)


def attend_back(
    sizes, steps, tokens, ints, qkv, probs, ctx, gctx, first, qkv_full, dproj, dup, ddown, dub, dvec
):
    rows = tokens.shape[0] // SEQ
    parts, nz = 2 * sizes["x"], sizes["z"]
    width, wide = D // parts, FF // parts
    part = (parts, THIRDS, 2, nz, split_rows(3 * width, 2 * THIRDS * nz), D)
    pieces = [dup.shape[-2:], ddown.shape[-2:], dup.shape[-2:], ddown.shape[-2:], dproj.shape[-2:]]
    pieces += [part[-2:]] * THIRDS
    early = lambda i: (jnp.minimum(i, rows - 1), 0)
    late = lambda i: (jnp.maximum(i - rows, 0), 0)
    hbm = pl.BlockSpec(memory_space=pl.ANY)

    def whole(*shape):
        return pl.BlockSpec(shape, lambda i: (0,) * len(shape))

    outs = [
        ((3 * width, D), BF16),
        ((2, width), F32),
        ((width, D), BF16),
        ((D, wide), BF16),
        ((1, wide), F32),
        ((D, wide), BF16),
        ((6, 1, D), F32),
    ]
    return pl.pallas_call(
        lambda *refs: back_kernel(sizes, *refs),
        name="attend_back",
        grid=(2 * rows,),
        in_specs=[
            whole(8, LANES),
            pl.BlockSpec((SEQ, D), late),
            pl.BlockSpec((SEQ, D), early),
            pl.BlockSpec((SEQ, 3 * D), early),
            pl.BlockSpec(
                (1, HEADS, 2, 256, 384), lambda i: (jnp.minimum(i, rows - 1), 0, 0, 0, 0)
            ),
            pl.BlockSpec((SEQ, D), early),
            pl.BlockSpec((SEQ, D), early),
            pl.BlockSpec((SEQ, D), late),
            whole(3, D, D),
            hbm,
            hbm,
            hbm,
            whole(*dub.shape),
            whole(*dvec.shape),
        ],
        out_specs=[pl.BlockSpec((SEQ, D), late)] + [whole(*shape) for shape, _ in outs],
        scratch_shapes=[
            pltpu.VMEM((rows, SEQ, 3 * D), BF16),
            pltpu.VMEM((3, D, D), F32),
            pltpu.VMEM((2, 8, D), F32),
            pltpu.VMEM(part, BF16),
        ]
        + sum([stream_scratch(sizes, o, *p) for o, p in zip(ORDERS, pieces)], [])
        + small_scratch(sizes, 16, D),
        out_shape=[jax.ShapeDtypeStruct((rows * SEQ, D), BF16)]
        + [jax.ShapeDtypeStruct(shape, kind) for shape, kind in outs],
        compiler_params=pltpu.CompilerParams(
            vmem_limit_bytes=VMEM_LIMIT, collective_id=1, has_side_effects=True
        ),
        cost_estimate=pl.CostEstimate(
            flops=rows * 6 * 10**9, bytes_accessed=rows * 8 * 10**6, transcendentals=0
        ),
    )(
        steps, tokens, ints, qkv, probs, ctx, gctx, first, qkv_full, dproj, dup, ddown, dub, dvec
    )

def local(
    tokens,
    segment_ids,
    row_lengths,
    qkv_weight,
    qv_bias,
    proj_weight,
    proj_bias,
    first_gain,
    first_shift,
    up_weight,
    up_bias,
    down_weight,
    down_bias,
    second_gain,
    second_shift,
    out_grad,
):
    rows = tokens.shape[0] // SEQ
    sizes = group_sizes(lax.axis_size("tensor"), lax.axis_size("dp"))
    ints, qkv, probs, ctx, qkv_full, steps, biases, proj_full, up_full, down_full = attend(
        sizes,
        row_lengths,
        tokens,
        segment_ids,
        qkv_weight,
        qv_bias,
        proj_weight,
        up_weight,
        down_weight,
        up_bias,
    )
    vecs = (proj_bias, first_gain, first_shift, down_bias, second_gain, second_shift)
    layer_out, grad_first, grad_ctx, dproj, dup, ddown, dub, dvec = feed_forward(
        sizes, steps, biases, tokens, ctx, out_grad, proj_full, up_full, down_full, vecs
    )
    sums = attend_back(
        sizes, steps, tokens, ints, qkv, probs, ctx, grad_ctx, grad_first, qkv_full,
        dproj, dup, ddown, dub, dvec,
    )
    tokens_grad, dqkv, dqv, dproj, dup, dub, ddown, *vec = deliver(
        steps, *sums, qkv_weight, proj_weight, up_weight, down_weight
    )
    return (
        layer_out, tokens_grad, dqkv, dqv, dproj, vec[0], vec[1], vec[2], dup, dub, ddown,
        vec[3], vec[4], vec[5],
    )


def solution(mesh):
    in_specs = (
        P(("dp", "tensor"), None),
        P("dp", None),
        P("dp"),
        P(None, None, "tensor"),
        P(None, "tensor"),
        P("tensor", None),
        P(),
        P(),
        P(),
        P(None, "tensor"),
        P("tensor"),
        P("tensor", None),
        P(),
        P(),
        P(),
        P(("dp", "tensor"), None),
    )
    out_specs = (
        P(("dp", "tensor"), None),
        P(("dp", "tensor"), None),
        P(None, None, "tensor"),
        P(None, "tensor"),
        P("tensor", None),
        P(),
        P(),
        P(),
        P(None, "tensor"),
        P("tensor"),
        P("tensor", None),
        P(),
        P(),
        P(),
    )
    return jax.shard_map(local, mesh=mesh, in_specs=in_specs, out_specs=out_specs, check_vma=False)
```

```python
import jax
import jax.numpy as jnp
from jax import lax
from jax.experimental import pallas as pl
from jax.experimental.pallas import tpu as pltpu
from jax.sharding import PartitionSpec as P

D = 512
HEADS = 8
HEAD_DIM = 64
FF = 2048
SEQ = 512
PAIRS = 4
LANES = 128
LEVELS = 127.0
EPS = 1e-12
MASKED = -1e30
LOG2E = 1.4426950408889634
SCORE_SCALE = 0.125 * LOG2E
VMEM_LIMIT = 58 << 20
F32 = jnp.float32
BF16 = jnp.bfloat16
TILES = ((0, 256, 0, 384), (256, 512, 128, 512))


def rounded(scaled):
    magnitude = jnp.floor(jnp.abs(scaled) + 0.5)
    return jnp.where(scaled < 0.0, -magnitude, magnitude)


def dot_nn(a, b):
    return lax.dot_general(a, b, (((1,), (0,)), ((), ())), preferred_element_type=F32)


def dot_nt(a, b):
    return lax.dot_general(a, b, (((1,), (1,)), ((), ())), preferred_element_type=F32)


def dot_tn(a, b):
    return lax.dot_general(a, b, (((0,), (0,)), ((), ())), preferred_element_type=F32)


def head_mask(head, rows):
    lane = lax.broadcasted_iota(jnp.int32, (rows, LANES), 1)
    return (lane < HEAD_DIM) if head == 0 else (lane >= HEAD_DIM)


def stacked(pair):
    zeros = jnp.zeros_like(pair)
    return jnp.concatenate(
        [jnp.where(head_mask(h, pair.shape[0]), pair, zeros) for h in range(2)], axis=0
    )


def unstacked(blocks):
    rows = blocks.shape[0] // 2
    return jnp.where(head_mask(0, rows), blocks[:rows], blocks[rows:])


def both(left, right):
    return jnp.concatenate([left[:128], left[128:] + right[:256], right[256:]], axis=0)


MESH = pl.DeviceIdType.MESH
MESH_AXES = ("tensor", "dp")


def group_sizes(tensor_size, dp_size):
    return {
        "core": 2,
        "x": tensor_size // 2,
        "y": 2,
        "z": dp_size // 2,
        "tensor": tensor_size,
        "dp": dp_size,
    }


class Place:
    def __init__(self, sizes):
        t, d = lax.axis_index("tensor"), lax.axis_index("dp")
        self.sizes = sizes
        self.part = t
        self.at = {"core": t % 2, "x": t // 2, "y": d % 2, "z": d // 2, "tensor": t, "dp": d}

    def size(self, group):
        return self.sizes[group]

    def peer(self, group, k):
        if group in MESH_AXES:
            at = {axis: lax.axis_index(axis) for axis in MESH_AXES}
            at[group] = (at[group] + k) % self.sizes[group]
            return at[group], (at["dp"], at["tensor"])
        at = dict(self.at)
        at[group] = (at[group] + k) % self.sizes[group]
        return at[group], (at["z"] * 2 + at["y"], at["x"] * 2 + at["core"])

    def greet(self):
        self.hello()
        self.welcome()

    def welcome(self, others=0):
        count = sum(self.sizes[group] - 1 for group in MESH_AXES) + others
        pl.semaphore_wait(pltpu.get_barrier_semaphore(), count)

    def plane(self):
        members = []
        for k in range(self.sizes["x"]):
            for side in range(2):
                if k or side:
                    at = dict(self.at)
                    at["x"] = (at["x"] + k) % self.sizes["x"]
                    at["y"] = (at["y"] + side) % 2
                    device = (at["z"] * 2 + at["y"], at["x"] * 2 + at["core"])
                    members.append((at["x"], at["y"], device))
        return members

    def hello(self, *others):
        barrier = pltpu.get_barrier_semaphore()
        for device in others:
            pl.semaphore_signal(barrier, inc=1, device_id=device, device_id_type=MESH)
        for group in MESH_AXES:
            for k in range(1, self.sizes[group]):
                pl.semaphore_signal(
                    barrier, inc=1, device_id=self.peer(group, k)[1], device_id_type=MESH
                )


class Sems:
    def __init__(self, send, recv):
        self.send, self.recv = send, recv

    def copy(self, at, source, target, device):
        return pltpu.make_async_remote_copy(
            src_ref=source,
            dst_ref=target,
            send_sem=self.send.at[at],
            recv_sem=self.recv.at[at],
            device_id=device,
            device_id_type=MESH,
        )


def exchange(place, group, source, target, sems, base):
    copies = []
    for k in range(1, place.size(group)):
        index, device = place.peer(group, k)
        copies.append(sems.copy(base + k - 1, source(k, index), target(k, index), device))
    return copies


def add(first, *others):
    if len(others) == 1:
        return first + others[0]
    total = first.astype(F32)
    for other in others:
        total = total + other.astype(F32)
    return total.astype(BF16)


class Stream:
    phases = 6

    def __init__(self, place, order, grad, held, got_c, got_1, got_2, got_z, out, send, recv, own):
        self.place, self.order, self.grad, self.held, self.out = place, order, grad, held, out
        self.got_c, self.got_1, self.got_2, self.got_z = got_c, got_1, got_2, got_z
        self.sems, self.own = Sems(send, recv), own

    def local(self):
        if self.own is None:
            return []
        return [
            pltpu.make_async_copy(
                self.grad(2 * i + self.place.at["core"]), self.held.at[i], self.own.at[i]
            )
            for i in range(self.place.size("x"))
        ]

    def copies(self, phase):
        place, at, held = self.place, self.place.at, self.held
        nx, nz = place.size("x"), place.size("z")
        base = [0, nx, 2 * nx, 3 * nx, 3 * nx + nz, 3 * nx + 2 * nz][phase]
        sems = self.sems
        if phase == 0:
            other, device = place.peer("core", 1)
            return [
                sems.copy(i, self.grad(2 * i + other), self.got_c.at[i], device) for i in range(nx)
            ]
        if self.order == "plane":
            if phase == 2:
                return []
            if phase == 1:
                return [
                    sems.copy(base + n, held.at[x, y], self.got_1.at[n], device)
                    for n, (x, y, device) in enumerate(place.plane())
                ]
        if phase == 1 and self.order == "xy":
            return exchange(
                place, "x", lambda k, j: held.at[j], lambda k, j: self.got_1.at[k - 1], sems, base
            )
        if phase == 2 and self.order == "xy":
            return exchange(
                place, "y", lambda k, j: held.at[at["x"], j], lambda k, j: self.got_2.at[0], sems, base
            )
        if phase == 1:
            other, device = place.peer("y", 1)
            return [
                sems.copy(base + i, held.at[i, other], self.got_1.at[i], device) for i in range(nx)
            ]
        if phase == 2:
            return exchange(
                place,
                "x",
                lambda k, j: held.at[j, at["y"]],
                lambda k, j: self.got_2.at[k - 1],
                sems,
                base,
            )
        if phase == 3:
            return exchange(
                place,
                "z",
                lambda k, j: held.at[at["x"], at["y"], j],
                lambda k, j: self.got_z.at[k - 1],
                sems,
                base,
            )
        if phase == 4:
            piece = self.out.at[at["y"], at["z"]]
            return exchange(place, "z", lambda k, j: piece, lambda k, j: piece, sems, base)
        half = self.out.at[at["y"]]
        return exchange(place, "y", lambda k, j: half, lambda k, j: half, sems, base)

    def start(self, phase):
        for copy in self.copies(phase) + (self.local() if phase == 0 else []):
            copy.start()

    def finish(self, phase):
        for copy in self.copies(phase) + (self.local() if phase == 0 else []):
            copy.wait()
        at, held = self.place.at, self.held
        nx, nz = self.place.size("x"), self.place.size("z")
        if phase == 0:
            for i in range(nx):
                for y in range(2):
                    own = held[i, y] if self.own is not None else self.grad(2 * i + at["core"])[y]
                    held[i, y] = add(own, self.got_c[i, y])
        elif phase == 1 and self.order == "xy":
            for y in range(2):
                held[at["x"], y] = add(
                    held[at["x"], y], *[self.got_1[k, y] for k in range(nx - 1)]
                )
        elif phase == 1 and self.order == "plane":
            held[at["x"], at["y"]] = add(
                held[at["x"], at["y"]], *[self.got_1[n] for n in range(2 * nx - 1)]
            )
        elif phase == 1:
            for i in range(nx):
                held[i, at["y"]] = add(held[i, at["y"]], self.got_1[i])
        elif phase == 2 and self.order != "plane":
            count = 1 if self.order == "xy" else nx - 1
            held[at["x"], at["y"]] = add(
                held[at["x"], at["y"]], *[self.got_2[k] for k in range(count)]
            )
        elif phase == 3:
            self.out[at["y"], at["z"]] = add(
                held[at["x"], at["y"], at["z"]], *[self.got_z[k] for k in range(nz - 1)]
            )


def stream_scratch(sizes, order, rows, lanes):
    nx, nz = sizes["x"], sizes["z"]
    count = 3 * nx + 2 * nz + 1
    piece = (nz, rows, lanes)
    first = {"xy": (nx - 1, 2), "yx": (nx,), "plane": (2 * nx - 1,)}[order]
    second = (nx - 1,) if order == "yx" else (1,)
    return [
        pltpu.VMEM((nx, 2) + piece, BF16),
        pltpu.VMEM((nx, 2) + piece, BF16),
        pltpu.VMEM(first + piece, BF16),
        pltpu.VMEM(second + piece, BF16),
        pltpu.VMEM((nz - 1,) + piece[1:], BF16),
        pltpu.VMEM((2,) + piece, BF16),
        pltpu.SemaphoreType.DMA((count,)),
        pltpu.SemaphoreType.DMA((count,)),
        pltpu.SemaphoreType.DMA((nx,)),
    ]


class Small:
    def __init__(self, place, combine, slots, send, recv):
        self.place, self.combine, self.slots, self.sems = place, combine, slots, Sems(send, recv)

    def offsets(self, phase):
        sizes = [self.place.size(g) for g in MESH_AXES]
        return sum(sizes[:phase]), sum(sizes[:phase]) - phase

    def copies(self, phase):
        slot, sem = self.offsets(phase)
        return exchange(
            self.place,
            MESH_AXES[phase],
            lambda k, j: self.slots.at[slot],
            lambda k, j: self.slots.at[slot + k],
            self.sems,
            sem,
        )

    def start(self, phase, values):
        self.slots[self.offsets(phase)[0]] = values
        for copy in self.copies(phase):
            copy.start()

    def finish(self, phase):
        for copy in self.copies(phase):
            copy.wait()
        slot = self.offsets(phase)[0]
        count, me = self.place.size(MESH_AXES[phase]), self.place.at[MESH_AXES[phase]]
        total = None
        for member in range(count):
            term = self.slots[slot + (me + count - member) % count]
            total = term if total is None else self.combine(total, term)
        return total


def small_scratch(sizes, rows, lanes):
    total = sum(sizes[g] for g in MESH_AXES)
    return [
        pltpu.VMEM((total, rows, lanes), F32),
        pltpu.SemaphoreType.DMA((total - 2,)),
        pltpu.SemaphoreType.DMA((total - 2,)),
    ]


class Gather:
    def __init__(self, place, own, every, send, recv, keep):
        self.place, self.own, self.every, self.sems, self.keep = place, own, every, Sems(send, recv), keep

    def far(self):
        place = self.place
        mine = self.every.at[place.part]
        return exchange(place, "x", lambda k, j: self.own, lambda k, j: mine, self.sems, 0)

    def near(self, step):
        place = self.place
        nx = place.size("x")
        device = place.peer("core", 1)[1]
        if step == 0:
            return self.sems.copy(nx - 1, self.own, self.every.at[place.part], device)
        chip = (place.at["x"] + nx - step) % nx
        block = self.every.at[chip * 2 + place.at["core"]]
        return self.sems.copy(nx - 1 + step, block, block, device)

    def mine(self):
        return pltpu.make_async_copy(self.own, self.every.at[self.place.part], self.keep.at[0])

    def start(self):
        for copy in self.far():
            copy.start()
        self.near(0).start()
        self.mine().start()

    def forward(self):
        for copy in self.far():
            copy.wait()
        for k in range(1, self.place.size("x")):
            self.near(k).start()

    def finish(self):
        for k in range(self.place.size("x")):
            self.near(k).wait()
        self.mine().wait()


class SplitGather(Gather):
    def far(self):
        place, y = self.place, self.place.at["y"]
        mine, half = self.every.at[place.part, y], self.own.at[y]
        return exchange(place, "x", lambda k, j: half, lambda k, j: mine, self.sems, 0)

    def side(self):
        place = self.place
        nx, y = place.size("x"), place.at["y"]
        copies = []
        for k in range(1, nx):
            chip = (place.at["x"] + nx - k) % nx
            half = self.every.at[chip * 2 + place.at["core"], y]
            copies.append(self.sems.copy(2 * nx - 2 + k, half, half, place.peer("y", 1)[1]))
        return copies

    def cross(self):
        for copy in self.far():
            copy.wait()
        for copy in self.side():
            copy.start()

    def forward(self):
        for copy in self.side():
            copy.wait()
        for k in range(1, self.place.size("x")):
            self.near(k).start()


def gather_scratch(sizes):
    count = 3 * sizes["x"] - 2
    return [
        pltpu.SemaphoreType.DMA((count,)),
        pltpu.SemaphoreType.DMA((count,)),
        pltpu.SemaphoreType.DMA((1,)),
    ]


def split_rows(rows, pieces):
    return -(-rows // (pieces * 8)) * 8


def spread(values, shape):
    count = 1
    for size in shape[:-1]:
        count *= size
    if count > values.shape[0]:
        zeros = jnp.zeros((count - values.shape[0], values.shape[1]), values.dtype)
        values = jnp.concatenate([values, zeros], axis=0)
    return values.reshape(shape)


def tile_rows(rows, height, lanes):
    filled = [r if r.shape[1] == lanes else jnp.concatenate([r, jnp.zeros((1, lanes - r.shape[1]), F32)], axis=1) for r in rows]
    at = lax.broadcasted_iota(jnp.int32, (height, lanes), 0)
    total = jnp.zeros((height, lanes), F32)
    for n, r in enumerate(filled):
        total = jnp.where(at == n, r, total)
    return total


def top(values):
    peak = jnp.max(jnp.abs(values.astype(F32)), axis=0, keepdims=True)
    return jnp.max(peak, axis=1, keepdims=True)


def attend_kernel(
    sizes,
    len_ref,
    tok_hbm,
    seg_ref,
    qkv_hbm,
    qvb_sh,
    proj_hbm,
    up_hbm,
    down_hbm,
    ub_sh,
    ints_ref,
    qkv_ref,
    probs_ref,
    ctx_ref,
    w_ref,
    step_ref,
    bias_ref,
    proj_all,
    up_all,
    down_all,
    mask_s,
    ints_s,
    tok_ref,
    qkv_sh,
    proj_sh,
    up_sh,
    down_sh,
    load_s,
    raw_all,
    bias_all,
    bias_own,
    proj_own,
    up_own,
    down_own,
    *sems,
):
    row = pl.program_id(0)
    last = pl.num_programs(0) - 1
    place = Place(sizes)
    parts = 2 * sizes["x"]
    width = D // parts
    early = [
        Gather(place, own, every, *sems[3 * n : 3 * n + 3])
        for n, (own, every) in enumerate(((qkv_sh, raw_all), (bias_own, bias_all)))
    ]
    late = [
        SplitGather(place, own, every, *sems[6 + 3 * n : 9 + 3 * n])
        for n, (own, every) in enumerate(
            ((proj_own, proj_all), (up_own, up_all), (down_own, down_all))
        )
    ]
    peaks = Small(place, jnp.maximum, *sems[15:18])

    @pl.when(row == 0)
    def _():
        place.hello()
        loads = [
            pltpu.make_async_copy(source, target, load_s.at[n])
            for n, (source, target) in enumerate(
                (
                    (tok_hbm, tok_ref),
                    (qkv_hbm, qkv_sh),
                    (proj_hbm, proj_sh),
                    (up_hbm, up_sh),
                    (down_hbm, down_sh),
                )
            )
        ]
        for load in loads:
            load.start()
        for load in loads:
            load.wait()
        bias_own[...] = tile_rows(
            [ub_sh[...].astype(F32)[None], qvb_sh[0:1].astype(F32), qvb_sh[1:2].astype(F32)],
            8,
            ub_sh.shape[0],
        )
        tops = [top(tok_ref[...])] + [top(qkv_sh[i]) for i in range(3)]
        tops += [top(proj_sh[...]), top(up_sh[...]), top(down_sh[...])]
        total = tile_rows([jnp.broadcast_to(t, (1, LANES)) for t in tops], 8, LANES)
        place.welcome()
        peaks.start(0, total)
        for gather in early:
            gather.start()
        peaks.start(1, peaks.finish(0))
        step_ref[...] = peaks.finish(1) / LEVELS
        for own, shard, r in ((proj_own, proj_sh, 4), (up_own, up_sh, 5), (down_own, down_sh, 6)):
            for h in range(2):
                half = shard[h * own.shape[1] : (h + 1) * own.shape[1]]
                own[h] = rounded(half.astype(F32) / step_ref[r : r + 1, 0:1]).astype(BF16)
        for r in range(ints_s.shape[0] // SEQ):
            rows = slice(r * SEQ, (r + 1) * SEQ)
            ints_s[rows] = rounded(tok_ref[rows].astype(F32) / step_ref[0:1, 0:1]).astype(BF16)
            if r == 0:
                for gather in early:
                    gather.forward()
        for gather in early:
            gather.finish()
        for gather in late:
            gather.start()
        bias_ref[...] = bias_all[...]
        for t in range(parts):
            for i in range(3):
                w_ref[i, :, t * width : (t + 1) * width] = rounded(
                    raw_all[t, i].astype(F32) / step_ref[1 + i : 2 + i, 0:1]
                ).astype(BF16)

    for n, gather in enumerate(late):
        pl.when(row == jnp.minimum((1, 1, 2)[n], last))(gather.cross)

    @pl.when(row == last)
    def _():
        for gather in late:
            gather.forward()

    step_tokens = step_ref[0:1, 0:1]
    ints = ints_s[pl.ds(pl.multiple_of(row * SEQ, SEQ), SEQ), :]
    ints_ref[...] = ints
    biases = [
        jnp.concatenate([bias_all[t, r : r + 1, :width] for t in range(parts)], axis=1)
        for r in (1, 2)
    ]
    for i in range(3):
        raw = dot_nn(ints, w_ref[i]) * (step_tokens * step_ref[1 + i : 2 + i, 0:1])
        if i == 0:
            raw = (raw + biases[0]) * SCORE_SCALE
        if i == 2:
            raw = raw + biases[1]
        qkv_ref[:, i * D : (i + 1) * D] = raw.astype(BF16)
    here = place.part * pl.num_programs(0) + row
    seg_q = seg_ref[pl.ds(here, 1), :].astype(F32)
    length = len_ref[here]
    spot = lax.broadcasted_iota(jnp.int32, (8, SEQ), 1)
    seg_k = jnp.where(spot < length, jnp.broadcast_to(seg_q, (8, SEQ)), -1.0)
    seg_k = jnp.transpose(seg_k)[:, 0:1]
    for n, (k0, k1, q0, q1) in enumerate(TILES):
        keys = lax.broadcasted_iota(jnp.int32, (k1 - k0, q1 - q0), 0) + k0
        queries = lax.broadcasted_iota(jnp.int32, (k1 - k0, q1 - q0), 1) + q0
        allowed = (seg_k[k0:k1] == seg_q[:, q0:q1]) | (keys == queries)
        mask_s[n] = jnp.where(allowed, 0.0, MASKED)

    def pair_step(p, carry):
        at = pl.multiple_of(p * LANES, LANES)
        q_pair = qkv_ref[:, pl.ds(at, LANES)]
        k_pair = qkv_ref[:, pl.ds(D + at, LANES)]
        v_pair = qkv_ref[:, pl.ds(2 * D + at, LANES)]
        scores = []
        for n, (k0, k1, q0, q1) in enumerate(TILES):
            s = dot_nt(stacked(k_pair[k0:k1]), q_pair[q0:q1])
            scores.append(s.reshape(2, 256, 384) + mask_s[n])
        peak = [jnp.max(s, axis=1, keepdims=True) for s in scores]
        high = jnp.concatenate(
            [
                peak[0][:, :, :128],
                jnp.maximum(peak[0][:, :, 128:], peak[1][:, :, :256]),
                peak[1][:, :, 256:],
            ],
            axis=2,
        )
        weights = [jnp.exp2(s - high[:, :, q0:q1]) for s, (k0, k1, q0, q1) in zip(scores, TILES)]
        sums = [jnp.sum(w, axis=1, keepdims=True) for w in weights]
        totals = jnp.concatenate(
            [
                sums[0][:, :, :128],
                sums[0][:, :, 128:] + sums[1][:, :, :256],
                sums[1][:, :, 256:],
            ],
            axis=2,
        )
        inverse = 1.0 / totals
        outs = []
        for n, (k0, k1, q0, q1) in enumerate(TILES):
            probs = (weights[n] * inverse[:, :, q0:q1]).astype(BF16)
            probs_ref[0, pl.ds(2 * p, 2), n] = probs
            outs.append(dot_tn(probs.reshape(512, 384), stacked(v_pair[k0:k1])))
        ctx_ref[:, pl.ds(at, LANES)] = both(*outs).astype(BF16)
        return carry

    lax.fori_loop(0, PAIRS, pair_step, 0)

    @pl.when(row == last)
    def _():
        for gather in late:
            gather.finish()


def attend(sizes, lens, tokens, segments, qkv_w, qv_bias, proj_w, up_w, down_w, up_b):
    rows = tokens.shape[0] // SEQ
    parts = 2 * sizes["x"]
    hbm = pl.BlockSpec(memory_space=pl.ANY)
    halves = [(2, w.shape[0] // 2, w.shape[1]) for w in (proj_w, up_w, down_w)]

    def whole(*shape):
        return pl.BlockSpec(shape, lambda i, *_: (0,) * len(shape))

    return pl.pallas_call(
        lambda *refs: attend_kernel(sizes, *refs),
        name="attend",
        grid_spec=pltpu.PrefetchScalarGridSpec(
            num_scalar_prefetch=0,
            grid=(rows,),
            in_specs=[
                pl.BlockSpec(memory_space=pltpu.SMEM),
                hbm,
                whole(*segments.shape),
                hbm,
                whole(*qv_bias.shape),
                hbm,
                hbm,
                hbm,
                whole(*up_b.shape),
            ],
            out_specs=[
                pl.BlockSpec((SEQ, D), lambda i, *_: (i, 0)),
                pl.BlockSpec((SEQ, 3 * D), lambda i, *_: (i, 0)),
                pl.BlockSpec((1, HEADS, 2, 256, 384), lambda i, *_: (i, 0, 0, 0, 0)),
                pl.BlockSpec((SEQ, D), lambda i, *_: (i, 0)),
                whole(3, D, D),
                whole(8, LANES),
                whole(parts, 8, up_b.shape[0]),
                hbm,
                hbm,
                hbm,
            ],
            scratch_shapes=[
                pltpu.VMEM((2, 256, 384), F32),
                pltpu.VMEM(tokens.shape, BF16),
                pltpu.VMEM(tokens.shape, BF16),
                pltpu.VMEM(qkv_w.shape, BF16),
                pltpu.VMEM(proj_w.shape, BF16),
                pltpu.VMEM(up_w.shape, BF16),
                pltpu.VMEM(down_w.shape, BF16),
                pltpu.SemaphoreType.DMA((5,)),
                pltpu.VMEM((parts,) + qkv_w.shape, BF16),
                pltpu.VMEM((parts, 8, up_b.shape[0]), F32),
                pltpu.VMEM((8, up_b.shape[0]), F32),
            ]
            + [pltpu.VMEM(shape, BF16) for shape in halves]
            + sum([gather_scratch(sizes) for _ in range(5)], [])
            + small_scratch(sizes, 8, LANES),
        ),
        out_shape=[
            jax.ShapeDtypeStruct((rows * SEQ, D), BF16),
            jax.ShapeDtypeStruct((rows * SEQ, 3 * D), BF16),
            jax.ShapeDtypeStruct((rows, HEADS, 2, 256, 384), BF16),
            jax.ShapeDtypeStruct((rows * SEQ, D), BF16),
            jax.ShapeDtypeStruct((3, D, D), BF16),
            jax.ShapeDtypeStruct((8, LANES), F32),
            jax.ShapeDtypeStruct((parts, 8, up_b.shape[0]), F32),
        ]
        + [jax.ShapeDtypeStruct((parts,) + shape, BF16) for shape in halves],
        compiler_params=pltpu.CompilerParams(
            vmem_limit_bytes=VMEM_LIMIT, collective_id=0, has_side_effects=True
        ),
        cost_estimate=pl.CostEstimate(
            flops=rows * 3 * 10**9, bytes_accessed=rows * 6 * 10**6, transcendentals=rows * 2 * 10**6
        ),
    )(lens, tokens, segments, qkv_w, qv_bias, proj_w, up_w, down_w, up_b)

INV_SQRT_2PI = 0.3989422804014327


def gelu_pair(pre):
    cdf = 0.5 + 0.5 * lax.erf(pre * 0.7071067811865476)
    bell = jnp.exp2(pre * pre * (-0.5 * LOG2E))
    return pre * cdf, cdf + (pre * INV_SQRT_2PI) * bell


def fold_rows(values):
    total = values[0:8]
    for r in range(8, values.shape[0], 8):
        total = total + values[r : r + 8]
    return total


def normalize(values):
    centred = values - jnp.mean(values, axis=-1, keepdims=True)
    inverse = lax.rsqrt(jnp.mean(centred * centred, axis=-1, keepdims=True) + EPS)
    return centred * inverse, inverse


def norm_back(scaled, standard, inverse):
    return inverse * (
        scaled
        - jnp.mean(scaled, axis=-1, keepdims=True)
        - standard * jnp.mean(scaled * standard, axis=-1, keepdims=True)
    )


TB = 512


def ffn_kernel(
    step_ref,
    bias_ref,
    tok_ref,
    ctx_ref,
    og_ref,
    proj_ref,
    up_hbm,
    down_hbm,
    pb_ref,
    fg_ref,
    fs_ref,
    db_ref,
    sg_ref,
    ss_ref,
    out_ref,
    first_ref,
    gctx_ref,
    dproj_ref,
    dup_ref,
    ddown_ref,
    dub_ref,
    dvec_ref,
    act_s,
    slope_s,
    dproj_s,
    dup_s,
    ddown_s,
    dub_s,
    dvec_s,
    up_ref,
    down_ref,
    load_s,
):
    at = pl.program_id(0)
    last = pl.num_programs(0) - 1
    parts = up_ref.shape[0]
    step_proj, step_up, step_down = [step_ref[r : r + 1, 0:1] for r in (4, 5, 6)]

    loads = [
        pltpu.make_async_copy(up_hbm, up_ref, load_s.at[0]),
        pltpu.make_async_copy(down_hbm, down_ref, load_s.at[1]),
    ]

    @pl.when(at == 0)
    def _():
        for load in loads:
            load.start()
        dproj_s[...] = jnp.zeros_like(dproj_s)
        dup_s[...] = jnp.zeros_like(dup_s)
        ddown_s[...] = jnp.zeros_like(ddown_s)
        dub_s[...] = jnp.zeros_like(dub_s)
        dvec_s[...] = jnp.zeros_like(dvec_s)

    proj_bias, first_gain, first_shift, down_bias, second_gain, second_shift = [
        r[...].astype(F32)[None] for r in (pb_ref, fg_ref, fs_ref, db_ref, sg_ref, ss_ref)
    ]
    ctx = ctx_ref[...]
    first_in = tok_ref[...].astype(F32) + (dot_nn(ctx, proj_ref[...]) * step_proj + proj_bias)
    n1, r1 = normalize(first_in)
    normed = n1 * first_gain + first_shift
    low = normed.astype(BF16)

    @pl.when(at == 0)
    def _():
        for load in loads:
            load.wait()

    branch = None
    pre = dot_nn(low, up_ref[0])
    for t in range(parts):
        follow = dot_nn(low, up_ref[t + 1]) if t + 1 < parts else None
        act, slope = gelu_pair(pre * step_up + bias_ref[t, 0:1])
        pre = follow
        act = act.astype(BF16)
        act_s[t] = act
        slope_s[t] = slope
        if t:
            term = dot_nn(held, down_ref[t - 1])
            branch = term if branch is None else branch + term
        held = act
    branch = branch + dot_nn(held, down_ref[parts - 1])
    second_in = normed + (branch * step_down + down_bias)
    n2, r2 = normalize(second_in)
    out_ref[...] = (n2 * second_gain + second_shift).astype(BF16)
    og = og_ref[...].astype(F32)
    grad_second = norm_back(og * second_gain, n2, r2)
    dvec_s[4] += fold_rows(og * n2)
    dvec_s[5] += fold_rows(og)
    dvec_s[3] += fold_rows(grad_second)
    grad_down = (grad_second * step_down).astype(BF16)
    back = grad_second
    grad_act = dot_nt(grad_down, down_ref[0])
    for t in range(parts):
        follow = dot_nt(grad_down, down_ref[t + 1]) if t + 1 < parts else None
        grad_pre = grad_act * slope_s[t]
        grad_act = follow
        dub_s[t] += fold_rows(grad_pre)
        grad_up = (grad_pre * step_up).astype(BF16)
        back = back + dot_nt(grad_up, up_ref[t])
        dup_s[t] += dot_tn(low, grad_up)
        ddown_s[t] += dot_tn(grad_down, act_s[t])
    dvec_s[1] += fold_rows(back * n1)
    dvec_s[2] += fold_rows(back)
    grad_first = norm_back(back * first_gain, n1, r1)
    dvec_s[0] += fold_rows(grad_first)
    first_ref[...] = grad_first
    grad_proj = (grad_first * step_proj).astype(BF16)
    dproj_s[...] += dot_tn(ctx, grad_proj)
    gctx_ref[...] = dot_nt(grad_proj, proj_ref[...]).astype(BF16)

    @pl.when(at == last)
    def _():
        width = D // parts
        for t in range(parts):
            rows = dproj_s[t * width : (t + 1) * width]
            dproj_ref[t] = spread(rows.astype(BF16), dproj_ref.shape[1:])
            dup_ref[t] = spread(dup_s[t].astype(BF16), dup_ref.shape[1:])
            ddown_ref[t] = spread(ddown_s[t].astype(BF16), ddown_ref.shape[1:])
            dub_ref[t] = jnp.sum(dub_s[t], axis=0, keepdims=True)
        dvec_ref[...] = jnp.sum(dvec_s[...], axis=1)


def feed_forward(sizes, steps, biases, tokens, ctx, out_grad, proj, up, down, vecs):
    count = tokens.shape[0]
    parts, nz = 2 * sizes["x"], sizes["z"]
    wide = FF // parts
    proj, up, down = proj.reshape(D, D), up.reshape(parts, D, wide), down.reshape(parts, wide, D)
    split = (parts, 2, 2, nz, split_rows(D, 4 * nz), wide)
    split_proj = (parts, 2, nz, split_rows(D // parts, 2 * nz), D)
    block = pl.BlockSpec((TB, D), lambda i, *_: (i, 0))

    def whole(*shape):
        return pl.BlockSpec(shape, lambda i, *_: (0,) * len(shape))

    return pl.pallas_call(
        ffn_kernel,
        name="feed_forward",
        grid=(count // TB,),
        in_specs=[
            whole(8, LANES),
            whole(parts, 8, wide),
            block,
            block,
            block,
            whole(D, D),
            pl.BlockSpec(memory_space=pl.ANY),
            pl.BlockSpec(memory_space=pl.ANY),
        ]
        + [whole(D)] * 6,
        out_specs=[
            block,
            block,
            block,
            whole(*split_proj),
            whole(*split),
            whole(*split),
            whole(parts, 1, wide),
            whole(6, D),
        ],
        scratch_shapes=[
            pltpu.VMEM((parts, TB, wide), BF16),
            pltpu.VMEM((parts, TB, wide), F32),
            pltpu.VMEM((D, D), F32),
            pltpu.VMEM((parts, D, wide), F32),
            pltpu.VMEM((parts, D, wide), F32),
            pltpu.VMEM((parts, 8, wide), F32),
            pltpu.VMEM((6, 8, D), F32),
            pltpu.VMEM((parts, D, wide), BF16),
            pltpu.VMEM((parts, wide, D), BF16),
            pltpu.SemaphoreType.DMA((2,)),
        ],
        out_shape=[
            jax.ShapeDtypeStruct((count, D), BF16),
            jax.ShapeDtypeStruct((count, D), F32),
            jax.ShapeDtypeStruct((count, D), BF16),
            jax.ShapeDtypeStruct(split_proj, BF16),
            jax.ShapeDtypeStruct(split, BF16),
            jax.ShapeDtypeStruct(split, BF16),
            jax.ShapeDtypeStruct((parts, 1, wide), F32),
            jax.ShapeDtypeStruct((6, D), F32),
        ],
        compiler_params=pltpu.CompilerParams(vmem_limit_bytes=VMEM_LIMIT),
        cost_estimate=pl.CostEstimate(
            flops=count * 14 * 10**6, bytes_accessed=count * 12000, transcendentals=count * 4096
        ),
    )(steps, biases, tokens, ctx, out_grad, proj, up, down, *vecs)


PLANS = (
    ((0, 2), (2, 6), (6, 9), (9, 12), (12, 15), (15, 19)),
    ((0, 2), (4, 8), (8, 11), (11, 14), (14, 17), (17, 21)),
    ((0, 3), (6, 11), (11, 14), (14, 19), (19, 24), (24, 31)),
    ((0, 3), (8, 13), (13, 16), (16, 20), (20, 26), (26, 34)),
    ((0, 3), (11, 14), (14, 16), (17, 22), (23, 27), (29, 36)),
    ((16, 19), (19, 23), (-1, -1), (24, 29), (29, 33), (33, 38)),
    ((16, 19), (19, 25), (-1, -1), (25, 30), (30, 35), (35, 39)),
    ((16, 19), (22, 28), (-1, -1), (28, 32), (32, 37), (37, 40)),
)
ORDERS = ('xy', 'xy', 'xy', 'xy', 'xy', 'plane', 'plane', 'plane')
THIRDS = 3


def passing(grads, weights, step):
    return jnp.where(weights.astype(F32) == 0.0, 0.0, grads.astype(F32)) / step


def back_kernel(
    sizes,
    step_ref,
    tok_ref,
    ints_ref,
    qkv_ref,
    probs_ref,
    ctx_ref,
    gctx_ref,
    first_ref,
    w_hbm,
    dproj_hbm,
    dup_hbm,
    ddown_hbm,
    dub_ref,
    dvec_ref,
    tg_ref,
    dqkv_out,
    dqv_out,
    dproj_out,
    dup_out,
    dub_out,
    ddown_out,
    vec_out,
    grad_s,
    dqkv_s,
    dqv_s,
    part_s,
    w_ref,
    load_s,
    *scratch,
):
    step = pl.program_id(0)
    rows = grad_s.shape[0]
    place = Place(sizes)
    parts = 2 * sizes["x"]
    width = D // parts
    step_tokens = step_ref[0:1, 0:1]
    sources = [
        lambda t: dup_hbm.at[t, 0],
        lambda t: ddown_hbm.at[t, 0],
        lambda t: dup_hbm.at[t, 1],
        lambda t: ddown_hbm.at[t, 1],
        lambda t: dproj_hbm.at[t],
    ]
    sources += [lambda t, q=q: part_s.at[t, q] for q in range(THIRDS)]
    streams = []
    for n, source in enumerate(sources):
        refs = scratch[9 * n : 9 * n + 9]
        own = refs[8] if n < 5 else None
        streams.append(Stream(place, ORDERS[n], source, *refs[:8], own))
    sums = Small(place, jnp.add, *scratch[9 * len(sources) :])

    load = pltpu.make_async_copy(w_hbm, w_ref, load_s.at[0])

    @pl.when(step == 0)
    def _():
        load.start()
        dqkv_s[...] = jnp.zeros_like(dqkv_s)
        dqv_s[...] = jnp.zeros_like(dqv_s)
        corners = [device for n, (_, _, device) in enumerate(place.plane()) if n > 1 and n % 2 == 0]
        place.hello(*corners)
        place.welcome(len(corners))

    def events(now):
        for s, plan in enumerate(PLANS):
            for k, p in enumerate(plan):
                if p[1] == now:
                    streams[s].finish(k)
        for s, plan in enumerate(PLANS):
            for k, p in enumerate(plan):
                if p[0] == now:
                    streams[s].start(k)

    def advance(tick, ticks):
        for now in ticks:
            if any(now in p for plan in PLANS for p in plan):
                pl.when(tick == now)(lambda: events(now))

    def pair_step(p, carry):
        for n in range(16 // (PAIRS * rows)):
            advance((step * PAIRS + p) * (16 // (PAIRS * rows)) + n, range(16))
        at = pl.multiple_of(p * LANES, LANES)
        q_pair = qkv_ref[:, pl.ds(at, LANES)]
        k_pair = qkv_ref[:, pl.ds(D + at, LANES)]
        v_pair = qkv_ref[:, pl.ds(2 * D + at, LANES)]
        g_pair = gctx_ref[:, pl.ds(at, LANES)]
        c_pair = ctx_ref[:, pl.ds(at, LANES)]
        product = (g_pair.astype(F32) * c_pair.astype(F32)).astype(BF16)
        lane = lax.broadcasted_iota(jnp.int32, (8, LANES), 1)
        line = lax.broadcasted_iota(jnp.int32, (8, LANES), 0)
        ones = jnp.where(lane // HEAD_DIM == line, 1.0, 0.0).astype(BF16)
        centre = dot_nt(ones, product)
        outs = []
        for n, (k0, k1, q0, q1) in enumerate(TILES):
            probs = probs_ref[0, pl.ds(2 * p, 2), n]
            gp = dot_nt(stacked(v_pair[k0:k1]), g_pair[q0:q1])
            gs = jnp.concatenate(
                [
                    (probs[h].astype(F32) * (gp[256 * h : 256 * h + 256] - centre[h : h + 1, q0:q1])).astype(BF16)
                    for h in range(2)
                ],
                axis=0,
            )
            d_values = unstacked(dot_nn(probs.reshape(512, 384), g_pair[q0:q1]))
            d_keys = unstacked(dot_nn(gs, q_pair[q0:q1]))
            outs.append(dot_tn(gs, stacked(k_pair[k0:k1])))
            grad_s[step, k0:k1, pl.ds(D + at, LANES)] = (
                d_keys * (step_tokens * step_ref[2:3, 0:1] * (1.0 / LOG2E))
            ).astype(BF16)
            dqv_s[1, :, pl.ds(at, LANES)] += fold_rows(d_values)
            grad_s[step, k0:k1, pl.ds(2 * D + at, LANES)] = (
                d_values * (step_tokens * step_ref[3:4, 0:1])
            ).astype(BF16)
        d_q = both(*outs) * 0.125
        dqv_s[0, :, pl.ds(at, LANES)] += fold_rows(d_q)
        grad_s[step, :, pl.ds(at, LANES)] = (d_q * (step_tokens * step_ref[1:2, 0:1])).astype(BF16)
        return carry

    @pl.when(step < rows)
    def _():
        lax.fori_loop(0, PAIRS, pair_step, 0)
        for i in range(3):
            dqkv_s[i] += dot_tn(grad_s[step, :, i * D : (i + 1) * D], ints_ref[...])

    pl.when(step == rows)(load.wait)

    @pl.when(step == rows)
    def _():
        for t in range(parts):
            piece = jnp.concatenate(
                [dqkv_s[i, t * width : (t + 1) * width] for i in range(3)], axis=0
            )
            part_s[t] = spread(piece.astype(BF16), part_s.shape[1:])
        dqv = jnp.sum(dqv_s[...], axis=1)
        vec = [dvec_ref[r : r + 1] for r in range(6)] + [dqv[0:1], dqv[1:2]]
        dub = jnp.concatenate([dub_ref[t] for t in range(parts)], axis=1)
        vec += [dub[:, r * D : (r + 1) * D] for r in range(4)]
        sums.start(0, tile_rows(vec, 16, D))

    @pl.when(step >= rows)
    def _():
        for n in range(4 // rows):
            advance(16 + (step - rows) * (4 // rows) + n, range(16, 20))

    def vectors():
        total = sums.finish(1)
        for n in range(6):
            vec_out[n] = total[n : n + 1]
        for t in range(parts):

            @pl.when(place.part == t)
            def _():
                dqv_out[...] = total[6:8, t * width : (t + 1) * width]
                wide = FF // parts
                dub_out[...] = total[
                    8 + t * wide // D : 9 + t * wide // D, t * wide % D : t * wide % D + wide
                ]

    @pl.when(step == rows + 1)
    def _():
        sums.start(1, sums.finish(0))

    @pl.when(step >= rows)
    def _():
        grads = grad_s[step - rows]
        total = None
        for i in range(3):
            term = dot_nt(grads[:, i * D : (i + 1) * D], w_ref[i])
            total = term if total is None else total + term
        tg_ref[...] = (first_ref[...] + passing(total, tok_ref[...], step_tokens)).astype(BF16)

    def joined(*group):
        halves = [streams[n].out[...].reshape(D // 2, FF // parts) for n in group]
        return jnp.concatenate(halves, axis=0)

    @pl.when(step == 2 * rows - 1)
    def _():
        ticks = sorted({n for plan in PLANS for p in plan for n in p if n >= 20})
        ended = [max(PLANS[s][5][1] for s in group) for group in ((0, 2), (1, 3), (4,))]
        for now in [19] + ticks:
            if now > 19:
                events(now)
            if now == ticks[len(ticks) // 3]:
                vectors()
            if now == max(19, ended[0]):
                dup_out[...] = joined(0, 2)
            if now == max(19, ended[1]):
                ddown_out[...] = joined(1, 3)
            if now == max(19, ended[2]):
                dproj_out[...] = streams[4].out[...].reshape(-1, D)[:width]
        whole = jnp.concatenate(
            [streams[5 + q].out[...].reshape(-1, D) for q in range(THIRDS)], axis=0
        )
        dqkv_out[...] = whole[: 3 * width]


def deliver_kernel(
    step_ref,
    tg_ref,
    dqkv_ref,
    dqv_ref,
    dproj_ref,
    dup_ref,
    dub_ref,
    ddown_ref,
    vec_ref,
    qkv_ref,
    proj_ref,
    up_ref,
    down_ref,
    tg_out,
    dqkv_out,
    dqv_out,
    dproj_out,
    dup_out,
    dub_out,
    ddown_out,
    *vec_outs,
):
    width = dqkv_out.shape[-1]
    tg_out[...] = tg_ref[...].astype(F32)
    for i in range(3):
        grad = jnp.transpose(dqkv_ref[i * width : (i + 1) * width].astype(F32))
        dqkv_out[i] = passing(grad, qkv_ref[i], step_ref[1 + i : 2 + i, 0:1])
    dproj_out[...] = passing(dproj_ref[...], proj_ref[...], step_ref[4:5, 0:1])
    dup_out[...] = passing(dup_ref[...], up_ref[...], step_ref[5:6, 0:1])
    grad = jnp.transpose(ddown_ref[...].astype(F32))
    ddown_out[...] = passing(grad, down_ref[...], step_ref[6:7, 0:1])
    dqv_out[...] = dqv_ref[...]
    dub_out[...] = dub_ref[0]
    for n, out in enumerate(vec_outs):
        out[...] = vec_ref[n, 0]


def deliver(steps, tokens_grad, dqkv, dqv, dproj, dup, dub, ddown, vec, qkv_w, proj_w, up_w, down_w):
    rows = tokens_grad.shape[0] // SEQ
    width, wide = qkv_w.shape[2], up_w.shape[1]

    def whole(*shape):
        return pl.BlockSpec(shape, lambda i: (0,) * len(shape))

    def down_rows(*shape):
        return pl.BlockSpec((shape[0] // rows,) + shape[1:], lambda i: (i, 0))

    def along(*shape):
        return pl.BlockSpec((shape[0], shape[1] // rows), lambda i: (0, i))

    qkv_block = pl.BlockSpec((3, D // rows, width), lambda i: (0, i, 0))
    outs = [
        (tokens_grad.shape, down_rows(*tokens_grad.shape)),
        (qkv_w.shape, qkv_block),
        ((2, width), whole(2, width)),
        (proj_w.shape, down_rows(*proj_w.shape)),
        (up_w.shape, down_rows(*up_w.shape)),
        ((wide,), whole(wide)),
        (down_w.shape, down_rows(*down_w.shape)),
    ] + [((D,), whole(D))] * 6
    return pl.pallas_call(
        deliver_kernel,
        name="deliver",
        grid=(rows,),
        in_specs=[
            whole(8, LANES),
            down_rows(*tokens_grad.shape),
            along(*dqkv.shape),
            whole(2, width),
            down_rows(*dproj.shape),
            down_rows(*dup.shape),
            whole(1, wide),
            along(*ddown.shape),
            whole(6, 1, D),
            qkv_block,
            down_rows(*proj_w.shape),
            down_rows(*up_w.shape),
            down_rows(*down_w.shape),
        ],
        out_specs=[spec for _, spec in outs],
        out_shape=[jax.ShapeDtypeStruct(shape, F32) for shape, _ in outs],
        compiler_params=pltpu.CompilerParams(vmem_limit_bytes=VMEM_LIMIT),
    )(steps, tokens_grad, dqkv, dqv, dproj, dup, dub, ddown, vec, qkv_w, proj_w, up_w, down_w)


def attend_back(
    sizes, steps, tokens, ints, qkv, probs, ctx, gctx, first, qkv_full, dproj, dup, ddown, dub, dvec
):
    rows = tokens.shape[0] // SEQ
    parts, nz = 2 * sizes["x"], sizes["z"]
    width, wide = D // parts, FF // parts
    part = (parts, THIRDS, 2, nz, split_rows(3 * width, 2 * THIRDS * nz), D)
    pieces = [dup.shape[-2:], ddown.shape[-2:], dup.shape[-2:], ddown.shape[-2:], dproj.shape[-2:]]
    pieces += [part[-2:]] * THIRDS
    early = lambda i: (jnp.minimum(i, rows - 1), 0)
    late = lambda i: (jnp.maximum(i - rows, 0), 0)
    hbm = pl.BlockSpec(memory_space=pl.ANY)

    def whole(*shape):
        return pl.BlockSpec(shape, lambda i: (0,) * len(shape))

    outs = [
        ((3 * width, D), BF16),
        ((2, width), F32),
        ((width, D), BF16),
        ((D, wide), BF16),
        ((1, wide), F32),
        ((D, wide), BF16),
        ((6, 1, D), F32),
    ]
    return pl.pallas_call(
        lambda *refs: back_kernel(sizes, *refs),
        name="attend_back",
        grid=(2 * rows,),
        in_specs=[
            whole(8, LANES),
            pl.BlockSpec((SEQ, D), late),
            pl.BlockSpec((SEQ, D), early),
            pl.BlockSpec((SEQ, 3 * D), early),
            pl.BlockSpec(
                (1, HEADS, 2, 256, 384), lambda i: (jnp.minimum(i, rows - 1), 0, 0, 0, 0)
            ),
            pl.BlockSpec((SEQ, D), early),
            pl.BlockSpec((SEQ, D), early),
            pl.BlockSpec((SEQ, D), late),
            hbm,
            hbm,
            hbm,
            hbm,
            whole(*dub.shape),
            whole(*dvec.shape),
        ],
        out_specs=[pl.BlockSpec((SEQ, D), late)] + [whole(*shape) for shape, _ in outs],
        scratch_shapes=[
            pltpu.VMEM((rows, SEQ, 3 * D), BF16),
            pltpu.VMEM((3, D, D), F32),
            pltpu.VMEM((2, 8, D), F32),
            pltpu.VMEM(part, BF16),
            pltpu.VMEM((3, D, D), BF16),
            pltpu.SemaphoreType.DMA((1,)),
        ]
        + sum([stream_scratch(sizes, o, *p) for o, p in zip(ORDERS, pieces)], [])
        + small_scratch(sizes, 16, D),
        out_shape=[jax.ShapeDtypeStruct((rows * SEQ, D), BF16)]
        + [jax.ShapeDtypeStruct(shape, kind) for shape, kind in outs],
        compiler_params=pltpu.CompilerParams(
            vmem_limit_bytes=VMEM_LIMIT, collective_id=1, has_side_effects=True
        ),
        cost_estimate=pl.CostEstimate(
            flops=rows * 6 * 10**9, bytes_accessed=rows * 8 * 10**6, transcendentals=0
        ),
    )(
        steps, tokens, ints, qkv, probs, ctx, gctx, first, qkv_full, dproj, dup, ddown, dub, dvec
    )

def local(
    tokens,
    segment_ids,
    row_lengths,
    qkv_weight,
    qv_bias,
    proj_weight,
    proj_bias,
    first_gain,
    first_shift,
    up_weight,
    up_bias,
    down_weight,
    down_bias,
    second_gain,
    second_shift,
    out_grad,
):
    rows = tokens.shape[0] // SEQ
    sizes = group_sizes(lax.axis_size("tensor"), lax.axis_size("dp"))
    ints, qkv, probs, ctx, qkv_full, steps, biases, proj_full, up_full, down_full = attend(
        sizes,
        row_lengths,
        tokens,
        segment_ids,
        qkv_weight,
        qv_bias,
        proj_weight,
        up_weight,
        down_weight,
        up_bias,
    )
    vecs = (proj_bias, first_gain, first_shift, down_bias, second_gain, second_shift)
    layer_out, grad_first, grad_ctx, dproj, dup, ddown, dub, dvec = feed_forward(
        sizes, steps, biases, tokens, ctx, out_grad, proj_full, up_full, down_full, vecs
    )
    sums = attend_back(
        sizes, steps, tokens, ints, qkv, probs, ctx, grad_ctx, grad_first, qkv_full,
        dproj, dup, ddown, dub, dvec,
    )
    tokens_grad, dqkv, dqv, dproj, dup, dub, ddown, *vec = deliver(
        steps, *sums, qkv_weight, proj_weight, up_weight, down_weight
    )
    return (
        layer_out, tokens_grad, dqkv, dqv, dproj, vec[0], vec[1], vec[2], dup, dub, ddown,
        vec[3], vec[4], vec[5],
    )


def solution(mesh):
    in_specs = (
        P(("dp", "tensor"), None),
        P("dp", None),
        P("dp"),
        P(None, None, "tensor"),
        P(None, "tensor"),
        P("tensor", None),
        P(),
        P(),
        P(),
        P(None, "tensor"),
        P("tensor"),
        P("tensor", None),
        P(),
        P(),
        P(),
        P(("dp", "tensor"), None),
    )
    out_specs = (
        P(("dp", "tensor"), None),
        P(("dp", "tensor"), None),
        P(None, None, "tensor"),
        P(None, "tensor"),
        P("tensor", None),
        P(),
        P(),
        P(),
        P(None, "tensor"),
        P("tensor"),
        P("tensor", None),
        P(),
        P(),
        P(),
    )
    return jax.shard_map(local, mesh=mesh, in_specs=in_specs, out_specs=out_specs, check_vma=False)
```

```python
import jax
import jax.numpy as jnp
from jax import lax
from jax.experimental import pallas as pl
from jax.experimental.pallas import tpu as pltpu
from jax.sharding import PartitionSpec as P

D = 512
HEADS = 8
HEAD_DIM = 64
FF = 2048
SEQ = 512
PAIRS = 4
LANES = 128
LEVELS = 127.0
EPS = 1e-12
MASKED = -1e30
LOG2E = 1.4426950408889634
SCORE_SCALE = 0.125 * LOG2E
VMEM_LIMIT = 58 << 20
F32 = jnp.float32
BF16 = jnp.bfloat16
TILES = ((0, 256, 0, 384), (256, 512, 128, 512))


def rounded(scaled):
    magnitude = jnp.floor(jnp.abs(scaled) + 0.5)
    return jnp.where(scaled < 0.0, -magnitude, magnitude)


def dot_nn(a, b):
    return lax.dot_general(a, b, (((1,), (0,)), ((), ())), preferred_element_type=F32)


def dot_nt(a, b):
    return lax.dot_general(a, b, (((1,), (1,)), ((), ())), preferred_element_type=F32)


def dot_tn(a, b):
    return lax.dot_general(a, b, (((0,), (0,)), ((), ())), preferred_element_type=F32)


def head_mask(head, rows):
    lane = lax.broadcasted_iota(jnp.int32, (rows, LANES), 1)
    return (lane < HEAD_DIM) if head == 0 else (lane >= HEAD_DIM)


def stacked(pair):
    zeros = jnp.zeros_like(pair)
    return jnp.concatenate(
        [jnp.where(head_mask(h, pair.shape[0]), pair, zeros) for h in range(2)], axis=0
    )


def unstacked(blocks):
    rows = blocks.shape[0] // 2
    return jnp.where(head_mask(0, rows), blocks[:rows], blocks[rows:])


def both(left, right):
    return jnp.concatenate([left[:128], left[128:] + right[:256], right[256:]], axis=0)


MESH = pl.DeviceIdType.MESH
MESH_AXES = ("tensor", "dp")


def group_sizes(tensor_size, dp_size):
    return {
        "core": 2,
        "x": tensor_size // 2,
        "y": 2,
        "z": dp_size // 2,
        "tensor": tensor_size,
        "dp": dp_size,
    }


class Place:
    def __init__(self, sizes):
        t, d = lax.axis_index("tensor"), lax.axis_index("dp")
        self.sizes = sizes
        self.part = t
        self.at = {"core": t % 2, "x": t // 2, "y": d % 2, "z": d // 2, "tensor": t, "dp": d}

    def size(self, group):
        return self.sizes[group]

    def peer(self, group, k):
        if group in MESH_AXES:
            at = {axis: lax.axis_index(axis) for axis in MESH_AXES}
            at[group] = (at[group] + k) % self.sizes[group]
            return at[group], (at["dp"], at["tensor"])
        at = dict(self.at)
        at[group] = (at[group] + k) % self.sizes[group]
        return at[group], (at["z"] * 2 + at["y"], at["x"] * 2 + at["core"])

    def greet(self):
        self.hello()
        self.welcome()

    def welcome(self, others=0):
        count = sum(self.sizes[group] - 1 for group in MESH_AXES) + others
        pl.semaphore_wait(pltpu.get_barrier_semaphore(), count)

    def plane(self):
        members = []
        for k in range(self.sizes["x"]):
            for side in range(2):
                if k or side:
                    at = dict(self.at)
                    at["x"] = (at["x"] + k) % self.sizes["x"]
                    at["y"] = (at["y"] + side) % 2
                    device = (at["z"] * 2 + at["y"], at["x"] * 2 + at["core"])
                    members.append((at["x"], at["y"], device))
        return members

    def hello(self, *others):
        barrier = pltpu.get_barrier_semaphore()
        for device in others:
            pl.semaphore_signal(barrier, inc=1, device_id=device, device_id_type=MESH)
        for group in MESH_AXES:
            for k in range(1, self.sizes[group]):
                pl.semaphore_signal(
                    barrier, inc=1, device_id=self.peer(group, k)[1], device_id_type=MESH
                )


class Sems:
    def __init__(self, send, recv):
        self.send, self.recv = send, recv

    def copy(self, at, source, target, device):
        return pltpu.make_async_remote_copy(
            src_ref=source,
            dst_ref=target,
            send_sem=self.send.at[at],
            recv_sem=self.recv.at[at],
            device_id=device,
            device_id_type=MESH,
        )


def exchange(place, group, source, target, sems, base):
    copies = []
    for k in range(1, place.size(group)):
        index, device = place.peer(group, k)
        copies.append(sems.copy(base + k - 1, source(k, index), target(k, index), device))
    return copies


def add(first, *others):
    if len(others) == 1:
        return first + others[0]
    total = first.astype(F32)
    for other in others:
        total = total + other.astype(F32)
    return total.astype(BF16)


class Stream:
    phases = 6

    def __init__(self, place, order, grad, held, got_c, got_1, got_2, got_z, out, send, recv, own):
        self.place, self.order, self.grad, self.held, self.out = place, order, grad, held, out
        self.got_c, self.got_1, self.got_2, self.got_z = got_c, got_1, got_2, got_z
        self.sems, self.own = Sems(send, recv), own

    def local(self):
        if self.own is None:
            return []
        return [
            pltpu.make_async_copy(
                self.grad(2 * i + self.place.at["core"]), self.held.at[i], self.own.at[i]
            )
            for i in range(self.place.size("x"))
        ]

    def copies(self, phase):
        place, at, held = self.place, self.place.at, self.held
        nx, nz = place.size("x"), place.size("z")
        base = [0, nx, 2 * nx, 3 * nx, 3 * nx + nz, 3 * nx + 2 * nz][phase]
        sems = self.sems
        if phase == 0:
            other, device = place.peer("core", 1)
            return [
                sems.copy(i, self.grad(2 * i + other), self.got_c.at[i], device) for i in range(nx)
            ]
        if self.order == "plane":
            if phase == 2:
                return []
            if phase == 1:
                return [
                    sems.copy(base + n, held.at[x, y], self.got_1.at[n], device)
                    for n, (x, y, device) in enumerate(place.plane())
                ]
        if phase == 1 and self.order == "xy":
            return exchange(
                place, "x", lambda k, j: held.at[j], lambda k, j: self.got_1.at[k - 1], sems, base
            )
        if phase == 2 and self.order == "xy":
            return exchange(
                place, "y", lambda k, j: held.at[at["x"], j], lambda k, j: self.got_2.at[0], sems, base
            )
        if phase == 1:
            other, device = place.peer("y", 1)
            return [
                sems.copy(base + i, held.at[i, other], self.got_1.at[i], device) for i in range(nx)
            ]
        if phase == 2:
            return exchange(
                place,
                "x",
                lambda k, j: held.at[j, at["y"]],
                lambda k, j: self.got_2.at[k - 1],
                sems,
                base,
            )
        if phase == 3:
            return exchange(
                place,
                "z",
                lambda k, j: held.at[at["x"], at["y"], j],
                lambda k, j: self.got_z.at[k - 1],
                sems,
                base,
            )
        if phase == 4:
            piece = self.out.at[at["y"], at["z"]]
            return exchange(place, "z", lambda k, j: piece, lambda k, j: piece, sems, base)
        half = self.out.at[at["y"]]
        return exchange(place, "y", lambda k, j: half, lambda k, j: half, sems, base)

    def start(self, phase):
        for copy in self.copies(phase) + (self.local() if phase == 0 else []):
            copy.start()

    def finish(self, phase):
        for copy in self.copies(phase) + (self.local() if phase == 0 else []):
            copy.wait()
        at, held = self.place.at, self.held
        nx, nz = self.place.size("x"), self.place.size("z")
        if phase == 0:
            for i in range(nx):
                for y in range(2):
                    own = held[i, y] if self.own is not None else self.grad(2 * i + at["core"])[y]
                    held[i, y] = add(own, self.got_c[i, y])
        elif phase == 1 and self.order == "xy":
            for y in range(2):
                held[at["x"], y] = add(
                    held[at["x"], y], *[self.got_1[k, y] for k in range(nx - 1)]
                )
        elif phase == 1 and self.order == "plane":
            held[at["x"], at["y"]] = add(
                held[at["x"], at["y"]], *[self.got_1[n] for n in range(2 * nx - 1)]
            )
        elif phase == 1:
            for i in range(nx):
                held[i, at["y"]] = add(held[i, at["y"]], self.got_1[i])
        elif phase == 2 and self.order != "plane":
            count = 1 if self.order == "xy" else nx - 1
            held[at["x"], at["y"]] = add(
                held[at["x"], at["y"]], *[self.got_2[k] for k in range(count)]
            )
        elif phase == 3:
            self.out[at["y"], at["z"]] = add(
                held[at["x"], at["y"], at["z"]], *[self.got_z[k] for k in range(nz - 1)]
            )


def stream_scratch(sizes, order, rows, lanes):
    nx, nz = sizes["x"], sizes["z"]
    count = 3 * nx + 2 * nz + 1
    piece = (nz, rows, lanes)
    first = {"xy": (nx - 1, 2), "yx": (nx,), "plane": (2 * nx - 1,)}[order]
    second = (nx - 1,) if order == "yx" else (1,)
    return [
        pltpu.VMEM((nx, 2) + piece, BF16),
        pltpu.VMEM((nx, 2) + piece, BF16),
        pltpu.VMEM(first + piece, BF16),
        pltpu.VMEM(second + piece, BF16),
        pltpu.VMEM((nz - 1,) + piece[1:], BF16),
        pltpu.VMEM((2,) + piece, BF16),
        pltpu.SemaphoreType.DMA((count,)),
        pltpu.SemaphoreType.DMA((count,)),
        pltpu.SemaphoreType.DMA((nx,)),
    ]


class Small:
    def __init__(self, place, combine, slots, send, recv):
        self.place, self.combine, self.slots, self.sems = place, combine, slots, Sems(send, recv)

    def offsets(self, phase):
        sizes = [self.place.size(g) for g in MESH_AXES]
        return sum(sizes[:phase]), sum(sizes[:phase]) - phase

    def copies(self, phase):
        slot, sem = self.offsets(phase)
        return exchange(
            self.place,
            MESH_AXES[phase],
            lambda k, j: self.slots.at[slot],
            lambda k, j: self.slots.at[slot + k],
            self.sems,
            sem,
        )

    def start(self, phase, values):
        self.slots[self.offsets(phase)[0]] = values
        for copy in self.copies(phase):
            copy.start()

    def finish(self, phase):
        for copy in self.copies(phase):
            copy.wait()
        slot = self.offsets(phase)[0]
        count, me = self.place.size(MESH_AXES[phase]), self.place.at[MESH_AXES[phase]]
        total = None
        for member in range(count):
            term = self.slots[slot + (me + count - member) % count]
            total = term if total is None else self.combine(total, term)
        return total


def small_scratch(sizes, rows, lanes):
    total = sum(sizes[g] for g in MESH_AXES)
    return [
        pltpu.VMEM((total, rows, lanes), F32),
        pltpu.SemaphoreType.DMA((total - 2,)),
        pltpu.SemaphoreType.DMA((total - 2,)),
    ]


class Gather:
    def __init__(self, place, own, every, send, recv, keep):
        self.place, self.own, self.every, self.sems, self.keep = place, own, every, Sems(send, recv), keep

    def far(self):
        place = self.place
        mine = self.every.at[place.part]
        return exchange(place, "x", lambda k, j: self.own, lambda k, j: mine, self.sems, 0)

    def near(self, step):
        place = self.place
        nx = place.size("x")
        device = place.peer("core", 1)[1]
        if step == 0:
            return self.sems.copy(nx - 1, self.own, self.every.at[place.part], device)
        chip = (place.at["x"] + nx - step) % nx
        block = self.every.at[chip * 2 + place.at["core"]]
        return self.sems.copy(nx - 1 + step, block, block, device)

    def mine(self):
        return pltpu.make_async_copy(self.own, self.every.at[self.place.part], self.keep.at[0])

    def start(self):
        for copy in self.far():
            copy.start()
        self.near(0).start()
        self.mine().start()

    def forward(self):
        for copy in self.far():
            copy.wait()
        for k in range(1, self.place.size("x")):
            self.near(k).start()

    def finish(self):
        for k in range(self.place.size("x")):
            self.near(k).wait()
        self.mine().wait()


class SplitGather(Gather):
    def far(self):
        place, y = self.place, self.place.at["y"]
        mine, half = self.every.at[place.part, y], self.own.at[y]
        return exchange(place, "x", lambda k, j: half, lambda k, j: mine, self.sems, 0)

    def side(self):
        place = self.place
        nx, y = place.size("x"), place.at["y"]
        copies = []
        for k in range(1, nx):
            chip = (place.at["x"] + nx - k) % nx
            half = self.every.at[chip * 2 + place.at["core"], y]
            copies.append(self.sems.copy(2 * nx - 2 + k, half, half, place.peer("y", 1)[1]))
        return copies

    def cross(self):
        for copy in self.far():
            copy.wait()
        for copy in self.side():
            copy.start()

    def forward(self):
        for copy in self.side():
            copy.wait()
        for k in range(1, self.place.size("x")):
            self.near(k).start()


def gather_scratch(sizes):
    count = 3 * sizes["x"] - 2
    return [
        pltpu.SemaphoreType.DMA((count,)),
        pltpu.SemaphoreType.DMA((count,)),
        pltpu.SemaphoreType.DMA((1,)),
    ]


def split_rows(rows, pieces):
    return -(-rows // (pieces * 8)) * 8


def spread(values, shape):
    count = 1
    for size in shape[:-1]:
        count *= size
    if count > values.shape[0]:
        zeros = jnp.zeros((count - values.shape[0], values.shape[1]), values.dtype)
        values = jnp.concatenate([values, zeros], axis=0)
    return values.reshape(shape)


def tile_rows(rows, height, lanes):
    filled = [r if r.shape[1] == lanes else jnp.concatenate([r, jnp.zeros((1, lanes - r.shape[1]), F32)], axis=1) for r in rows]
    at = lax.broadcasted_iota(jnp.int32, (height, lanes), 0)
    total = jnp.zeros((height, lanes), F32)
    for n, r in enumerate(filled):
        total = jnp.where(at == n, r, total)
    return total


def top(values):
    peak = jnp.max(jnp.abs(values.astype(F32)), axis=0, keepdims=True)
    return jnp.max(peak, axis=1, keepdims=True)


def attend_kernel(
    sizes,
    len_ref,
    tok_hbm,
    seg_ref,
    qkv_hbm,
    qvb_sh,
    proj_hbm,
    up_hbm,
    down_hbm,
    ub_sh,
    ints_ref,
    qkv_ref,
    probs_ref,
    ctx_ref,
    w_ref,
    step_ref,
    bias_ref,
    proj_all,
    up_all,
    down_all,
    mask_s,
    ints_s,
    tok_ref,
    qkv_sh,
    proj_sh,
    up_sh,
    down_sh,
    load_s,
    raw_all,
    bias_all,
    bias_own,
    proj_own,
    up_own,
    down_own,
    *sems,
):
    row = pl.program_id(0)
    last = pl.num_programs(0) - 1
    place = Place(sizes)
    parts = 2 * sizes["x"]
    width = D // parts
    early = [
        Gather(place, own, every, *sems[3 * n : 3 * n + 3])
        for n, (own, every) in enumerate(((qkv_sh, raw_all), (bias_own, bias_all)))
    ]
    late = [
        SplitGather(place, own, every, *sems[6 + 3 * n : 9 + 3 * n])
        for n, (own, every) in enumerate(
            ((proj_own, proj_all), (up_own, up_all), (down_own, down_all))
        )
    ]
    peaks = Small(place, jnp.maximum, *sems[15:18])

    @pl.when(row == 0)
    def _():
        place.hello()
        loads = [
            pltpu.make_async_copy(source, target, load_s.at[n])
            for n, (source, target) in enumerate(
                (
                    (tok_hbm, tok_ref),
                    (qkv_hbm, qkv_sh),
                    (proj_hbm, proj_sh),
                    (up_hbm, up_sh),
                    (down_hbm, down_sh),
                )
            )
        ]
        for load in loads:
            load.start()
        for load in loads:
            load.wait()
        bias_own[...] = tile_rows(
            [ub_sh[...].astype(F32)[None], qvb_sh[0:1].astype(F32), qvb_sh[1:2].astype(F32)],
            8,
            ub_sh.shape[0],
        )
        tops = [top(tok_ref[...])] + [top(qkv_sh[i]) for i in range(3)]
        tops += [top(proj_sh[...]), top(up_sh[...]), top(down_sh[...])]
        total = tile_rows([jnp.broadcast_to(t, (1, LANES)) for t in tops], 8, LANES)
        place.welcome()
        peaks.start(0, total)
        for gather in early:
            gather.start()
        peaks.start(1, peaks.finish(0))
        step_ref[...] = peaks.finish(1) / LEVELS
        for own, shard, r in ((proj_own, proj_sh, 4), (up_own, up_sh, 5), (down_own, down_sh, 6)):
            for h in range(2):
                half = shard[h * own.shape[1] : (h + 1) * own.shape[1]]
                own[h] = rounded(half.astype(F32) / step_ref[r : r + 1, 0:1]).astype(BF16)
        for r in range(ints_s.shape[0] // SEQ):
            rows = slice(r * SEQ, (r + 1) * SEQ)
            ints_s[rows] = rounded(tok_ref[rows].astype(F32) / step_ref[0:1, 0:1]).astype(BF16)
            if r == 0:
                for gather in early:
                    gather.forward()
        for gather in early:
            gather.finish()
        for gather in late:
            gather.start()
        bias_ref[...] = bias_all[...]
        for t in range(parts):
            for i in range(3):
                w_ref[i, :, t * width : (t + 1) * width] = rounded(
                    raw_all[t, i].astype(F32) / step_ref[1 + i : 2 + i, 0:1]
                ).astype(BF16)

    for n, gather in enumerate(late):
        pl.when(row == jnp.minimum((1, 1, 2)[n], last))(gather.cross)

    @pl.when(row == last)
    def _():
        for gather in late:
            gather.forward()

    step_tokens = step_ref[0:1, 0:1]
    ints = ints_s[pl.ds(pl.multiple_of(row * SEQ, SEQ), SEQ), :]
    ints_ref[...] = ints
    biases = [
        jnp.concatenate([bias_all[t, r : r + 1, :width] for t in range(parts)], axis=1)
        for r in (1, 2)
    ]
    for i in range(3):
        raw = dot_nn(ints, w_ref[i]) * (step_tokens * step_ref[1 + i : 2 + i, 0:1])
        if i == 0:
            raw = (raw + biases[0]) * SCORE_SCALE
        if i == 2:
            raw = raw + biases[1]
        qkv_ref[:, i * D : (i + 1) * D] = raw.astype(BF16)
    here = place.part * pl.num_programs(0) + row
    seg_q = seg_ref[pl.ds(here, 1), :].astype(F32)
    length = len_ref[here]
    spot = lax.broadcasted_iota(jnp.int32, (8, SEQ), 1)
    seg_k = jnp.where(spot < length, jnp.broadcast_to(seg_q, (8, SEQ)), -1.0)
    seg_k = jnp.transpose(seg_k)[:, 0:1]
    for n, (k0, k1, q0, q1) in enumerate(TILES):
        keys = lax.broadcasted_iota(jnp.int32, (k1 - k0, q1 - q0), 0) + k0
        queries = lax.broadcasted_iota(jnp.int32, (k1 - k0, q1 - q0), 1) + q0
        allowed = (seg_k[k0:k1] == seg_q[:, q0:q1]) | (keys == queries)
        mask_s[n] = jnp.where(allowed, 0.0, MASKED)

    def pair_step(p, carry):
        at = pl.multiple_of(p * LANES, LANES)
        q_pair = qkv_ref[:, pl.ds(at, LANES)]
        k_pair = qkv_ref[:, pl.ds(D + at, LANES)]
        v_pair = qkv_ref[:, pl.ds(2 * D + at, LANES)]
        scores = []
        for n, (k0, k1, q0, q1) in enumerate(TILES):
            s = dot_nt(stacked(k_pair[k0:k1]), q_pair[q0:q1])
            scores.append(s.reshape(2, 256, 384) + mask_s[n])
        peak = [jnp.max(s, axis=1, keepdims=True) for s in scores]
        high = jnp.concatenate(
            [
                peak[0][:, :, :128],
                jnp.maximum(peak[0][:, :, 128:], peak[1][:, :, :256]),
                peak[1][:, :, 256:],
            ],
            axis=2,
        )
        weights = [jnp.exp2(s - high[:, :, q0:q1]) for s, (k0, k1, q0, q1) in zip(scores, TILES)]
        sums = [jnp.sum(w, axis=1, keepdims=True) for w in weights]
        totals = jnp.concatenate(
            [
                sums[0][:, :, :128],
                sums[0][:, :, 128:] + sums[1][:, :, :256],
                sums[1][:, :, 256:],
            ],
            axis=2,
        )
        inverse = 1.0 / totals
        outs = []
        for n, (k0, k1, q0, q1) in enumerate(TILES):
            probs = (weights[n] * inverse[:, :, q0:q1]).astype(BF16)
            probs_ref[0, pl.ds(2 * p, 2), n] = probs
            outs.append(dot_tn(probs.reshape(512, 384), stacked(v_pair[k0:k1])))
        ctx_ref[:, pl.ds(at, LANES)] = both(*outs).astype(BF16)
        return carry

    lax.fori_loop(0, PAIRS, pair_step, 0)

    @pl.when(row == last)
    def _():
        for gather in late:
            gather.finish()


def attend(sizes, lens, tokens, segments, qkv_w, qv_bias, proj_w, up_w, down_w, up_b):
    rows = tokens.shape[0] // SEQ
    parts = 2 * sizes["x"]
    hbm = pl.BlockSpec(memory_space=pl.ANY)
    halves = [(2, w.shape[0] // 2, w.shape[1]) for w in (proj_w, up_w, down_w)]

    def whole(*shape):
        return pl.BlockSpec(shape, lambda i, *_: (0,) * len(shape))

    return pl.pallas_call(
        lambda *refs: attend_kernel(sizes, *refs),
        name="attend",
        grid_spec=pltpu.PrefetchScalarGridSpec(
            num_scalar_prefetch=0,
            grid=(rows,),
            in_specs=[
                pl.BlockSpec(memory_space=pltpu.SMEM),
                hbm,
                whole(*segments.shape),
                hbm,
                whole(*qv_bias.shape),
                hbm,
                hbm,
                hbm,
                whole(*up_b.shape),
            ],
            out_specs=[
                pl.BlockSpec((SEQ, D), lambda i, *_: (i, 0)),
                pl.BlockSpec((SEQ, 3 * D), lambda i, *_: (i, 0)),
                pl.BlockSpec((1, HEADS, 2, 256, 384), lambda i, *_: (i, 0, 0, 0, 0)),
                pl.BlockSpec((SEQ, D), lambda i, *_: (i, 0)),
                whole(3, D, D),
                whole(8, LANES),
                whole(parts, 8, up_b.shape[0]),
                hbm,
                hbm,
                hbm,
            ],
            scratch_shapes=[
                pltpu.VMEM((2, 256, 384), F32),
                pltpu.VMEM(tokens.shape, BF16),
                pltpu.VMEM(tokens.shape, BF16),
                pltpu.VMEM(qkv_w.shape, BF16),
                pltpu.VMEM(proj_w.shape, BF16),
                pltpu.VMEM(up_w.shape, BF16),
                pltpu.VMEM(down_w.shape, BF16),
                pltpu.SemaphoreType.DMA((5,)),
                pltpu.VMEM((parts,) + qkv_w.shape, BF16),
                pltpu.VMEM((parts, 8, up_b.shape[0]), F32),
                pltpu.VMEM((8, up_b.shape[0]), F32),
            ]
            + [pltpu.VMEM(shape, BF16) for shape in halves]
            + sum([gather_scratch(sizes) for _ in range(5)], [])
            + small_scratch(sizes, 8, LANES),
        ),
        out_shape=[
            jax.ShapeDtypeStruct((rows * SEQ, D), BF16),
            jax.ShapeDtypeStruct((rows * SEQ, 3 * D), BF16),
            jax.ShapeDtypeStruct((rows, HEADS, 2, 256, 384), BF16),
            jax.ShapeDtypeStruct((rows * SEQ, D), BF16),
            jax.ShapeDtypeStruct((3, D, D), BF16),
            jax.ShapeDtypeStruct((8, LANES), F32),
            jax.ShapeDtypeStruct((parts, 8, up_b.shape[0]), F32),
        ]
        + [jax.ShapeDtypeStruct((parts,) + shape, BF16) for shape in halves],
        compiler_params=pltpu.CompilerParams(
            vmem_limit_bytes=VMEM_LIMIT, collective_id=0, has_side_effects=True
        ),
        cost_estimate=pl.CostEstimate(
            flops=rows * 3 * 10**9, bytes_accessed=rows * 6 * 10**6, transcendentals=rows * 2 * 10**6
        ),
    )(lens, tokens, segments, qkv_w, qv_bias, proj_w, up_w, down_w, up_b)

INV_SQRT_2PI = 0.3989422804014327


def gelu_pair(pre):
    cdf = 0.5 + 0.5 * lax.erf(pre * 0.7071067811865476)
    bell = jnp.exp2(pre * pre * (-0.5 * LOG2E))
    return pre * cdf, cdf + (pre * INV_SQRT_2PI) * bell


def fold_rows(values):
    total = values[0:8]
    for r in range(8, values.shape[0], 8):
        total = total + values[r : r + 8]
    return total


def normalize(values):
    centred = values - jnp.mean(values, axis=-1, keepdims=True)
    inverse = lax.rsqrt(jnp.mean(centred * centred, axis=-1, keepdims=True) + EPS)
    return centred * inverse, inverse


def norm_back(scaled, standard, inverse):
    return inverse * (
        scaled
        - jnp.mean(scaled, axis=-1, keepdims=True)
        - standard * jnp.mean(scaled * standard, axis=-1, keepdims=True)
    )


TB = 512


def ffn_kernel(
    step_ref,
    bias_ref,
    tok_ref,
    ctx_ref,
    og_ref,
    proj_ref,
    up_hbm,
    down_hbm,
    pb_ref,
    fg_ref,
    fs_ref,
    db_ref,
    sg_ref,
    ss_ref,
    out_ref,
    first_ref,
    gctx_ref,
    dproj_ref,
    dup_ref,
    ddown_ref,
    dub_ref,
    dvec_ref,
    act_s,
    slope_s,
    dproj_s,
    dup_s,
    ddown_s,
    dub_s,
    dvec_s,
    up_ref,
    down_ref,
    load_s,
):
    at = pl.program_id(0)
    last = pl.num_programs(0) - 1
    parts = up_ref.shape[0]
    step_proj, step_up, step_down = [step_ref[r : r + 1, 0:1] for r in (4, 5, 6)]

    loads = [
        pltpu.make_async_copy(up_hbm, up_ref, load_s.at[0]),
        pltpu.make_async_copy(down_hbm, down_ref, load_s.at[1]),
    ]

    @pl.when(at == 0)
    def _():
        for load in loads:
            load.start()
        dproj_s[...] = jnp.zeros_like(dproj_s)
        dup_s[...] = jnp.zeros_like(dup_s)
        ddown_s[...] = jnp.zeros_like(ddown_s)
        dub_s[...] = jnp.zeros_like(dub_s)
        dvec_s[...] = jnp.zeros_like(dvec_s)

    proj_bias, first_gain, first_shift, down_bias, second_gain, second_shift = [
        r[...].astype(F32)[None] for r in (pb_ref, fg_ref, fs_ref, db_ref, sg_ref, ss_ref)
    ]
    ctx = ctx_ref[...]
    first_in = tok_ref[...].astype(F32) + (dot_nn(ctx, proj_ref[...]) * step_proj + proj_bias)
    n1, r1 = normalize(first_in)
    normed = n1 * first_gain + first_shift
    low = normed.astype(BF16)

    @pl.when(at == 0)
    def _():
        for load in loads:
            load.wait()

    branch = None
    pre = dot_nn(low, up_ref[0])
    for t in range(parts):
        follow = dot_nn(low, up_ref[t + 1]) if t + 1 < parts else None
        act, slope = gelu_pair(pre * step_up + bias_ref[t, 0:1])
        pre = follow
        act = act.astype(BF16)
        act_s[t] = act
        slope_s[t] = slope
        if t:
            term = dot_nn(held, down_ref[t - 1])
            branch = term if branch is None else branch + term
        held = act
    branch = branch + dot_nn(held, down_ref[parts - 1])
    second_in = normed + (branch * step_down + down_bias)
    n2, r2 = normalize(second_in)
    out_ref[...] = (n2 * second_gain + second_shift).astype(BF16)
    og = og_ref[...].astype(F32)
    grad_second = norm_back(og * second_gain, n2, r2)
    dvec_s[4] += fold_rows(og * n2)
    dvec_s[5] += fold_rows(og)
    dvec_s[3] += fold_rows(grad_second)
    grad_down = (grad_second * step_down).astype(BF16)
    back = grad_second
    grad_act = dot_nt(grad_down, down_ref[0])
    for t in range(parts):
        follow = dot_nt(grad_down, down_ref[t + 1]) if t + 1 < parts else None
        grad_pre = grad_act * slope_s[t]
        grad_act = follow
        dub_s[t] += fold_rows(grad_pre)
        grad_up = (grad_pre * step_up).astype(BF16)
        back = back + dot_nt(grad_up, up_ref[t])
        dup_s[t] += dot_tn(low, grad_up)
        ddown_s[t] += dot_tn(grad_down, act_s[t])
    dvec_s[1] += fold_rows(back * n1)
    dvec_s[2] += fold_rows(back)
    grad_first = norm_back(back * first_gain, n1, r1)
    dvec_s[0] += fold_rows(grad_first)
    first_ref[...] = grad_first.astype(BF16)
    grad_proj = (grad_first * step_proj).astype(BF16)
    dproj_s[...] += dot_tn(ctx, grad_proj)
    gctx_ref[...] = dot_nt(grad_proj, proj_ref[...]).astype(BF16)

    @pl.when(at == last)
    def _():
        width = D // parts
        for t in range(parts):
            rows = dproj_s[t * width : (t + 1) * width]
            dproj_ref[t] = spread(rows.astype(BF16), dproj_ref.shape[1:])
            dup_ref[t] = spread(dup_s[t].astype(BF16), dup_ref.shape[1:])
            ddown_ref[t] = spread(ddown_s[t].astype(BF16), ddown_ref.shape[1:])
            dub_ref[t] = jnp.sum(dub_s[t], axis=0, keepdims=True)
        dvec_ref[...] = jnp.sum(dvec_s[...], axis=1)


def feed_forward(sizes, steps, biases, tokens, ctx, out_grad, proj, up, down, vecs):
    count = tokens.shape[0]
    parts, nz = 2 * sizes["x"], sizes["z"]
    wide = FF // parts
    proj, up, down = proj.reshape(D, D), up.reshape(parts, D, wide), down.reshape(parts, wide, D)
    split = (parts, 2, 2, nz, split_rows(D, 4 * nz), wide)
    split_proj = (parts, 2, nz, split_rows(D // parts, 2 * nz), D)
    block = pl.BlockSpec((TB, D), lambda i, *_: (i, 0))

    def whole(*shape):
        return pl.BlockSpec(shape, lambda i, *_: (0,) * len(shape))

    return pl.pallas_call(
        ffn_kernel,
        name="feed_forward",
        grid=(count // TB,),
        in_specs=[
            whole(8, LANES),
            whole(parts, 8, wide),
            block,
            block,
            block,
            whole(D, D),
            pl.BlockSpec(memory_space=pl.ANY),
            pl.BlockSpec(memory_space=pl.ANY),
        ]
        + [whole(D)] * 6,
        out_specs=[
            block,
            block,
            block,
            whole(*split_proj),
            whole(*split),
            whole(*split),
            whole(parts, 1, wide),
            whole(6, D),
        ],
        scratch_shapes=[
            pltpu.VMEM((parts, TB, wide), BF16),
            pltpu.VMEM((parts, TB, wide), F32),
            pltpu.VMEM((D, D), F32),
            pltpu.VMEM((parts, D, wide), F32),
            pltpu.VMEM((parts, D, wide), F32),
            pltpu.VMEM((parts, 8, wide), F32),
            pltpu.VMEM((6, 8, D), F32),
            pltpu.VMEM((parts, D, wide), BF16),
            pltpu.VMEM((parts, wide, D), BF16),
            pltpu.SemaphoreType.DMA((2,)),
        ],
        out_shape=[
            jax.ShapeDtypeStruct((count, D), BF16),
            jax.ShapeDtypeStruct((count, D), BF16),
            jax.ShapeDtypeStruct((count, D), BF16),
            jax.ShapeDtypeStruct(split_proj, BF16),
            jax.ShapeDtypeStruct(split, BF16),
            jax.ShapeDtypeStruct(split, BF16),
            jax.ShapeDtypeStruct((parts, 1, wide), F32),
            jax.ShapeDtypeStruct((6, D), F32),
        ],
        compiler_params=pltpu.CompilerParams(vmem_limit_bytes=VMEM_LIMIT),
        cost_estimate=pl.CostEstimate(
            flops=count * 14 * 10**6, bytes_accessed=count * 12000, transcendentals=count * 4096
        ),
    )(steps, biases, tokens, ctx, out_grad, proj, up, down, *vecs)


PLANS = (
    ((0, 2), (2, 6), (6, 9), (9, 12), (12, 15), (15, 19)),
    ((0, 2), (4, 8), (8, 11), (11, 14), (14, 17), (17, 21)),
    ((0, 3), (6, 11), (11, 14), (14, 19), (19, 24), (24, 31)),
    ((0, 3), (8, 13), (13, 16), (16, 20), (20, 26), (26, 34)),
    ((0, 3), (11, 14), (14, 16), (17, 22), (23, 27), (29, 36)),
    ((16, 19), (19, 23), (-1, -1), (24, 29), (29, 33), (33, 38)),
    ((16, 19), (19, 25), (-1, -1), (25, 30), (30, 35), (35, 39)),
    ((16, 19), (22, 28), (-1, -1), (28, 32), (32, 37), (37, 40)),
)
ORDERS = ('xy', 'xy', 'xy', 'xy', 'xy', 'plane', 'plane', 'plane')
THIRDS = 3


def passing(grads, weights, step):
    return jnp.where(weights.astype(F32) == 0.0, 0.0, grads.astype(F32)) / step


def back_kernel(
    sizes,
    step_ref,
    tok_ref,
    ints_ref,
    qkv_ref,
    probs_ref,
    ctx_ref,
    gctx_ref,
    first_ref,
    w_hbm,
    dproj_hbm,
    dup_hbm,
    ddown_hbm,
    dub_ref,
    dvec_ref,
    tg_ref,
    dqkv_out,
    dqv_out,
    dproj_out,
    dup_out,
    dub_out,
    ddown_out,
    vec_out,
    grad_s,
    dqkv_s,
    dqv_s,
    part_s,
    w_ref,
    load_s,
    *scratch,
):
    step = pl.program_id(0)
    rows = grad_s.shape[0]
    place = Place(sizes)
    parts = 2 * sizes["x"]
    width = D // parts
    step_tokens = step_ref[0:1, 0:1]
    sources = [
        lambda t: dup_hbm.at[t, 0],
        lambda t: ddown_hbm.at[t, 0],
        lambda t: dup_hbm.at[t, 1],
        lambda t: ddown_hbm.at[t, 1],
        lambda t: dproj_hbm.at[t],
    ]
    sources += [lambda t, q=q: part_s.at[t, q] for q in range(THIRDS)]
    streams = []
    for n, source in enumerate(sources):
        refs = scratch[9 * n : 9 * n + 9]
        own = refs[8] if n < 5 else None
        streams.append(Stream(place, ORDERS[n], source, *refs[:8], own))
    sums = Small(place, jnp.add, *scratch[9 * len(sources) :])

    load = pltpu.make_async_copy(w_hbm, w_ref, load_s.at[0])

    @pl.when(step == 0)
    def _():
        load.start()
        dqkv_s[...] = jnp.zeros_like(dqkv_s)
        dqv_s[...] = jnp.zeros_like(dqv_s)
        corners = [device for n, (_, _, device) in enumerate(place.plane()) if n > 1 and n % 2 == 0]
        place.hello(*corners)
        place.welcome(len(corners))

    def events(now):
        for s, plan in enumerate(PLANS):
            for k, p in enumerate(plan):
                if p[1] == now:
                    streams[s].finish(k)
        for s, plan in enumerate(PLANS):
            for k, p in enumerate(plan):
                if p[0] == now:
                    streams[s].start(k)

    def advance(tick, ticks):
        for now in ticks:
            if any(now in p for plan in PLANS for p in plan):
                pl.when(tick == now)(lambda: events(now))

    def pair_step(p, carry):
        for n in range(16 // (PAIRS * rows)):
            advance((step * PAIRS + p) * (16 // (PAIRS * rows)) + n, range(16))
        at = pl.multiple_of(p * LANES, LANES)
        q_pair = qkv_ref[:, pl.ds(at, LANES)]
        k_pair = qkv_ref[:, pl.ds(D + at, LANES)]
        v_pair = qkv_ref[:, pl.ds(2 * D + at, LANES)]
        g_pair = gctx_ref[:, pl.ds(at, LANES)]
        c_pair = ctx_ref[:, pl.ds(at, LANES)]
        product = (g_pair.astype(F32) * c_pair.astype(F32)).astype(BF16)
        lane = lax.broadcasted_iota(jnp.int32, (8, LANES), 1)
        line = lax.broadcasted_iota(jnp.int32, (8, LANES), 0)
        ones = jnp.where(lane // HEAD_DIM == line, 1.0, 0.0).astype(BF16)
        centre = dot_nt(ones, product)
        outs = []
        for n, (k0, k1, q0, q1) in enumerate(TILES):
            probs = probs_ref[0, pl.ds(2 * p, 2), n]
            gp = dot_nt(stacked(v_pair[k0:k1]), g_pair[q0:q1])
            gs = jnp.concatenate(
                [
                    (probs[h].astype(F32) * (gp[256 * h : 256 * h + 256] - centre[h : h + 1, q0:q1])).astype(BF16)
                    for h in range(2)
                ],
                axis=0,
            )
            d_values = unstacked(dot_nn(probs.reshape(512, 384), g_pair[q0:q1]))
            d_keys = unstacked(dot_nn(gs, q_pair[q0:q1]))
            outs.append(dot_tn(gs, stacked(k_pair[k0:k1])))
            grad_s[step, k0:k1, pl.ds(D + at, LANES)] = (
                d_keys * (step_tokens * step_ref[2:3, 0:1] * (1.0 / LOG2E))
            ).astype(BF16)
            dqv_s[1, :, pl.ds(at, LANES)] += fold_rows(d_values)
            grad_s[step, k0:k1, pl.ds(2 * D + at, LANES)] = (
                d_values * (step_tokens * step_ref[3:4, 0:1])
            ).astype(BF16)
        d_q = both(*outs) * 0.125
        dqv_s[0, :, pl.ds(at, LANES)] += fold_rows(d_q)
        grad_s[step, :, pl.ds(at, LANES)] = (d_q * (step_tokens * step_ref[1:2, 0:1])).astype(BF16)
        return carry

    @pl.when(step < rows)
    def _():
        lax.fori_loop(0, PAIRS, pair_step, 0)
        for i in range(3):
            dqkv_s[i] += dot_tn(grad_s[step, :, i * D : (i + 1) * D], ints_ref[...])

    pl.when(step == rows)(load.wait)

    @pl.when(step == rows)
    def _():
        for t in range(parts):
            piece = jnp.concatenate(
                [dqkv_s[i, t * width : (t + 1) * width] for i in range(3)], axis=0
            )
            part_s[t] = spread(piece.astype(BF16), part_s.shape[1:])
        dqv = jnp.sum(dqv_s[...], axis=1)
        vec = [dvec_ref[r : r + 1] for r in range(6)] + [dqv[0:1], dqv[1:2]]
        dub = jnp.concatenate([dub_ref[t] for t in range(parts)], axis=1)
        vec += [dub[:, r * D : (r + 1) * D] for r in range(4)]
        sums.start(0, tile_rows(vec, 16, D))

    @pl.when(step >= rows)
    def _():
        for n in range(4 // rows):
            advance(16 + (step - rows) * (4 // rows) + n, range(16, 20))

    def vectors():
        total = sums.finish(1)
        for n in range(6):
            vec_out[n] = total[n : n + 1]
        for t in range(parts):

            @pl.when(place.part == t)
            def _():
                dqv_out[...] = total[6:8, t * width : (t + 1) * width]
                wide = FF // parts
                dub_out[...] = total[
                    8 + t * wide // D : 9 + t * wide // D, t * wide % D : t * wide % D + wide
                ]

    @pl.when(step == rows + 1)
    def _():
        sums.start(1, sums.finish(0))

    @pl.when(step >= rows)
    def _():
        grads = grad_s[step - rows]
        total = None
        for i in range(3):
            term = dot_nt(grads[:, i * D : (i + 1) * D], w_ref[i])
            total = term if total is None else total + term
        tg_ref[...] = (first_ref[...].astype(F32) + passing(total, tok_ref[...], step_tokens)).astype(BF16)

    def joined(*group):
        halves = [streams[n].out[...].reshape(D // 2, FF // parts) for n in group]
        return jnp.concatenate(halves, axis=0)

    @pl.when(step == 2 * rows - 1)
    def _():
        ticks = sorted({n for plan in PLANS for p in plan for n in p if n >= 20})
        ended = [max(PLANS[s][5][1] for s in group) for group in ((0, 2), (1, 3), (4,))]
        for now in [19] + ticks:
            if now > 19:
                events(now)
            if now == ticks[len(ticks) // 3]:
                vectors()
            if now == max(19, ended[0]):
                dup_out[...] = joined(0, 2)
            if now == max(19, ended[1]):
                ddown_out[...] = joined(1, 3)
            if now == max(19, ended[2]):
                dproj_out[...] = streams[4].out[...].reshape(-1, D)[:width]
        whole = jnp.concatenate(
            [streams[5 + q].out[...].reshape(-1, D) for q in range(THIRDS)], axis=0
        )
        dqkv_out[...] = whole[: 3 * width]


def deliver_kernel(
    step_ref,
    tg_ref,
    dqkv_ref,
    dqv_ref,
    dproj_ref,
    dup_ref,
    dub_ref,
    ddown_ref,
    vec_ref,
    qkv_ref,
    proj_ref,
    up_ref,
    down_ref,
    tg_out,
    dqkv_out,
    dqv_out,
    dproj_out,
    dup_out,
    dub_out,
    ddown_out,
    *vec_outs,
):
    width = dqkv_out.shape[-1]
    tg_out[...] = tg_ref[...].astype(F32)
    for i in range(3):
        grad = jnp.transpose(dqkv_ref[i * width : (i + 1) * width].astype(F32))
        dqkv_out[i] = passing(grad, qkv_ref[i], step_ref[1 + i : 2 + i, 0:1])
    dproj_out[...] = passing(dproj_ref[...], proj_ref[...], step_ref[4:5, 0:1])
    dup_out[...] = passing(dup_ref[...], up_ref[...], step_ref[5:6, 0:1])
    grad = jnp.transpose(ddown_ref[...].astype(F32))
    ddown_out[...] = passing(grad, down_ref[...], step_ref[6:7, 0:1])
    dqv_out[...] = dqv_ref[...]
    dub_out[...] = dub_ref[0]
    for n, out in enumerate(vec_outs):
        out[...] = vec_ref[n, 0]


def deliver(steps, tokens_grad, dqkv, dqv, dproj, dup, dub, ddown, vec, qkv_w, proj_w, up_w, down_w):
    rows = max(1, tokens_grad.shape[0] // SEQ // 2)
    width, wide = qkv_w.shape[2], up_w.shape[1]

    def whole(*shape):
        return pl.BlockSpec(shape, lambda i: (0,) * len(shape))

    def down_rows(*shape):
        return pl.BlockSpec((shape[0] // rows,) + shape[1:], lambda i: (i, 0))

    def along(*shape):
        return pl.BlockSpec((shape[0], shape[1] // rows), lambda i: (0, i))

    qkv_block = pl.BlockSpec((3, D // rows, width), lambda i: (0, i, 0))
    outs = [
        (tokens_grad.shape, down_rows(*tokens_grad.shape)),
        (qkv_w.shape, qkv_block),
        ((2, width), whole(2, width)),
        (proj_w.shape, down_rows(*proj_w.shape)),
        (up_w.shape, down_rows(*up_w.shape)),
        ((wide,), whole(wide)),
        (down_w.shape, down_rows(*down_w.shape)),
    ] + [((D,), whole(D))] * 6
    return pl.pallas_call(
        deliver_kernel,
        name="deliver",
        grid=(rows,),
        in_specs=[
            whole(8, LANES),
            down_rows(*tokens_grad.shape),
            along(*dqkv.shape),
            whole(2, width),
            down_rows(*dproj.shape),
            down_rows(*dup.shape),
            whole(1, wide),
            along(*ddown.shape),
            whole(6, 1, D),
            qkv_block,
            down_rows(*proj_w.shape),
            down_rows(*up_w.shape),
            down_rows(*down_w.shape),
        ],
        out_specs=[spec for _, spec in outs],
        out_shape=[jax.ShapeDtypeStruct(shape, F32) for shape, _ in outs],
        compiler_params=pltpu.CompilerParams(vmem_limit_bytes=VMEM_LIMIT),
    )(steps, tokens_grad, dqkv, dqv, dproj, dup, dub, ddown, vec, qkv_w, proj_w, up_w, down_w)


def attend_back(
    sizes, steps, tokens, ints, qkv, probs, ctx, gctx, first, qkv_full, dproj, dup, ddown, dub, dvec
):
    rows = tokens.shape[0] // SEQ
    parts, nz = 2 * sizes["x"], sizes["z"]
    width, wide = D // parts, FF // parts
    part = (parts, THIRDS, 2, nz, split_rows(3 * width, 2 * THIRDS * nz), D)
    pieces = [dup.shape[-2:], ddown.shape[-2:], dup.shape[-2:], ddown.shape[-2:], dproj.shape[-2:]]
    pieces += [part[-2:]] * THIRDS
    early = lambda i: (jnp.minimum(i, rows - 1), 0)
    late = lambda i: (jnp.maximum(i - rows, 0), 0)
    hbm = pl.BlockSpec(memory_space=pl.ANY)

    def whole(*shape):
        return pl.BlockSpec(shape, lambda i: (0,) * len(shape))

    outs = [
        ((3 * width, D), BF16),
        ((2, width), F32),
        ((width, D), BF16),
        ((D, wide), BF16),
        ((1, wide), F32),
        ((D, wide), BF16),
        ((6, 1, D), F32),
    ]
    return pl.pallas_call(
        lambda *refs: back_kernel(sizes, *refs),
        name="attend_back",
        grid=(2 * rows,),
        in_specs=[
            whole(8, LANES),
            pl.BlockSpec((SEQ, D), late),
            pl.BlockSpec((SEQ, D), early),
            pl.BlockSpec((SEQ, 3 * D), early),
            pl.BlockSpec(
                (1, HEADS, 2, 256, 384), lambda i: (jnp.minimum(i, rows - 1), 0, 0, 0, 0)
            ),
            pl.BlockSpec((SEQ, D), early),
            pl.BlockSpec((SEQ, D), early),
            pl.BlockSpec((SEQ, D), late),
            hbm,
            hbm,
            hbm,
            hbm,
            whole(*dub.shape),
            whole(*dvec.shape),
        ],
        out_specs=[pl.BlockSpec((SEQ, D), late)] + [whole(*shape) for shape, _ in outs],
        scratch_shapes=[
            pltpu.VMEM((rows, SEQ, 3 * D), BF16),
            pltpu.VMEM((3, D, D), F32),
            pltpu.VMEM((2, 8, D), F32),
            pltpu.VMEM(part, BF16),
            pltpu.VMEM((3, D, D), BF16),
            pltpu.SemaphoreType.DMA((1,)),
        ]
        + sum([stream_scratch(sizes, o, *p) for o, p in zip(ORDERS, pieces)], [])
        + small_scratch(sizes, 16, D),
        out_shape=[jax.ShapeDtypeStruct((rows * SEQ, D), BF16)]
        + [jax.ShapeDtypeStruct(shape, kind) for shape, kind in outs],
        compiler_params=pltpu.CompilerParams(
            vmem_limit_bytes=VMEM_LIMIT, collective_id=1, has_side_effects=True
        ),
        cost_estimate=pl.CostEstimate(
            flops=rows * 6 * 10**9, bytes_accessed=rows * 8 * 10**6, transcendentals=0
        ),
    )(
        steps, tokens, ints, qkv, probs, ctx, gctx, first, qkv_full, dproj, dup, ddown, dub, dvec
    )

def local(
    tokens,
    segment_ids,
    row_lengths,
    qkv_weight,
    qv_bias,
    proj_weight,
    proj_bias,
    first_gain,
    first_shift,
    up_weight,
    up_bias,
    down_weight,
    down_bias,
    second_gain,
    second_shift,
    out_grad,
):
    rows = tokens.shape[0] // SEQ
    sizes = group_sizes(lax.axis_size("tensor"), lax.axis_size("dp"))
    ints, qkv, probs, ctx, qkv_full, steps, biases, proj_full, up_full, down_full = attend(
        sizes,
        row_lengths,
        tokens,
        segment_ids,
        qkv_weight,
        qv_bias,
        proj_weight,
        up_weight,
        down_weight,
        up_bias,
    )
    vecs = (proj_bias, first_gain, first_shift, down_bias, second_gain, second_shift)
    layer_out, grad_first, grad_ctx, dproj, dup, ddown, dub, dvec = feed_forward(
        sizes, steps, biases, tokens, ctx, out_grad, proj_full, up_full, down_full, vecs
    )
    sums = attend_back(
        sizes, steps, tokens, ints, qkv, probs, ctx, grad_ctx, grad_first, qkv_full,
        dproj, dup, ddown, dub, dvec,
    )
    tokens_grad, dqkv, dqv, dproj, dup, dub, ddown, *vec = deliver(
        steps, *sums, qkv_weight, proj_weight, up_weight, down_weight
    )
    return (
        layer_out, tokens_grad, dqkv, dqv, dproj, vec[0], vec[1], vec[2], dup, dub, ddown,
        vec[3], vec[4], vec[5],
    )


def solution(mesh):
    in_specs = (
        P(("dp", "tensor"), None),
        P("dp", None),
        P("dp"),
        P(None, None, "tensor"),
        P(None, "tensor"),
        P("tensor", None),
        P(),
        P(),
        P(),
        P(None, "tensor"),
        P("tensor"),
        P("tensor", None),
        P(),
        P(),
        P(),
        P(("dp", "tensor"), None),
    )
    out_specs = (
        P(("dp", "tensor"), None),
        P(("dp", "tensor"), None),
        P(None, None, "tensor"),
        P(None, "tensor"),
        P("tensor", None),
        P(),
        P(),
        P(),
        P(None, "tensor"),
        P("tensor"),
        P("tensor", None),
        P(),
        P(),
        P(),
    )
    return jax.shard_map(local, mesh=mesh, in_specs=in_specs, out_specs=out_specs, check_vma=False)
```

```python
import jax
import jax.numpy as jnp
from jax import lax
from jax.experimental import pallas as pl
from jax.experimental.pallas import tpu as pltpu
from jax.sharding import PartitionSpec as P

D = 512
HEADS = 8
HEAD_DIM = 64
FF = 2048
SEQ = 512
PAIRS = 4
LANES = 128
LEVELS = 127.0
EPS = 1e-12
MASKED = -1e30
LOG2E = 1.4426950408889634
SCORE_SCALE = 0.125 * LOG2E
VMEM_LIMIT = 58 << 20
F32 = jnp.float32
BF16 = jnp.bfloat16
TILES = ((0, 256, 0, 384), (256, 512, 128, 512))


def rounded(scaled):
    magnitude = jnp.floor(jnp.abs(scaled) + 0.5)
    return jnp.where(scaled < 0.0, -magnitude, magnitude)


def dot_nn(a, b):
    return lax.dot_general(a, b, (((1,), (0,)), ((), ())), preferred_element_type=F32)


def dot_nt(a, b):
    return lax.dot_general(a, b, (((1,), (1,)), ((), ())), preferred_element_type=F32)


def dot_tn(a, b):
    return lax.dot_general(a, b, (((0,), (0,)), ((), ())), preferred_element_type=F32)


def head_mask(head, rows):
    lane = lax.broadcasted_iota(jnp.int32, (rows, LANES), 1)
    return (lane < HEAD_DIM) if head == 0 else (lane >= HEAD_DIM)


def stacked(pair):
    zeros = jnp.zeros_like(pair)
    return jnp.concatenate(
        [jnp.where(head_mask(h, pair.shape[0]), pair, zeros) for h in range(2)], axis=0
    )


def unstacked(blocks):
    rows = blocks.shape[0] // 2
    return jnp.where(head_mask(0, rows), blocks[:rows], blocks[rows:])


def both(left, right):
    return jnp.concatenate([left[:128], left[128:] + right[:256], right[256:]], axis=0)


MESH = pl.DeviceIdType.MESH
MESH_AXES = ("tensor", "dp")


def group_sizes(tensor_size, dp_size):
    return {
        "core": 2,
        "x": tensor_size // 2,
        "y": 2,
        "z": dp_size // 2,
        "tensor": tensor_size,
        "dp": dp_size,
    }


class Place:
    def __init__(self, sizes):
        t, d = lax.axis_index("tensor"), lax.axis_index("dp")
        self.sizes = sizes
        self.part = t
        self.at = {"core": t % 2, "x": t // 2, "y": d % 2, "z": d // 2, "tensor": t, "dp": d}

    def size(self, group):
        return self.sizes[group]

    def peer(self, group, k):
        if group in MESH_AXES:
            at = {axis: lax.axis_index(axis) for axis in MESH_AXES}
            at[group] = (at[group] + k) % self.sizes[group]
            return at[group], (at["dp"], at["tensor"])
        at = dict(self.at)
        at[group] = (at[group] + k) % self.sizes[group]
        return at[group], (at["z"] * 2 + at["y"], at["x"] * 2 + at["core"])

    def greet(self):
        self.hello()
        self.welcome()

    def welcome(self, others=0):
        count = sum(self.sizes[group] - 1 for group in MESH_AXES) + others
        pl.semaphore_wait(pltpu.get_barrier_semaphore(), count)

    def plane(self):
        members = []
        for k in range(self.sizes["x"]):
            for side in range(2):
                if k or side:
                    at = dict(self.at)
                    at["x"] = (at["x"] + k) % self.sizes["x"]
                    at["y"] = (at["y"] + side) % 2
                    device = (at["z"] * 2 + at["y"], at["x"] * 2 + at["core"])
                    members.append((at["x"], at["y"], device))
        return members

    def hello(self, *others):
        barrier = pltpu.get_barrier_semaphore()
        for device in others:
            pl.semaphore_signal(barrier, inc=1, device_id=device, device_id_type=MESH)
        for group in MESH_AXES:
            for k in range(1, self.sizes[group]):
                pl.semaphore_signal(
                    barrier, inc=1, device_id=self.peer(group, k)[1], device_id_type=MESH
                )


class Sems:
    def __init__(self, send, recv):
        self.send, self.recv = send, recv

    def copy(self, at, source, target, device):
        return pltpu.make_async_remote_copy(
            src_ref=source,
            dst_ref=target,
            send_sem=self.send.at[at],
            recv_sem=self.recv.at[at],
            device_id=device,
            device_id_type=MESH,
        )


def exchange(place, group, source, target, sems, base):
    copies = []
    for k in range(1, place.size(group)):
        index, device = place.peer(group, k)
        copies.append(sems.copy(base + k - 1, source(k, index), target(k, index), device))
    return copies


def add(first, *others):
    if len(others) == 1:
        return first + others[0]
    total = first.astype(F32)
    for other in others:
        total = total + other.astype(F32)
    return total.astype(BF16)


class Stream:
    phases = 6

    def __init__(self, place, order, grad, held, got_c, got_1, got_2, got_z, out, send, recv, own):
        self.place, self.order, self.grad, self.held, self.out = place, order, grad, held, out
        self.got_c, self.got_1, self.got_2, self.got_z = got_c, got_1, got_2, got_z
        self.sems, self.own = Sems(send, recv), own

    def local(self):
        if self.own is None:
            return []
        return [
            pltpu.make_async_copy(
                self.grad(2 * i + self.place.at["core"]), self.held.at[i], self.own.at[i]
            )
            for i in range(self.place.size("x"))
        ]

    def copies(self, phase):
        place, at, held = self.place, self.place.at, self.held
        nx, nz = place.size("x"), place.size("z")
        base = [0, nx, 2 * nx, 3 * nx, 3 * nx + nz, 3 * nx + 2 * nz][phase]
        sems = self.sems
        if phase == 0:
            other, device = place.peer("core", 1)
            return [
                sems.copy(i, self.grad(2 * i + other), self.got_c.at[i], device) for i in range(nx)
            ]
        if self.order == "plane":
            if phase == 2:
                return []
            if phase == 1:
                return [
                    sems.copy(base + n, held.at[x, y], self.got_1.at[n], device)
                    for n, (x, y, device) in enumerate(place.plane())
                ]
        if phase == 1 and self.order == "xy":
            return exchange(
                place, "x", lambda k, j: held.at[j], lambda k, j: self.got_1.at[k - 1], sems, base
            )
        if phase == 2 and self.order == "xy":
            return exchange(
                place, "y", lambda k, j: held.at[at["x"], j], lambda k, j: self.got_2.at[0], sems, base
            )
        if phase == 1:
            other, device = place.peer("y", 1)
            return [
                sems.copy(base + i, held.at[i, other], self.got_1.at[i], device) for i in range(nx)
            ]
        if phase == 2:
            return exchange(
                place,
                "x",
                lambda k, j: held.at[j, at["y"]],
                lambda k, j: self.got_2.at[k - 1],
                sems,
                base,
            )
        if phase == 3:
            return exchange(
                place,
                "z",
                lambda k, j: held.at[at["x"], at["y"], j],
                lambda k, j: self.got_z.at[k - 1],
                sems,
                base,
            )
        if phase == 4:
            piece = self.out.at[at["y"], at["z"]]
            return exchange(place, "z", lambda k, j: piece, lambda k, j: piece, sems, base)
        half = self.out.at[at["y"]]
        return exchange(place, "y", lambda k, j: half, lambda k, j: half, sems, base)

    def start(self, phase):
        for copy in self.copies(phase) + (self.local() if phase == 0 else []):
            copy.start()

    def finish(self, phase):
        for copy in self.copies(phase) + (self.local() if phase == 0 else []):
            copy.wait()
        at, held = self.place.at, self.held
        nx, nz = self.place.size("x"), self.place.size("z")
        if phase == 0:
            for i in range(nx):
                for y in range(2):
                    own = held[i, y] if self.own is not None else self.grad(2 * i + at["core"])[y]
                    held[i, y] = add(own, self.got_c[i, y])
        elif phase == 1 and self.order == "xy":
            for y in range(2):
                held[at["x"], y] = add(
                    held[at["x"], y], *[self.got_1[k, y] for k in range(nx - 1)]
                )
        elif phase == 1 and self.order == "plane":
            held[at["x"], at["y"]] = add(
                held[at["x"], at["y"]], *[self.got_1[n] for n in range(2 * nx - 1)]
            )
        elif phase == 1:
            for i in range(nx):
                held[i, at["y"]] = add(held[i, at["y"]], self.got_1[i])
        elif phase == 2 and self.order != "plane":
            count = 1 if self.order == "xy" else nx - 1
            held[at["x"], at["y"]] = add(
                held[at["x"], at["y"]], *[self.got_2[k] for k in range(count)]
            )
        elif phase == 3:
            self.out[at["y"], at["z"]] = add(
                held[at["x"], at["y"], at["z"]], *[self.got_z[k] for k in range(nz - 1)]
            )


def stream_scratch(sizes, order, rows, lanes):
    nx, nz = sizes["x"], sizes["z"]
    count = 3 * nx + 2 * nz + 1
    piece = (nz, rows, lanes)
    first = {"xy": (nx - 1, 2), "yx": (nx,), "plane": (2 * nx - 1,)}[order]
    second = (nx - 1,) if order == "yx" else (1,)
    return [
        pltpu.VMEM((nx, 2) + piece, BF16),
        pltpu.VMEM((nx, 2) + piece, BF16),
        pltpu.VMEM(first + piece, BF16),
        pltpu.VMEM(second + piece, BF16),
        pltpu.VMEM((nz - 1,) + piece[1:], BF16),
        pltpu.VMEM((2,) + piece, BF16),
        pltpu.SemaphoreType.DMA((count,)),
        pltpu.SemaphoreType.DMA((count,)),
        pltpu.SemaphoreType.DMA((nx,)),
    ]


class Small:
    def __init__(self, place, combine, slots, send, recv):
        self.place, self.combine, self.slots, self.sems = place, combine, slots, Sems(send, recv)

    def offsets(self, phase):
        sizes = [self.place.size(g) for g in MESH_AXES]
        return sum(sizes[:phase]), sum(sizes[:phase]) - phase

    def copies(self, phase):
        slot, sem = self.offsets(phase)
        return exchange(
            self.place,
            MESH_AXES[phase],
            lambda k, j: self.slots.at[slot],
            lambda k, j: self.slots.at[slot + k],
            self.sems,
            sem,
        )

    def start(self, phase, values):
        self.slots[self.offsets(phase)[0]] = values
        for copy in self.copies(phase):
            copy.start()

    def finish(self, phase):
        for copy in self.copies(phase):
            copy.wait()
        slot = self.offsets(phase)[0]
        count, me = self.place.size(MESH_AXES[phase]), self.place.at[MESH_AXES[phase]]
        total = None
        for member in range(count):
            term = self.slots[slot + (me + count - member) % count]
            total = term if total is None else self.combine(total, term)
        return total


def small_scratch(sizes, rows, lanes):
    total = sum(sizes[g] for g in MESH_AXES)
    return [
        pltpu.VMEM((total, rows, lanes), F32),
        pltpu.SemaphoreType.DMA((total - 2,)),
        pltpu.SemaphoreType.DMA((total - 2,)),
    ]


class Gather:
    def __init__(self, place, own, every, send, recv, keep):
        self.place, self.own, self.every, self.sems, self.keep = place, own, every, Sems(send, recv), keep

    def far(self):
        place = self.place
        mine = self.every.at[place.part]
        return exchange(place, "x", lambda k, j: self.own, lambda k, j: mine, self.sems, 0)

    def near(self, step):
        place = self.place
        nx = place.size("x")
        device = place.peer("core", 1)[1]
        if step == 0:
            return self.sems.copy(nx - 1, self.own, self.every.at[place.part], device)
        chip = (place.at["x"] + nx - step) % nx
        block = self.every.at[chip * 2 + place.at["core"]]
        return self.sems.copy(nx - 1 + step, block, block, device)

    def mine(self):
        return pltpu.make_async_copy(self.own, self.every.at[self.place.part], self.keep.at[0])

    def start(self):
        for copy in self.far():
            copy.start()
        self.near(0).start()
        self.mine().start()

    def forward(self):
        for copy in self.far():
            copy.wait()
        for k in range(1, self.place.size("x")):
            self.near(k).start()

    def finish(self):
        for k in range(self.place.size("x")):
            self.near(k).wait()
        self.mine().wait()


class SplitGather(Gather):
    def far(self):
        place, y = self.place, self.place.at["y"]
        mine, half = self.every.at[place.part, y], self.own.at[y]
        return exchange(place, "x", lambda k, j: half, lambda k, j: mine, self.sems, 0)

    def side(self):
        place = self.place
        nx, y = place.size("x"), place.at["y"]
        copies = []
        for k in range(1, nx):
            chip = (place.at["x"] + nx - k) % nx
            half = self.every.at[chip * 2 + place.at["core"], y]
            copies.append(self.sems.copy(2 * nx - 2 + k, half, half, place.peer("y", 1)[1]))
        return copies

    def cross(self):
        for copy in self.far():
            copy.wait()
        for copy in self.side():
            copy.start()

    def forward(self):
        for copy in self.side():
            copy.wait()
        for k in range(1, self.place.size("x")):
            self.near(k).start()


def gather_scratch(sizes):
    count = 3 * sizes["x"] - 2
    return [
        pltpu.SemaphoreType.DMA((count,)),
        pltpu.SemaphoreType.DMA((count,)),
        pltpu.SemaphoreType.DMA((1,)),
    ]


def split_rows(rows, pieces):
    return -(-rows // (pieces * 8)) * 8


def spread(values, shape):
    count = 1
    for size in shape[:-1]:
        count *= size
    if count > values.shape[0]:
        zeros = jnp.zeros((count - values.shape[0], values.shape[1]), values.dtype)
        values = jnp.concatenate([values, zeros], axis=0)
    return values.reshape(shape)


def tile_rows(rows, height, lanes):
    filled = [r if r.shape[1] == lanes else jnp.concatenate([r, jnp.zeros((1, lanes - r.shape[1]), F32)], axis=1) for r in rows]
    at = lax.broadcasted_iota(jnp.int32, (height, lanes), 0)
    total = jnp.zeros((height, lanes), F32)
    for n, r in enumerate(filled):
        total = jnp.where(at == n, r, total)
    return total


def top(values):
    peak = jnp.max(jnp.abs(values.astype(F32)), axis=0, keepdims=True)
    return jnp.max(peak, axis=1, keepdims=True)


def attend_kernel(
    sizes,
    len_ref,
    tok_hbm,
    seg_ref,
    qkv_hbm,
    qvb_sh,
    proj_hbm,
    up_hbm,
    down_hbm,
    ub_sh,
    ints_ref,
    qkv_ref,
    probs_ref,
    ctx_ref,
    w_ref,
    step_ref,
    bias_ref,
    proj_all,
    up_all,
    down_all,
    mask_s,
    ints_s,
    tok_ref,
    qkv_sh,
    proj_sh,
    up_sh,
    down_sh,
    load_s,
    raw_all,
    bias_all,
    bias_own,
    proj_own,
    up_own,
    down_own,
    *sems,
):
    row = pl.program_id(0)
    last = pl.num_programs(0) - 1
    place = Place(sizes)
    parts = 2 * sizes["x"]
    width = D // parts
    early = [
        Gather(place, own, every, *sems[3 * n : 3 * n + 3])
        for n, (own, every) in enumerate(
            [(bias_own, bias_all)] + [(qkv_sh.at[i], raw_all.at[i]) for i in range(3)]
        )
    ]
    late = [
        SplitGather(place, own, every, *sems[12 + 3 * n : 15 + 3 * n])
        for n, (own, every) in enumerate(
            ((proj_own, proj_all), (up_own, up_all), (down_own, down_all))
        )
    ]
    peaks = Small(place, jnp.maximum, *sems[21:24])

    @pl.when(row == 0)
    def _():
        place.hello()
        loads = [
            pltpu.make_async_copy(source, target, load_s.at[n])
            for n, (source, target) in enumerate(
                (
                    (tok_hbm, tok_ref),
                    (qkv_hbm, qkv_sh),
                    (proj_hbm, proj_sh),
                    (up_hbm, up_sh),
                    (down_hbm, down_sh),
                )
            )
        ]
        for load in loads:
            load.start()
        for load in loads:
            load.wait()
        bias_own[...] = tile_rows(
            [ub_sh[...].astype(F32)[None], qvb_sh[0:1].astype(F32), qvb_sh[1:2].astype(F32)],
            8,
            ub_sh.shape[0],
        )
        tops = [top(tok_ref[...])] + [top(qkv_sh[i]) for i in range(3)]
        tops += [top(proj_sh[...]), top(up_sh[...]), top(down_sh[...])]
        total = tile_rows([jnp.broadcast_to(t, (1, LANES)) for t in tops], 8, LANES)
        place.welcome()
        peaks.start(0, total)
        for gather in early:
            gather.start()
        peaks.start(1, peaks.finish(0))
        step_ref[...] = peaks.finish(1) / LEVELS
        for own, shard, r in ((proj_own, proj_sh, 4), (up_own, up_sh, 5), (down_own, down_sh, 6)):
            for h in range(2):
                half = shard[h * own.shape[1] : (h + 1) * own.shape[1]]
                own[h] = rounded(half.astype(F32) / step_ref[r : r + 1, 0:1]).astype(BF16)
        for r in range(ints_s.shape[0] // SEQ):
            rows = slice(r * SEQ, (r + 1) * SEQ)
            ints_s[rows] = rounded(tok_ref[rows].astype(F32) / step_ref[0:1, 0:1]).astype(BF16)
        for gather in early[:2]:
            gather.forward()
        for i in range(3):
            if i < 2:
                early[2 + i].forward()
            early[1 + i].finish()
            for t in range(parts):
                w_ref[i, :, t * width : (t + 1) * width] = rounded(
                    raw_all[i, t].astype(F32) / step_ref[1 + i : 2 + i, 0:1]
                ).astype(BF16)
        for gather in late:
            gather.start()
        early[0].finish()
        bias_ref[...] = bias_all[...]

    for n, gather in enumerate(late):
        pl.when(row == jnp.minimum((1, 1, 2)[n], last))(gather.cross)

    @pl.when(row == last)
    def _():
        for gather in late:
            gather.forward()

    step_tokens = step_ref[0:1, 0:1]
    ints = ints_s[pl.ds(pl.multiple_of(row * SEQ, SEQ), SEQ), :]
    ints_ref[...] = ints
    biases = [
        jnp.concatenate([bias_all[t, r : r + 1, :width] for t in range(parts)], axis=1)
        for r in (1, 2)
    ]
    for i in range(3):
        raw = dot_nn(ints, w_ref[i]) * (step_tokens * step_ref[1 + i : 2 + i, 0:1])
        if i == 0:
            raw = (raw + biases[0]) * SCORE_SCALE
        if i == 2:
            raw = raw + biases[1]
        qkv_ref[:, i * D : (i + 1) * D] = raw.astype(BF16)
    here = place.part * pl.num_programs(0) + row
    seg_q = seg_ref[pl.ds(here, 1), :].astype(F32)
    length = len_ref[here]
    spot = lax.broadcasted_iota(jnp.int32, (8, SEQ), 1)
    seg_k = jnp.where(spot < length, jnp.broadcast_to(seg_q, (8, SEQ)), -1.0)
    seg_k = jnp.transpose(seg_k)[:, 0:1]
    for n, (k0, k1, q0, q1) in enumerate(TILES):
        keys = lax.broadcasted_iota(jnp.int32, (k1 - k0, q1 - q0), 0) + k0
        queries = lax.broadcasted_iota(jnp.int32, (k1 - k0, q1 - q0), 1) + q0
        allowed = (seg_k[k0:k1] == seg_q[:, q0:q1]) | (keys == queries)
        mask_s[n] = jnp.where(allowed, 0.0, MASKED)

    def pair_step(p, carry):
        at = pl.multiple_of(p * LANES, LANES)
        q_pair = qkv_ref[:, pl.ds(at, LANES)]
        k_pair = qkv_ref[:, pl.ds(D + at, LANES)]
        v_pair = qkv_ref[:, pl.ds(2 * D + at, LANES)]
        scores = []
        for n, (k0, k1, q0, q1) in enumerate(TILES):
            s = dot_nt(stacked(k_pair[k0:k1]), q_pair[q0:q1])
            scores.append(s.reshape(2, 256, 384) + mask_s[n])
        peak = [jnp.max(s, axis=1, keepdims=True) for s in scores]
        high = jnp.concatenate(
            [
                peak[0][:, :, :128],
                jnp.maximum(peak[0][:, :, 128:], peak[1][:, :, :256]),
                peak[1][:, :, 256:],
            ],
            axis=2,
        )
        weights = [jnp.exp2(s - high[:, :, q0:q1]) for s, (k0, k1, q0, q1) in zip(scores, TILES)]
        sums = [jnp.sum(w, axis=1, keepdims=True) for w in weights]
        totals = jnp.concatenate(
            [
                sums[0][:, :, :128],
                sums[0][:, :, 128:] + sums[1][:, :, :256],
                sums[1][:, :, 256:],
            ],
            axis=2,
        )
        inverse = 1.0 / totals
        outs = []
        for n, (k0, k1, q0, q1) in enumerate(TILES):
            probs = (weights[n] * inverse[:, :, q0:q1]).astype(BF16)
            probs_ref[0, pl.ds(2 * p, 2), n] = probs
            outs.append(dot_tn(probs.reshape(512, 384), stacked(v_pair[k0:k1])))
        ctx_ref[:, pl.ds(at, LANES)] = both(*outs).astype(BF16)
        return carry

    lax.fori_loop(0, PAIRS, pair_step, 0)

    @pl.when(row == last)
    def _():
        for gather in late:
            gather.finish()


def attend(sizes, lens, tokens, segments, qkv_w, qv_bias, proj_w, up_w, down_w, up_b):
    rows = tokens.shape[0] // SEQ
    parts = 2 * sizes["x"]
    hbm = pl.BlockSpec(memory_space=pl.ANY)
    halves = [(2, w.shape[0] // 2, w.shape[1]) for w in (proj_w, up_w, down_w)]

    def whole(*shape):
        return pl.BlockSpec(shape, lambda i, *_: (0,) * len(shape))

    return pl.pallas_call(
        lambda *refs: attend_kernel(sizes, *refs),
        name="attend",
        grid_spec=pltpu.PrefetchScalarGridSpec(
            num_scalar_prefetch=0,
            grid=(rows,),
            in_specs=[
                pl.BlockSpec(memory_space=pltpu.SMEM),
                hbm,
                whole(*segments.shape),
                hbm,
                whole(*qv_bias.shape),
                hbm,
                hbm,
                hbm,
                whole(*up_b.shape),
            ],
            out_specs=[
                pl.BlockSpec((SEQ, D), lambda i, *_: (i, 0)),
                pl.BlockSpec((SEQ, 3 * D), lambda i, *_: (i, 0)),
                pl.BlockSpec((1, HEADS, 2, 256, 384), lambda i, *_: (i, 0, 0, 0, 0)),
                pl.BlockSpec((SEQ, D), lambda i, *_: (i, 0)),
                whole(3, D, D),
                whole(8, LANES),
                whole(parts, 8, up_b.shape[0]),
                hbm,
                hbm,
                hbm,
            ],
            scratch_shapes=[
                pltpu.VMEM((2, 256, 384), F32),
                pltpu.VMEM(tokens.shape, BF16),
                pltpu.VMEM(tokens.shape, BF16),
                pltpu.VMEM(qkv_w.shape, BF16),
                pltpu.VMEM(proj_w.shape, BF16),
                pltpu.VMEM(up_w.shape, BF16),
                pltpu.VMEM(down_w.shape, BF16),
                pltpu.SemaphoreType.DMA((5,)),
                pltpu.VMEM((3, parts) + qkv_w.shape[1:], BF16),
                pltpu.VMEM((parts, 8, up_b.shape[0]), F32),
                pltpu.VMEM((8, up_b.shape[0]), F32),
            ]
            + [pltpu.VMEM(shape, BF16) for shape in halves]
            + sum([gather_scratch(sizes) for _ in range(7)], [])
            + small_scratch(sizes, 8, LANES),
        ),
        out_shape=[
            jax.ShapeDtypeStruct((rows * SEQ, D), BF16),
            jax.ShapeDtypeStruct((rows * SEQ, 3 * D), BF16),
            jax.ShapeDtypeStruct((rows, HEADS, 2, 256, 384), BF16),
            jax.ShapeDtypeStruct((rows * SEQ, D), BF16),
            jax.ShapeDtypeStruct((3, D, D), BF16),
            jax.ShapeDtypeStruct((8, LANES), F32),
            jax.ShapeDtypeStruct((parts, 8, up_b.shape[0]), F32),
        ]
        + [jax.ShapeDtypeStruct((parts,) + shape, BF16) for shape in halves],
        compiler_params=pltpu.CompilerParams(
            vmem_limit_bytes=VMEM_LIMIT, collective_id=0, has_side_effects=True
        ),
        cost_estimate=pl.CostEstimate(
            flops=rows * 3 * 10**9, bytes_accessed=rows * 6 * 10**6, transcendentals=rows * 2 * 10**6
        ),
    )(lens, tokens, segments, qkv_w, qv_bias, proj_w, up_w, down_w, up_b)

INV_SQRT_2PI = 0.3989422804014327


def gelu_pair(pre):
    cdf = 0.5 + 0.5 * lax.erf(pre * 0.7071067811865476)
    bell = jnp.exp2(pre * pre * (-0.5 * LOG2E))
    return pre * cdf, cdf + (pre * INV_SQRT_2PI) * bell


def fold_rows(values):
    total = values[0:8]
    for r in range(8, values.shape[0], 8):
        total = total + values[r : r + 8]
    return total


def normalize(values):
    centred = values - jnp.mean(values, axis=-1, keepdims=True)
    inverse = lax.rsqrt(jnp.mean(centred * centred, axis=-1, keepdims=True) + EPS)
    return centred * inverse, inverse


def norm_back(scaled, standard, inverse):
    return inverse * (
        scaled
        - jnp.mean(scaled, axis=-1, keepdims=True)
        - standard * jnp.mean(scaled * standard, axis=-1, keepdims=True)
    )


TB = 512


def ffn_kernel(
    step_ref,
    bias_ref,
    tok_ref,
    ctx_ref,
    og_ref,
    proj_ref,
    up_hbm,
    down_hbm,
    pb_ref,
    fg_ref,
    fs_ref,
    db_ref,
    sg_ref,
    ss_ref,
    out_ref,
    first_ref,
    gctx_ref,
    dproj_ref,
    dup_ref,
    ddown_ref,
    dub_ref,
    dvec_ref,
    act_s,
    slope_s,
    dproj_s,
    dup_s,
    ddown_s,
    dub_s,
    dvec_s,
    up_ref,
    down_ref,
    load_s,
):
    at = pl.program_id(0)
    last = pl.num_programs(0) - 1
    parts = up_ref.shape[0]
    step_proj, step_up, step_down = [step_ref[r : r + 1, 0:1] for r in (4, 5, 6)]

    loads = [
        pltpu.make_async_copy(up_hbm, up_ref, load_s.at[0]),
        pltpu.make_async_copy(down_hbm, down_ref, load_s.at[1]),
    ]

    @pl.when(at == 0)
    def _():
        for load in loads:
            load.start()
        dproj_s[...] = jnp.zeros_like(dproj_s)
        dup_s[...] = jnp.zeros_like(dup_s)
        ddown_s[...] = jnp.zeros_like(ddown_s)
        dub_s[...] = jnp.zeros_like(dub_s)
        dvec_s[...] = jnp.zeros_like(dvec_s)

    proj_bias, first_gain, first_shift, down_bias, second_gain, second_shift = [
        r[...].astype(F32)[None] for r in (pb_ref, fg_ref, fs_ref, db_ref, sg_ref, ss_ref)
    ]
    ctx = ctx_ref[...]
    first_in = tok_ref[...].astype(F32) + (dot_nn(ctx, proj_ref[...]) * step_proj + proj_bias)
    n1, r1 = normalize(first_in)
    normed = n1 * first_gain + first_shift
    low = normed.astype(BF16)

    @pl.when(at == 0)
    def _():
        for load in loads:
            load.wait()

    branch = None
    pre = dot_nn(low, up_ref[0])
    for t in range(parts):
        follow = dot_nn(low, up_ref[t + 1]) if t + 1 < parts else None
        act, slope = gelu_pair(pre * step_up + bias_ref[t, 0:1])
        pre = follow
        act = act.astype(BF16)
        act_s[t] = act
        slope_s[t] = slope
        if t:
            term = dot_nn(held, down_ref[t - 1])
            branch = term if branch is None else branch + term
        held = act
    branch = branch + dot_nn(held, down_ref[parts - 1])
    second_in = normed + (branch * step_down + down_bias)
    n2, r2 = normalize(second_in)
    out_ref[...] = (n2 * second_gain + second_shift).astype(BF16)
    og = og_ref[...].astype(F32)
    grad_second = norm_back(og * second_gain, n2, r2)
    dvec_s[4] += fold_rows(og * n2)
    dvec_s[5] += fold_rows(og)
    dvec_s[3] += fold_rows(grad_second)
    grad_down = (grad_second * step_down).astype(BF16)
    back = grad_second
    grad_act = dot_nt(grad_down, down_ref[0])
    for t in range(parts):
        follow = dot_nt(grad_down, down_ref[t + 1]) if t + 1 < parts else None
        grad_pre = grad_act * slope_s[t]
        grad_act = follow
        dub_s[t] += fold_rows(grad_pre)
        grad_up = (grad_pre * step_up).astype(BF16)
        back = back + dot_nt(grad_up, up_ref[t])
        dup_s[t] += dot_tn(low, grad_up)
        ddown_s[t] += dot_tn(grad_down, act_s[t])
    dvec_s[1] += fold_rows(back * n1)
    dvec_s[2] += fold_rows(back)
    grad_first = norm_back(back * first_gain, n1, r1)
    dvec_s[0] += fold_rows(grad_first)
    first_ref[...] = grad_first.astype(BF16)
    grad_proj = (grad_first * step_proj).astype(BF16)
    dproj_s[...] += dot_tn(ctx, grad_proj)
    gctx_ref[...] = dot_nt(grad_proj, proj_ref[...]).astype(BF16)

    @pl.when(at == last)
    def _():
        width = D // parts
        for t in range(parts):
            rows = dproj_s[t * width : (t + 1) * width]
            dproj_ref[t] = spread(rows.astype(BF16), dproj_ref.shape[1:])
            dup_ref[t] = spread(dup_s[t].astype(BF16), dup_ref.shape[1:])
            ddown_ref[t] = spread(ddown_s[t].astype(BF16), ddown_ref.shape[1:])
            dub_ref[t] = jnp.sum(dub_s[t], axis=0, keepdims=True)
        dvec_ref[...] = jnp.sum(dvec_s[...], axis=1)


def feed_forward(sizes, steps, biases, tokens, ctx, out_grad, proj, up, down, vecs):
    count = tokens.shape[0]
    parts, nz = 2 * sizes["x"], sizes["z"]
    wide = FF // parts
    proj, up, down = proj.reshape(D, D), up.reshape(parts, D, wide), down.reshape(parts, wide, D)
    split = (parts, 2, 2, nz, split_rows(D, 4 * nz), wide)
    split_proj = (parts, 2, nz, split_rows(D // parts, 2 * nz), D)
    block = pl.BlockSpec((TB, D), lambda i, *_: (i, 0))

    def whole(*shape):
        return pl.BlockSpec(shape, lambda i, *_: (0,) * len(shape))

    return pl.pallas_call(
        ffn_kernel,
        name="feed_forward",
        grid=(count // TB,),
        in_specs=[
            whole(8, LANES),
            whole(parts, 8, wide),
            block,
            block,
            block,
            whole(D, D),
            pl.BlockSpec(memory_space=pl.ANY),
            pl.BlockSpec(memory_space=pl.ANY),
        ]
        + [whole(D)] * 6,
        out_specs=[
            block,
            block,
            block,
            whole(*split_proj),
            whole(*split),
            whole(*split),
            whole(parts, 1, wide),
            whole(6, D),
        ],
        scratch_shapes=[
            pltpu.VMEM((parts, TB, wide), BF16),
            pltpu.VMEM((parts, TB, wide), F32),
            pltpu.VMEM((D, D), F32),
            pltpu.VMEM((parts, D, wide), F32),
            pltpu.VMEM((parts, D, wide), F32),
            pltpu.VMEM((parts, 8, wide), F32),
            pltpu.VMEM((6, 8, D), F32),
            pltpu.VMEM((parts, D, wide), BF16),
            pltpu.VMEM((parts, wide, D), BF16),
            pltpu.SemaphoreType.DMA((2,)),
        ],
        out_shape=[
            jax.ShapeDtypeStruct((count, D), BF16),
            jax.ShapeDtypeStruct((count, D), BF16),
            jax.ShapeDtypeStruct((count, D), BF16),
            jax.ShapeDtypeStruct(split_proj, BF16),
            jax.ShapeDtypeStruct(split, BF16),
            jax.ShapeDtypeStruct(split, BF16),
            jax.ShapeDtypeStruct((parts, 1, wide), F32),
            jax.ShapeDtypeStruct((6, D), F32),
        ],
        compiler_params=pltpu.CompilerParams(vmem_limit_bytes=VMEM_LIMIT),
        cost_estimate=pl.CostEstimate(
            flops=count * 14 * 10**6, bytes_accessed=count * 12000, transcendentals=count * 4096
        ),
    )(steps, biases, tokens, ctx, out_grad, proj, up, down, *vecs)


PLANS = (
    ((0, 2), (2, 6), (6, 9), (9, 12), (12, 15), (15, 19)),
    ((0, 2), (4, 8), (8, 11), (11, 14), (14, 17), (17, 21)),
    ((0, 3), (6, 11), (11, 14), (14, 19), (19, 24), (24, 31)),
    ((0, 3), (8, 13), (13, 16), (16, 20), (20, 26), (26, 34)),
    ((0, 3), (11, 14), (14, 16), (17, 22), (23, 27), (29, 36)),
    ((16, 19), (19, 23), (-1, -1), (24, 29), (29, 33), (33, 38)),
    ((16, 19), (19, 25), (-1, -1), (25, 30), (30, 35), (35, 39)),
    ((16, 19), (22, 28), (-1, -1), (28, 32), (32, 37), (37, 40)),
)
ORDERS = ('xy', 'xy', 'xy', 'xy', 'xy', 'plane', 'plane', 'plane')
THIRDS = 3


def passing(grads, weights, step):
    return jnp.where(weights.astype(F32) == 0.0, 0.0, grads.astype(F32)) / step


def back_kernel(
    sizes,
    step_ref,
    tok_ref,
    ints_ref,
    qkv_ref,
    probs_ref,
    ctx_ref,
    gctx_ref,
    first_ref,
    w_hbm,
    dproj_hbm,
    dup_hbm,
    ddown_hbm,
    dub_ref,
    dvec_ref,
    tg_ref,
    dqkv_out,
    dqv_out,
    dproj_out,
    dup_out,
    dub_out,
    ddown_out,
    vec_out,
    grad_s,
    dqkv_s,
    dqv_s,
    part_s,
    w_ref,
    load_s,
    *scratch,
):
    step = pl.program_id(0)
    rows = grad_s.shape[0]
    place = Place(sizes)
    parts = 2 * sizes["x"]
    width = D // parts
    step_tokens = step_ref[0:1, 0:1]
    sources = [
        lambda t: dup_hbm.at[t, 0],
        lambda t: ddown_hbm.at[t, 0],
        lambda t: dup_hbm.at[t, 1],
        lambda t: ddown_hbm.at[t, 1],
        lambda t: dproj_hbm.at[t],
    ]
    sources += [lambda t, q=q: part_s.at[t, q] for q in range(THIRDS)]
    streams = []
    for n, source in enumerate(sources):
        refs = scratch[9 * n : 9 * n + 9]
        own = refs[8] if n < 5 else None
        streams.append(Stream(place, ORDERS[n], source, *refs[:8], own))
    sums = Small(place, jnp.add, *scratch[9 * len(sources) :])

    load = pltpu.make_async_copy(w_hbm, w_ref, load_s.at[0])

    @pl.when(step == 0)
    def _():
        load.start()
        dqkv_s[...] = jnp.zeros_like(dqkv_s)
        dqv_s[...] = jnp.zeros_like(dqv_s)
        corners = [device for n, (_, _, device) in enumerate(place.plane()) if n > 1 and n % 2 == 0]
        place.hello(*corners)
        place.welcome(len(corners))

    def events(now):
        for s, plan in enumerate(PLANS):
            for k, p in enumerate(plan):
                if p[1] == now:
                    streams[s].finish(k)
        for s, plan in enumerate(PLANS):
            for k, p in enumerate(plan):
                if p[0] == now:
                    streams[s].start(k)

    def advance(tick, ticks):
        for now in ticks:
            if any(now in p for plan in PLANS for p in plan):
                pl.when(tick == now)(lambda: events(now))

    def pair_step(p, carry):
        for n in range(16 // (PAIRS * rows)):
            advance((step * PAIRS + p) * (16 // (PAIRS * rows)) + n, range(16))
        at = pl.multiple_of(p * LANES, LANES)
        q_pair = qkv_ref[:, pl.ds(at, LANES)]
        k_pair = qkv_ref[:, pl.ds(D + at, LANES)]
        v_pair = qkv_ref[:, pl.ds(2 * D + at, LANES)]
        g_pair = gctx_ref[:, pl.ds(at, LANES)]
        c_pair = ctx_ref[:, pl.ds(at, LANES)]
        product = (g_pair.astype(F32) * c_pair.astype(F32)).astype(BF16)
        lane = lax.broadcasted_iota(jnp.int32, (8, LANES), 1)
        line = lax.broadcasted_iota(jnp.int32, (8, LANES), 0)
        ones = jnp.where(lane // HEAD_DIM == line, 1.0, 0.0).astype(BF16)
        centre = dot_nt(ones, product)
        outs = []
        for n, (k0, k1, q0, q1) in enumerate(TILES):
            probs = probs_ref[0, pl.ds(2 * p, 2), n]
            gp = dot_nt(stacked(v_pair[k0:k1]), g_pair[q0:q1])
            gs = jnp.concatenate(
                [
                    (probs[h].astype(F32) * (gp[256 * h : 256 * h + 256] - centre[h : h + 1, q0:q1])).astype(BF16)
                    for h in range(2)
                ],
                axis=0,
            )
            d_values = unstacked(dot_nn(probs.reshape(512, 384), g_pair[q0:q1]))
            d_keys = unstacked(dot_nn(gs, q_pair[q0:q1]))
            outs.append(dot_tn(gs, stacked(k_pair[k0:k1])))
            grad_s[step, k0:k1, pl.ds(D + at, LANES)] = (
                d_keys * (step_tokens * step_ref[2:3, 0:1] * (1.0 / LOG2E))
            ).astype(BF16)
            dqv_s[1, :, pl.ds(at, LANES)] += fold_rows(d_values)
            grad_s[step, k0:k1, pl.ds(2 * D + at, LANES)] = (
                d_values * (step_tokens * step_ref[3:4, 0:1])
            ).astype(BF16)
        d_q = both(*outs) * 0.125
        dqv_s[0, :, pl.ds(at, LANES)] += fold_rows(d_q)
        grad_s[step, :, pl.ds(at, LANES)] = (d_q * (step_tokens * step_ref[1:2, 0:1])).astype(BF16)
        return carry

    @pl.when(step < rows)
    def _():
        lax.fori_loop(0, PAIRS, pair_step, 0)
        for i in range(3):
            dqkv_s[i] += dot_tn(grad_s[step, :, i * D : (i + 1) * D], ints_ref[...])

    pl.when(step == rows)(load.wait)

    @pl.when(step == rows)
    def _():
        for t in range(parts):
            piece = jnp.concatenate(
                [dqkv_s[i, t * width : (t + 1) * width] for i in range(3)], axis=0
            )
            part_s[t] = spread(piece.astype(BF16), part_s.shape[1:])
        dqv = jnp.sum(dqv_s[...], axis=1)
        vec = [dvec_ref[r : r + 1] for r in range(6)] + [dqv[0:1], dqv[1:2]]
        dub = jnp.concatenate([dub_ref[t] for t in range(parts)], axis=1)
        vec += [dub[:, r * D : (r + 1) * D] for r in range(4)]
        sums.start(0, tile_rows(vec, 16, D))

    @pl.when(step >= rows)
    def _():
        for n in range(4 // rows):
            advance(16 + (step - rows) * (4 // rows) + n, range(16, 20))

    def vectors():
        total = sums.finish(1)
        for n in range(6):
            vec_out[n] = total[n : n + 1]
        for t in range(parts):

            @pl.when(place.part == t)
            def _():
                dqv_out[...] = total[6:8, t * width : (t + 1) * width]
                wide = FF // parts
                dub_out[...] = total[
                    8 + t * wide // D : 9 + t * wide // D, t * wide % D : t * wide % D + wide
                ]

    @pl.when(step == rows + 1)
    def _():
        sums.start(1, sums.finish(0))

    @pl.when(step >= rows)
    def _():
        grads = grad_s[step - rows]
        total = None
        for i in range(3):
            term = dot_nt(grads[:, i * D : (i + 1) * D], w_ref[i])
            total = term if total is None else total + term
        tg_ref[...] = (first_ref[...].astype(F32) + passing(total, tok_ref[...], step_tokens)).astype(BF16)

    def joined(*group):
        halves = [streams[n].out[...].reshape(D // 2, FF // parts) for n in group]
        return jnp.concatenate(halves, axis=0)

    @pl.when(step == 2 * rows - 1)
    def _():
        ticks = sorted({n for plan in PLANS for p in plan for n in p if n >= 20})
        ended = [max(PLANS[s][5][1] for s in group) for group in ((0, 2), (1, 3), (4,))]
        for now in [19] + ticks:
            if now > 19:
                events(now)
            if now == ticks[len(ticks) // 3]:
                vectors()
            if now == max(19, ended[0]):
                dup_out[...] = joined(0, 2)
            if now == max(19, ended[1]):
                ddown_out[...] = joined(1, 3)
            if now == max(19, ended[2]):
                dproj_out[...] = streams[4].out[...].reshape(-1, D)[:width]
        whole = jnp.concatenate(
            [streams[5 + q].out[...].reshape(-1, D) for q in range(THIRDS)], axis=0
        )
        dqkv_out[...] = whole[: 3 * width]


def deliver_kernel(
    step_ref,
    tg_ref,
    dqkv_ref,
    dqv_ref,
    dproj_ref,
    dup_ref,
    dub_ref,
    ddown_ref,
    vec_ref,
    qkv_ref,
    proj_ref,
    up_ref,
    down_ref,
    tg_out,
    dqkv_out,
    dqv_out,
    dproj_out,
    dup_out,
    dub_out,
    ddown_out,
    *vec_outs,
):
    width = dqkv_out.shape[-1]
    tg_out[...] = tg_ref[...].astype(F32)
    for i in range(3):
        grad = jnp.transpose(dqkv_ref[i * width : (i + 1) * width].astype(F32))
        dqkv_out[i] = passing(grad, qkv_ref[i], step_ref[1 + i : 2 + i, 0:1])
    dproj_out[...] = passing(dproj_ref[...], proj_ref[...], step_ref[4:5, 0:1])
    dup_out[...] = passing(dup_ref[...], up_ref[...], step_ref[5:6, 0:1])
    grad = jnp.transpose(ddown_ref[...].astype(F32))
    ddown_out[...] = passing(grad, down_ref[...], step_ref[6:7, 0:1])
    dqv_out[...] = dqv_ref[...]
    dub_out[...] = dub_ref[0]
    for n, out in enumerate(vec_outs):
        out[...] = vec_ref[n, 0]


def deliver(steps, tokens_grad, dqkv, dqv, dproj, dup, dub, ddown, vec, qkv_w, proj_w, up_w, down_w):
    rows = max(1, tokens_grad.shape[0] // SEQ // 2)
    width, wide = qkv_w.shape[2], up_w.shape[1]

    def whole(*shape):
        return pl.BlockSpec(shape, lambda i: (0,) * len(shape))

    def down_rows(*shape):
        return pl.BlockSpec((shape[0] // rows,) + shape[1:], lambda i: (i, 0))

    def along(*shape):
        return pl.BlockSpec((shape[0], shape[1] // rows), lambda i: (0, i))

    qkv_block = pl.BlockSpec((3, D // rows, width), lambda i: (0, i, 0))
    outs = [
        (tokens_grad.shape, down_rows(*tokens_grad.shape)),
        (qkv_w.shape, qkv_block),
        ((2, width), whole(2, width)),
        (proj_w.shape, down_rows(*proj_w.shape)),
        (up_w.shape, down_rows(*up_w.shape)),
        ((wide,), whole(wide)),
        (down_w.shape, down_rows(*down_w.shape)),
    ] + [((D,), whole(D))] * 6
    return pl.pallas_call(
        deliver_kernel,
        name="deliver",
        grid=(rows,),
        in_specs=[
            whole(8, LANES),
            down_rows(*tokens_grad.shape),
            along(*dqkv.shape),
            whole(2, width),
            down_rows(*dproj.shape),
            down_rows(*dup.shape),
            whole(1, wide),
            along(*ddown.shape),
            whole(6, 1, D),
            qkv_block,
            down_rows(*proj_w.shape),
            down_rows(*up_w.shape),
            down_rows(*down_w.shape),
        ],
        out_specs=[spec for _, spec in outs],
        out_shape=[jax.ShapeDtypeStruct(shape, F32) for shape, _ in outs],
        compiler_params=pltpu.CompilerParams(vmem_limit_bytes=VMEM_LIMIT),
    )(steps, tokens_grad, dqkv, dqv, dproj, dup, dub, ddown, vec, qkv_w, proj_w, up_w, down_w)


def attend_back(
    sizes, steps, tokens, ints, qkv, probs, ctx, gctx, first, qkv_full, dproj, dup, ddown, dub, dvec
):
    rows = tokens.shape[0] // SEQ
    parts, nz = 2 * sizes["x"], sizes["z"]
    width, wide = D // parts, FF // parts
    part = (parts, THIRDS, 2, nz, split_rows(3 * width, 2 * THIRDS * nz), D)
    pieces = [dup.shape[-2:], ddown.shape[-2:], dup.shape[-2:], ddown.shape[-2:], dproj.shape[-2:]]
    pieces += [part[-2:]] * THIRDS
    early = lambda i: (jnp.minimum(i, rows - 1), 0)
    late = lambda i: (jnp.maximum(i - rows, 0), 0)
    hbm = pl.BlockSpec(memory_space=pl.ANY)

    def whole(*shape):
        return pl.BlockSpec(shape, lambda i: (0,) * len(shape))

    outs = [
        ((3 * width, D), BF16),
        ((2, width), F32),
        ((width, D), BF16),
        ((D, wide), BF16),
        ((1, wide), F32),
        ((D, wide), BF16),
        ((6, 1, D), F32),
    ]
    return pl.pallas_call(
        lambda *refs: back_kernel(sizes, *refs),
        name="attend_back",
        grid=(2 * rows,),
        in_specs=[
            whole(8, LANES),
            pl.BlockSpec((SEQ, D), late),
            pl.BlockSpec((SEQ, D), early),
            pl.BlockSpec((SEQ, 3 * D), early),
            pl.BlockSpec(
                (1, HEADS, 2, 256, 384), lambda i: (jnp.minimum(i, rows - 1), 0, 0, 0, 0)
            ),
            pl.BlockSpec((SEQ, D), early),
            pl.BlockSpec((SEQ, D), early),
            pl.BlockSpec((SEQ, D), late),
            hbm,
            hbm,
            hbm,
            hbm,
            whole(*dub.shape),
            whole(*dvec.shape),
        ],
        out_specs=[pl.BlockSpec((SEQ, D), late)] + [whole(*shape) for shape, _ in outs],
        scratch_shapes=[
            pltpu.VMEM((rows, SEQ, 3 * D), BF16),
            pltpu.VMEM((3, D, D), F32),
            pltpu.VMEM((2, 8, D), F32),
            pltpu.VMEM(part, BF16),
            pltpu.VMEM((3, D, D), BF16),
            pltpu.SemaphoreType.DMA((1,)),
        ]
        + sum([stream_scratch(sizes, o, *p) for o, p in zip(ORDERS, pieces)], [])
        + small_scratch(sizes, 16, D),
        out_shape=[jax.ShapeDtypeStruct((rows * SEQ, D), BF16)]
        + [jax.ShapeDtypeStruct(shape, kind) for shape, kind in outs],
        compiler_params=pltpu.CompilerParams(
            vmem_limit_bytes=VMEM_LIMIT, collective_id=1, has_side_effects=True
        ),
        cost_estimate=pl.CostEstimate(
            flops=rows * 6 * 10**9, bytes_accessed=rows * 8 * 10**6, transcendentals=0
        ),
    )(
        steps, tokens, ints, qkv, probs, ctx, gctx, first, qkv_full, dproj, dup, ddown, dub, dvec
    )

def local(
    tokens,
    segment_ids,
    row_lengths,
    qkv_weight,
    qv_bias,
    proj_weight,
    proj_bias,
    first_gain,
    first_shift,
    up_weight,
    up_bias,
    down_weight,
    down_bias,
    second_gain,
    second_shift,
    out_grad,
):
    rows = tokens.shape[0] // SEQ
    sizes = group_sizes(lax.axis_size("tensor"), lax.axis_size("dp"))
    ints, qkv, probs, ctx, qkv_full, steps, biases, proj_full, up_full, down_full = attend(
        sizes,
        row_lengths,
        tokens,
        segment_ids,
        qkv_weight,
        qv_bias,
        proj_weight,
        up_weight,
        down_weight,
        up_bias,
    )
    vecs = (proj_bias, first_gain, first_shift, down_bias, second_gain, second_shift)
    layer_out, grad_first, grad_ctx, dproj, dup, ddown, dub, dvec = feed_forward(
        sizes, steps, biases, tokens, ctx, out_grad, proj_full, up_full, down_full, vecs
    )
    sums = attend_back(
        sizes, steps, tokens, ints, qkv, probs, ctx, grad_ctx, grad_first, qkv_full,
        dproj, dup, ddown, dub, dvec,
    )
    tokens_grad, dqkv, dqv, dproj, dup, dub, ddown, *vec = deliver(
        steps, *sums, qkv_weight, proj_weight, up_weight, down_weight
    )
    return (
        layer_out, tokens_grad, dqkv, dqv, dproj, vec[0], vec[1], vec[2], dup, dub, ddown,
        vec[3], vec[4], vec[5],
    )


def solution(mesh):
    in_specs = (
        P(("dp", "tensor"), None),
        P("dp", None),
        P("dp"),
        P(None, None, "tensor"),
        P(None, "tensor"),
        P("tensor", None),
        P(),
        P(),
        P(),
        P(None, "tensor"),
        P("tensor"),
        P("tensor", None),
        P(),
        P(),
        P(),
        P(("dp", "tensor"), None),
    )
    out_specs = (
        P(("dp", "tensor"), None),
        P(("dp", "tensor"), None),
        P(None, None, "tensor"),
        P(None, "tensor"),
        P("tensor", None),
        P(),
        P(),
        P(),
        P(None, "tensor"),
        P("tensor"),
        P("tensor", None),
        P(),
        P(),
        P(),
    )
    return jax.shard_map(local, mesh=mesh, in_specs=in_specs, out_specs=out_specs, check_vma=False)
```
